32 devices in a mesh: rep: 2 (over x), fsdp: 4 (over z), ctx: 4 (over y, core).
Axes of the slice: x: 2, y: 2, z: 4, core: 2. Of those that a mesh axis runs over, the one named last changes fastest.
Arguments:
- inputs: bfloat16 [8, 1024, 2048], P(('rep', 'fsdp'), 'ctx'), may hold values from -6 to 6
- prefix: int32 [8], P(('rep', 'fsdp')), may hold values from 102 to 512
- joined_weight: bfloat16 [2048, 6144], P(('fsdp', 'ctx')), may hold values from -0.125 to 0.125
- query_bias: bfloat16 [2048], P(('fsdp', 'ctx')), may hold values from -3 to 3
- value_bias: bfloat16 [2048], P(('fsdp', 'ctx')), may hold values from -3 to 3
- dense_weight: bfloat16 [2048, 2048], P(('fsdp', 'ctx')), may hold values from -0.5 to 0.5
- dense_bias: bfloat16 [2048], P(('fsdp', 'ctx')), may hold values from -2 to 2
- expand_weight: bfloat16 [2048, 8192], P(('fsdp', 'ctx')), may hold values from -0.125 to 0.125
- expand_bias: bfloat16 [8192], P(('fsdp', 'ctx')), may hold values from -3 to 3
- shrink_weight: bfloat16 [8192, 2048], P(('fsdp', 'ctx')), may hold values from -0.0625 to 0.0625
- shrink_bias: bfloat16 [2048], P(('fsdp', 'ctx')), may hold values from -2 to 2
- first_gain: bfloat16 [2048], P(('fsdp', 'ctx')), may hold values from 0.5 to 1.5
- first_shift: bfloat16 [2048], P(('fsdp', 'ctx')), may hold values from -2 to 2
- second_gain: bfloat16 [2048], P(('fsdp', 'ctx')), may hold values from 0.5 to 1.5
- second_shift: bfloat16 [2048], P(('fsdp', 'ctx')), may hold values from -2 to 2
- cotangent: bfloat16 [8, 1024, 2048], P(('rep', 'fsdp'), 'ctx'), may hold values from -6 to 6
Outputs:
- layer_output: float32 [8, 1024, 2048], P(('rep', 'fsdp'), 'ctx')
- input_gradient: float32 [8, 1024, 2048], P(('rep', 'fsdp'), 'ctx')
- joined_gradient: float32 [2048, 6144], P(('fsdp', 'ctx'))
- query_bias_gradient: float32 [2048], P(('fsdp', 'ctx'))
- value_bias_gradient: float32 [2048], P(('fsdp', 'ctx'))
- dense_gradient: float32 [2048, 2048], P(('fsdp', 'ctx'))
- dense_bias_gradient: float32 [2048], P(('fsdp', 'ctx'))
- expand_gradient: float32 [2048, 8192], P(('fsdp', 'ctx'))
- expand_bias_gradient: float32 [8192], P(('fsdp', 'ctx'))
- shrink_gradient: float32 [8192, 2048], P(('fsdp', 'ctx'))
- shrink_bias_gradient: float32 [2048], P(('fsdp', 'ctx'))
- first_gain_gradient: float32 [2048], P(('fsdp', 'ctx'))
- first_shift_gradient: float32 [2048], P(('fsdp', 'ctx'))
- second_gain_gradient: float32 [2048], P(('fsdp', 'ctx'))
- second_shift_gradient: float32 [2048], P(('fsdp', 'ctx'))
The draws below stay inside these ranges and needn't reach their ends.
All inputs are finite; a program needn't handle non-finite values.
Results may differ from the reference program's by a relative error of at most 0.014.
Values may be sent and summed in bfloat16 or wider, within the bound.
No kernel may reach another device: no remote copies, remote signals or barrier semaphores. Data moves between devices by JAX's collectives and lax.ppermute only.
A program may use at most 576 MiB of HBM per device.

```python
import jax
import jax.numpy as jnp
from jax import lax

D = 2048
H = 32
HD = 64
FF = 8192
SEQ = 1024
SEQS = 8


def with_ends(values, own_key, smallest, high):
    dims = values.shape
    index_at = [jax.random.randint(jax.random.fold_in(own_key, axis), (), 0, dims[axis]) for axis in range(len(dims))]
    values = values.at[tuple(index_at)].set(smallest)
    longest = dims.index(max(dims))
    index_at[longest] = (index_at[longest] + 1) % dims[longest]
    return values.at[tuple(index_at)].set(high)


def steps_of(key, dims, shards, low, top_value):
    def one(axis_at, blocks):
        heights = jax.random.uniform(jax.random.fold_in(jax.random.fold_in(key, 6), axis_at), (blocks,), jnp.float32, low / len(shards), top_value / len(shards))
        return jnp.repeat(jnp.exp(heights), dims[axis_at] // blocks).reshape((-1,) + (1,) * (len(dims) - axis_at - 1))

    level = one(*shards[0])
    for cut in shards[1:]:
        level = level * one(*cut)
    return level


def noise(stream_key, dims, deviation, bound, pieces=(), kind=jnp.bfloat16):
    values = deviation * jax.random.normal(stream_key, dims, jnp.float32)
    if pieces:
        values = values * steps_of(stream_key, dims, pieces, -0.22, 0.18)
    return jnp.clip(values, -bound, bound).astype(kind)


def setup_inputs(seed: int = 0) -> dict:
    arg_keys = jax.random.split(jax.random.key(seed), 17)
    inputs = noise(arg_keys[0], (SEQS, SEQ, D), 1.0, 6.0, ((0, 8), (1, 4)))
    prefix = with_ends(jax.random.randint(arg_keys[1], (SEQS,), SEQ // 10, SEQ // 2 + 1), jax.random.fold_in(arg_keys[1], 1), SEQ // 10, (SEQ // 2 + 1) - 1).astype(jnp.int32)
    joined_weight = noise(arg_keys[2], (D, 3 * D), D ** -0.5, 0.125, ((0, 16),))
    query_bias = noise(arg_keys[3], (D,), 0.5, 3.0, ((0, 16),))
    value_bias = noise(arg_keys[4], (D,), 0.5, 3.0, ((0, 16),))
    dense_weight = noise(arg_keys[5], (D, D), (D // 16) ** -0.5, 0.5, ((0, 16),))
    dense_bias = noise(arg_keys[6], (D,), 0.3, 2.0, ((0, 16),))
    expand_weight = noise(arg_keys[7], (D, FF), D ** -0.5, 0.125, ((0, 16),))
    expand_bias = noise(arg_keys[8], (FF,), 0.5, 3.0, ((0, 16),))
    shrink_weight = noise(arg_keys[9], (FF, D), FF ** -0.5, 0.0625, ((0, 16),))
    shrink_bias = noise(arg_keys[10], (D,), 0.3, 2.0, ((0, 16),))
    first_gain = jnp.clip(1.0 + 0.1 * jax.random.normal(arg_keys[11], (D,), jnp.float32), 0.5, 1.5).astype(jnp.bfloat16)
    first_shift = noise(arg_keys[12], (D,), 0.3, 2.0, ((0, 16),))
    second_gain = jnp.clip(1.0 + 0.1 * jax.random.normal(arg_keys[13], (D,), jnp.float32), 0.5, 1.5).astype(jnp.bfloat16)
    second_shift = noise(arg_keys[14], (D,), 0.3, 2.0, ((0, 16),))
    cotangent = noise(arg_keys[15], (SEQS, SEQ, D), 1.0, 6.0, ((0, 8), (1, 4)))
    return {"inputs": inputs, "prefix": prefix, "joined_weight": joined_weight, "query_bias": query_bias, "value_bias": value_bias, "dense_weight": dense_weight, "dense_bias": dense_bias, "expand_weight": expand_weight, "expand_bias": expand_bias, "shrink_weight": shrink_weight, "shrink_bias": shrink_bias, "first_gain": first_gain, "first_shift": first_shift, "second_gain": second_gain, "second_shift": second_shift, "cotangent": cotangent}


@jax.custom_vjp
def low(v):
    return lax.optimization_barrier(v.astype(jnp.bfloat16)).astype(jnp.float32)

@jax.custom_vjp
def low_back(v):
    return v

def low_keep(v):
    return (low(v), None)

def low_pass(kept, grad):
    return (grad,)

def back_keep(v):
    return (v, None)

def back_low(kept, grad):
    return (low(grad),)
low.defvjp(low_keep, low_pass)
low_back.defvjp(back_keep, back_low)

def layer_norm(values, gain, shift):
    average = lax.optimization_barrier(jnp.mean(values, axis=-1, keepdims=True))
    centred = values - average
    variance = lax.optimization_barrier(jnp.mean(centred * centred, axis=-1, keepdims=True))
    return centred * lax.rsqrt(variance + 1e-05) * gain + shift

def one_sequence(sequence, boundary, params):
    joined_weight, query_bias, value_bias, dense_weight, dense_bias, expand_weight, expand_bias, shrink_weight, shrink_bias, first_gain, first_shift, second_gain, second_shift = params
    length = sequence.shape[0]
    features = sequence.shape[1]
    highest = lax.Precision.HIGHEST
    normed = low(layer_norm(sequence, first_gain, first_shift))
    projected = jnp.dot(normed, joined_weight, precision=highest)
    queries = low(low_back(projected[:, :features] + query_bias))
    keys = low(low_back(projected[:, features:2 * features]))
    values = low(low_back(projected[:, 2 * features:] + value_bias))
    query_heads = queries.reshape(length, H, HD)
    key_heads = keys.reshape(length, H, HD)
    value_heads = values.reshape(length, H, HD)
    raw = low_back(jnp.einsum('qhe,khe->hqk', query_heads, key_heads, precision=highest))
    places = jnp.arange(length, dtype=jnp.int32)
    distance = jnp.abs(places[:, None] - places[None, :]).astype(jnp.float32)
    allowed = (places[None, :] <= places[:, None]) | (places[None, :] < boundary)
    order = jnp.arange(H).astype(jnp.float32)
    slopes = jnp.exp2(-8.0 * (order + 1.0) / H)
    logits = raw * 0.125 - slopes[:, None, None] * distance[None]
    probs = low(jax.nn.softmax(jnp.where(allowed[None], logits, -1e+30), axis=-1))
    mixture = jnp.einsum('hqk,khe->qhe', probs, value_heads, precision=highest)
    attended = low(low_back(mixture.reshape(length, features)))
    branch = low_back(jnp.dot(attended, dense_weight, precision=highest) + dense_bias)
    midway = sequence + branch
    normed_two = low(layer_norm(midway, second_gain, second_shift))
    expanded = low_back(jnp.dot(normed_two, expand_weight, precision=highest) + expand_bias)
    activated = low(jax.nn.gelu(expanded, approximate=False))
    return midway + jnp.dot(activated, shrink_weight, precision=highest) + shrink_bias

def reference(inputs, prefix, joined_weight, query_bias, value_bias, dense_weight, dense_bias, expand_weight, expand_bias, shrink_weight, shrink_bias, first_gain, first_shift, second_gain, second_shift, cotangent):
    params = tuple((member.astype(jnp.float32) for member in (joined_weight, query_bias, value_bias, dense_weight, dense_bias, expand_weight, expand_bias, shrink_weight, shrink_bias, first_gain, first_shift, second_gain, second_shift)))
    start = inputs.astype(jnp.float32)

    def whole(sequences, weights):

        def advance(carried, element):
            return (carried, jax.checkpoint(one_sequence)(element[0], element[1], weights))
        return lax.scan(advance, None, (sequences, prefix))[1]
    result, pullback = jax.vjp(whole, start, params)
    input_gradient, grads = pullback(cotangent.astype(jnp.float32))
    return (result, input_gradient, grads[0], grads[1], grads[2], grads[3], grads[4], grads[5], grads[6], grads[7], grads[8], grads[9], grads[10], grads[11], grads[12])
```

```python
import jax
import jax.numpy as jnp
from jax import lax
from jax.sharding import PartitionSpec as P

H = 32
HD = 64
TP = ("rep", "ctx")
BF = jnp.bfloat16
F32 = jnp.float32


def dot(a, b, ca, cb):
    return lax.dot_general(a, b, (((ca,), (cb,)), ((), ())), preferred_element_type=F32)


def norm_stats(values):
    average = jnp.mean(values, axis=-1, keepdims=True)
    centred = values - average
    variance = jnp.mean(centred * centred, axis=-1, keepdims=True)
    inverse = lax.rsqrt(variance + 1e-05)
    return centred * inverse, inverse


def norm_back(normed, inverse, gain, grad):
    u = grad * gain
    mean_u = jnp.mean(u, axis=-1, keepdims=True)
    mean_un = jnp.mean(u * normed, axis=-1, keepdims=True)
    return (u - mean_u - normed * mean_un) * inverse


def gelu(values):
    return 0.5 * values * (1.0 + lax.erf(values * 0.7071067811865476))


def gelu_slope(values):
    density = jnp.exp(values * values * -0.5) * 0.3989422804014327
    return 0.5 * (1.0 + lax.erf(values * 0.7071067811865476)) + values * density


def gather_tp(x):
    return lax.all_gather(x, TP, axis=0, tiled=True)


def scatter_tp(x):
    return lax.psum_scatter(x, TP, scatter_dimension=0, tiled=True)


def swap_tp(x):
    return lax.all_to_all(x, TP, 0, 0, tiled=True)


def attention_logits(q, k, heads, prefix):
    raw = jnp.einsum("sqhe,skhe->shqk", q, k, preferred_element_type=F32)
    length = k.shape[1]
    place = jnp.arange(length, dtype=jnp.int32)
    distance = jnp.abs(place[:, None] - place[None, :]).astype(F32)
    allowed = (place[None, None, :] <= place[None, :, None]) | (place[None, None, :] < prefix[:, None, None])
    slopes = jnp.exp2(-8.0 * (heads.astype(F32) + 1.0) / H)
    logits = raw * 0.125 - slopes[None, :, None, None] * distance[None, None]
    return logits, allowed[:, None]


def attention_forward(q, k, v, heads, prefix):
    logits, allowed = attention_logits(q, k, heads, prefix)
    masked = jnp.where(allowed, logits, -1e30)
    largest = jnp.max(masked, axis=-1, keepdims=True)
    exponent = jnp.exp(masked - largest)
    totals = jnp.sum(exponent, axis=-1, keepdims=True)
    probs = (exponent / totals).astype(BF)
    out = jnp.einsum("shqk,skhe->sqhe", probs, v, preferred_element_type=F32).astype(BF)
    return out, largest + jnp.log(totals)


def attention_backward(q, k, v, lse, d_out, heads, prefix):
    logits, allowed = attention_logits(q, k, heads, prefix)
    probs = jnp.where(allowed, jnp.exp(logits - lse), 0.0)
    d_probs = jnp.einsum("sqhe,skhe->shqk", d_out, v, preferred_element_type=F32)
    weighted = jnp.sum(probs * d_probs, axis=-1, keepdims=True)
    d_raw = (probs * (d_probs - weighted) * 0.125).astype(BF)
    low = probs.astype(BF)
    d_q = jnp.einsum("shqk,skhe->sqhe", d_raw, k, preferred_element_type=F32).astype(BF)
    d_k = jnp.einsum("shqk,sqhe->skhe", d_raw, q, preferred_element_type=F32).astype(BF)
    d_v = jnp.einsum("shqk,sqhe->skhe", low, d_out, preferred_element_type=F32).astype(BF)
    return d_q, d_k, d_v


def shards(
    sizes,
    inputs,
    prefix,
    joined_weight,
    query_bias,
    value_bias,
    dense_weight,
    dense_bias,
    expand_weight,
    expand_bias,
    shrink_weight,
    shrink_bias,
    first_gain,
    first_shift,
    second_gain,
    second_shift,
    cotangent,
):
    R, F, C = sizes
    N = R * C
    rep = lax.axis_index("rep")
    ctx = lax.axis_index("ctx")
    S, T, D = inputs.shape
    t = S * T
    B = joined_weight.shape[0]
    FFB = shrink_weight.shape[0]
    FF = FFB * F * C
    E = FFB // R
    W = D // N
    aligned = (B // R) % HD == 0

    def split_columns(weight, groups):
        n = weight.shape[1] // groups
        if aligned or groups == 1:
            pieces = weight.reshape(B, groups, F, C, R, n // (F * C * R))
            mine = lax.dynamic_index_in_dim(pieces, rep, 4, keepdims=False)
            mine = mine.transpose(3, 0, 1, 2, 4)
        else:
            pieces = weight.reshape(B, groups, R, C, n // (C * R))
            mine = lax.dynamic_index_in_dim(pieces, rep, 2, keepdims=False)
            mine = mine.transpose(2, 0, 1, 3)
        return mine.reshape(C, B, groups * n // N)

    def columns(weight, groups):
        blocks = lax.all_to_all(split_columns(weight, groups), "ctx", 0, 0, tiled=True)
        return lax.all_gather(blocks.reshape(C * B, -1), "fsdp", axis=0, tiled=True)

    def join_columns(grad, groups):
        part = lax.psum_scatter(grad.astype(BF), "fsdp", scatter_dimension=0, tiled=True)
        blocks = lax.all_to_all(part.reshape(C, B, -1), "ctx", 0, 0, tiled=True)
        both = lax.all_gather(blocks, "rep", axis=0, tiled=False)
        if aligned or groups == 1:
            both = both.reshape(R, C, B, groups, F, -1).transpose(2, 3, 4, 1, 0, 5)
        else:
            both = both.reshape(R, C, B, groups, -1).transpose(2, 3, 0, 1, 4)
        return both.reshape(B, -1).astype(F32)

    def half_rows(weight):
        n = weight.shape[0] // R
        return lax.dynamic_slice_in_dim(weight, rep * n, n, 0)

    def join_rows(part):
        return lax.all_gather(part, "rep", axis=0, tiled=True).astype(F32)

    small = jnp.concatenate(
        [first_gain, first_shift, second_gain, second_shift, dense_bias, shrink_bias, query_bias, value_bias, expand_bias]
    )
    small = lax.all_gather(small, ("fsdp", "ctx"), axis=0, tiled=False).astype(F32)
    gain_one, shift_one, gain_two, shift_two, dbias, sbias, qbias, vbias = [
        small[:, i * B : (i + 1) * B].reshape(D) for i in range(8)
    ]
    ebias = small[:, 8 * B :].reshape(F, C, R, E)
    ebias = lax.dynamic_index_in_dim(lax.dynamic_index_in_dim(ebias, ctx, 1, False), rep, 1, False).reshape(F * E)

    def my_features(vector):
        if aligned:
            v = vector.reshape(F, C, R, -1)
            return lax.dynamic_index_in_dim(lax.dynamic_index_in_dim(v, ctx, 1, False), rep, 1, False).reshape(W)
        return lax.dynamic_slice_in_dim(vector, (rep * C + ctx) * W, W, 0)

    my_heads = my_features(jnp.repeat(jnp.arange(H, dtype=jnp.int32), HD)).reshape(-1, HD)[:, 0]
    prefix_all = lax.all_gather(prefix, "rep", axis=0, tiled=True)

    joined_cols = columns(joined_weight, 3)
    dense_rows = lax.all_gather(half_rows(dense_weight), "fsdp", axis=0, tiled=True) if aligned else None
    expand_cols = columns(expand_weight, 1)
    shrink_rows = lax.all_gather(half_rows(shrink_weight), "fsdp", axis=0, tiled=True)
    if aligned:
        dense_all = gather_tp(dense_rows)
    else:
        dense_all = lax.all_gather(dense_weight, ("fsdp", "ctx"), axis=0, tiled=True)

    def to_sequences(a):
        return a.reshape(R, C, S, T, -1).transpose(0, 2, 1, 3, 4).reshape(R * S, C * T, -1)

    def from_sequences(a):
        return a.reshape(R, S, C, T, -1).transpose(0, 2, 1, 3, 4).reshape(N * t, -1)

    start = inputs.astype(F32).reshape(t, D)
    n1, inv1 = norm_stats(start)
    a1 = (n1 * gain_one + shift_one).astype(BF)
    a1_all = gather_tp(a1)
    g = cotangent.reshape(t, D)
    g_all = gather_tp(g)
    qkv = dot(a1_all, joined_cols, 1, 0)
    q = (qkv[:, :W] + my_features(qbias)).astype(BF)
    k = qkv[:, W : 2 * W].astype(BF)
    v = (qkv[:, 2 * W :] + my_features(vbias)).astype(BF)
    heads = lambda a: to_sequences(a).reshape(R * S, C * T, W // HD, HD)
    q, k, v = heads(q), heads(k), heads(v)
    out, lse = attention_forward(q, k, v, my_heads, prefix_all)
    o = swap_tp(from_sequences(out).reshape(N, t, W))
    o = o.transpose(1, 0, 2).reshape(t, D)
    midway = start + dot(o, dense_all, 1, 0) + dbias

    n2, inv2 = norm_stats(midway)
    a2 = (n2 * gain_two + shift_two).astype(BF)
    a2_all = gather_tp(a2)
    expanded = dot(a2_all, expand_cols, 1, 0) + ebias
    act = gelu(expanded).astype(BF)
    branch = scatter_tp(dot(act, shrink_rows, 1, 0).astype(BF))
    layer_output = midway + branch.astype(F32) + sbias

    g_float = g.astype(F32)
    d_act = dot(g_all, shrink_rows, 1, 1)
    d_exp = (d_act * gelu_slope(expanded)).astype(BF)
    d_a2 = scatter_tp(dot(d_exp, expand_cols, 1, 1).astype(BF)).astype(F32)
    shrink_grad = dot(act, g_all, 0, 0).astype(BF)
    expand_grad = dot(a2_all, d_exp, 0, 0)
    ebias_grad = jnp.sum(d_exp.astype(F32), axis=0)
    sbias_grad = jnp.sum(g_float, axis=0)
    d_mid = g_float + norm_back(n2, inv2, gain_two, d_a2)
    gain_two_grad = jnp.sum(d_a2 * n2, axis=0)
    shift_two_grad = jnp.sum(d_a2, axis=0)
    d_att = d_mid.astype(BF)

    dense_grad = dot(o, d_att, 0, 0)
    dbias_grad = jnp.sum(d_att.astype(F32), axis=0)
    d_o = dot(d_att, dense_all, 1, 1).astype(BF)
    d_o = swap_tp(d_o.reshape(t, N, W).transpose(1, 0, 2)).reshape(N * t, W)
    d_q, d_k, d_v = attention_backward(q, k, v, lse, heads(d_o), my_heads, prefix_all)
    d_qkv = jnp.concatenate([from_sequences(a.reshape(R * S, C * T, W)) for a in (d_q, d_k, d_v)], axis=1)
    d_a1 = scatter_tp(dot(d_qkv, joined_cols, 1, 1).astype(BF)).astype(F32)
    joined_grad = dot(a1_all, d_qkv, 0, 0)
    qkv_bias_grad = jnp.sum(d_qkv.astype(F32), axis=0)
    input_gradient = d_mid + norm_back(n1, inv1, gain_one, d_a1)
    gain_one_grad = jnp.sum(d_a1 * n1, axis=0)
    shift_one_grad = jnp.sum(d_a1, axis=0)

    shrink_out = join_rows(lax.psum_scatter(shrink_grad, "fsdp", scatter_dimension=0, tiled=True))
    expand_out = join_columns(expand_grad, 1)
    if aligned:
        part = scatter_tp(dense_grad.astype(BF))
        dense_out = join_rows(lax.psum_scatter(part, "fsdp", scatter_dimension=0, tiled=True))
    else:
        part = lax.psum_scatter(dense_grad.astype(BF), ("fsdp", "ctx"), scatter_dimension=0, tiled=True)
        dense_out = lax.psum(part, "rep").astype(F32)
    joined_out = join_columns(joined_grad, 3)

    def spread(vector, width):
        if aligned or width != D:
            full = jnp.zeros((F, C, R, width // (F * C * R)), F32)
            full = lax.dynamic_update_slice(full, vector.reshape(F, 1, 1, -1), (0, ctx, rep, 0))
        else:
            full = lax.dynamic_update_slice_in_dim(jnp.zeros((width,), F32), vector, (rep * C + ctx) * W, 0)
        return full.reshape(F * C, -1)

    tokens = [gain_one_grad, shift_one_grad, gain_two_grad, shift_two_grad, dbias_grad, sbias_grad]
    rows = [a.reshape(F * C, B) for a in tokens]
    rows += [spread(qkv_bias_grad[:W], D), spread(qkv_bias_grad[2 * W :], D), spread(ebias_grad, FF)]
    little = jnp.concatenate(rows, axis=1)
    little = lax.psum(lax.psum_scatter(little, ("fsdp", "ctx"), scatter_dimension=0, tiled=True), "rep").reshape(-1)
    gain_one_out, shift_one_out, gain_two_out, shift_two_out, dbias_out, sbias_out, qbias_out, vbias_out = [
        little[i * B : (i + 1) * B] for i in range(8)
    ]
    ebias_out = little[8 * B :]

    return (
        layer_output.reshape(S, T, D),
        input_gradient.reshape(S, T, D),
        joined_out,
        qbias_out,
        vbias_out,
        dense_out,
        dbias_out,
        expand_out,
        ebias_out,
        shrink_out,
        sbias_out,
        gain_one_out,
        shift_one_out,
        gain_two_out,
        shift_two_out,
    )


def solution(mesh):
    sizes = (mesh.shape["rep"], mesh.shape["fsdp"], mesh.shape["ctx"])
    tokens = P(("rep", "fsdp"), "ctx", None)
    matrix = P(("fsdp", "ctx"), None)
    vector = P(("fsdp", "ctx"))
    in_specs = (
        tokens,
        P(("rep", "fsdp")),
        matrix,
        vector,
        vector,
        matrix,
        vector,
        matrix,
        vector,
        matrix,
        vector,
        vector,
        vector,
        vector,
        vector,
        tokens,
    )
    out_specs = (
        tokens,
        tokens,
        matrix,
        vector,
        vector,
        matrix,
        vector,
        matrix,
        vector,
        matrix,
        vector,
        vector,
        vector,
        vector,
        vector,
    )

    def step(*arrays):
        return shards(sizes, *arrays)

    return jax.shard_map(step, mesh=mesh, in_specs=in_specs, out_specs=out_specs, check_vma=False)
```

```python
import functools

import jax
import jax.numpy as jnp
from jax import lax
from jax.experimental import pallas as pl
from jax.experimental.pallas import tpu as pltpu
from jax.sharding import PartitionSpec as P

H = 32
HD = 64
BF = jnp.bfloat16
F32 = jnp.float32
LONGEST = 512


def dot(a, b, ca, cb):
    return lax.dot_general(a, b, (((ca,), (cb,)), ((), ())), preferred_element_type=F32)


def head_probs(query, key, slope, place, prefix, lanes):
    raw = dot(jnp.where(lanes, query, jnp.zeros_like(query)), key, 1, 1)
    row = place + lax.broadcasted_iota(jnp.int32, raw.shape, 0)
    column = lax.broadcasted_iota(jnp.int32, raw.shape, 1)
    distance = jnp.abs(row - column).astype(F32)
    allowed = column <= jnp.maximum(row, prefix - 1)
    logits = jnp.where(allowed, raw - slope * distance, -1e30)
    largest = jnp.max(logits, axis=-1, keepdims=True)
    exponent = jnp.exp(logits - largest)
    return exponent * (1.0 / jnp.sum(exponent, axis=-1, keepdims=True))


def forward_kernel(W, order_ref, prefix_ref, slope_ref, qkv_ref, out_ref):
    C, T = qkv_ref.shape[1], qkv_ref.shape[2]
    seq, pair = pl.program_id(0), pl.program_id(1)
    at = lambda part: pl.ds(pl.multiple_of(part * W + pair * 128, 128), 128)
    first = lax.broadcasted_iota(jnp.int32, (T, 128), 1) < HD
    prefix = prefix_ref[seq]
    key = [qkv_ref[0, order_ref[c], :, at(1)] for c in range(C)]
    value = [qkv_ref[0, order_ref[c], :, at(2)] for c in range(C)]
    for c in range(C):
        n = min(C, max(c + 1, -(-LONGEST // T)))
        keys = jnp.concatenate(key[:n], axis=0)
        values = jnp.concatenate(value[:n], axis=0)
        query = qkv_ref[0, order_ref[c], :, at(0)] * 0.125
        out = []
        for h in range(2):
            probs = head_probs(query, keys, slope_ref[2 * pair + h], c * T, prefix, first if h == 0 else ~first)
            out.append(dot(probs.astype(BF), values, 1, 0))
        out_ref[0, order_ref[c], :, at(0)] = jnp.where(first, out[0], out[1]).astype(BF)


def backward_kernel(W, order_ref, prefix_ref, slope_ref, qkv_ref, d_out_ref, d_qkv_ref, d_key, d_value):
    C, T = qkv_ref.shape[1], qkv_ref.shape[2]
    seq, pair = pl.program_id(0), pl.program_id(1)
    at = lambda part: pl.ds(pl.multiple_of(part * W + pair * 128, 128), 128)
    first = lax.broadcasted_iota(jnp.int32, (T, 128), 1) < HD
    prefix = prefix_ref[seq]
    d_key[...] = jnp.zeros_like(d_key)
    d_value[...] = jnp.zeros_like(d_value)
    key = [qkv_ref[0, order_ref[c], :, at(1)] for c in range(C)]
    value = [qkv_ref[0, order_ref[c], :, at(2)] for c in range(C)]
    for c in range(C):
        n = min(C, max(c + 1, -(-LONGEST // T)))
        keys = jnp.concatenate(key[:n], axis=0)
        values = jnp.concatenate(value[:n], axis=0)
        query = qkv_ref[0, order_ref[c], :, at(0)]
        d_out = d_out_ref[0, order_ref[c], :, at(0)]
        d_query = []
        for h in range(2):
            lanes = first if h == 0 else ~first
            probs = head_probs(query * 0.125, keys, slope_ref[2 * pair + h], c * T, prefix, lanes)
            mine = jnp.where(lanes, d_out, jnp.zeros_like(d_out))
            d_probs = dot(mine, values, 1, 1)
            weighted = jnp.sum(probs * d_probs, axis=-1, keepdims=True)
            d_raw = (probs * (d_probs - weighted) * 0.125).astype(BF)
            d_query.append(dot(d_raw, keys, 1, 0))
            d_value[: n * T] += dot(probs.astype(BF), mine, 0, 0)
            d_key[: n * T] += dot(d_raw, jnp.where(lanes, query, jnp.zeros_like(query)), 0, 0)
        d_qkv_ref[0, order_ref[c], :, at(0)] = jnp.where(first, d_query[0], d_query[1]).astype(BF)
    for c in range(C):
        d_qkv_ref[0, order_ref[c], :, at(1)] = d_key[c * T : (c + 1) * T].astype(BF)
        d_qkv_ref[0, order_ref[c], :, at(2)] = d_value[c * T : (c + 1) * T].astype(BF)


def attention_call(kernel, widths, out_width, scratch, flops, order, prefix, slopes, *arrays):
    n, C, T = arrays[0].shape[:3]
    W = widths[-1]
    spec = lambda width: pl.BlockSpec((1, C, T, width), lambda s, p, *_: (s, 0, 0, 0))
    return pl.pallas_call(
        functools.partial(kernel, W),
        out_shape=jax.ShapeDtypeStruct((n, C, T, out_width), BF),
        grid_spec=pltpu.PrefetchScalarGridSpec(
            num_scalar_prefetch=3,
            grid=(n, W // 128),
            in_specs=[spec(a.shape[3]) for a in arrays],
            out_specs=spec(out_width),
            scratch_shapes=scratch,
        ),
        compiler_params=pltpu.CompilerParams(
            dimension_semantics=("arbitrary", "arbitrary"), vmem_limit_bytes=48 * 1024 * 1024
        ),
        cost_estimate=pl.CostEstimate(
            flops=flops * n * C * C * T * T * W, transcendentals=n * C * C * T * T * W // HD, bytes_accessed=sum(a.size * 2 for a in arrays)
        ),
    )(order, prefix, slopes, *arrays)


def attention_forward(order, prefix, slopes, qkv):
    W = qkv.shape[3] // 3
    return attention_call(forward_kernel, (W,), W, [], 4, order, prefix, slopes, qkv)


def attention_backward(order, prefix, slopes, qkv, d_out):
    W = qkv.shape[3] // 3
    L = qkv.shape[1] * qkv.shape[2]
    scratch = [pltpu.VMEM((L, 128), F32), pltpu.VMEM((L, 128), F32)]
    return attention_call(backward_kernel, (W,), 3 * W, scratch, 10, order, prefix, slopes, qkv, d_out)


def norm_stats(values):
    average = jnp.mean(values, axis=-1, keepdims=True)
    centred = values - average
    variance = jnp.mean(centred * centred, axis=-1, keepdims=True)
    inverse = lax.rsqrt(variance + 1e-05)
    return centred * inverse, inverse


def norm_back(normed, inverse, gain, grad):
    u = grad * gain
    mean_u = jnp.mean(u, axis=-1, keepdims=True)
    mean_un = jnp.mean(u * normed, axis=-1, keepdims=True)
    return (u - mean_u - normed * mean_un) * inverse


def gelu(values):
    return 0.5 * values * (1.0 + lax.erf(values * 0.7071067811865476))


def gelu_slope(values):
    density = jnp.exp(values * values * -0.5) * 0.3989422804014327
    return 0.5 * (1.0 + lax.erf(values * 0.7071067811865476)) + values * density


class Plain:
    def __init__(self, R, C):
        self.R, self.C, self.N = R, C, R * C
        self.axes = ("rep", "ctx")
        self.order = jnp.arange(C, dtype=jnp.int32)

    def gather(self, x):
        return lax.all_gather(x, self.axes, axis=0, tiled=False)

    def scatter(self, parts):
        out = lax.psum_scatter(parts.astype(BF), self.axes, scatter_dimension=0, tiled=True)
        return out.reshape(parts.shape[1:]).astype(F32)

    def swap(self, parts):
        return lax.all_to_all(parts, self.axes, 0, 0, tiled=True)

    def swap_ctx(self, blocks):
        return lax.all_to_all(blocks, "ctx", 0, 0, tiled=True)

    def prefixes(self, prefix):
        return lax.all_gather(prefix, "rep", axis=0, tiled=True)

    def both_reps(self, x):
        return lax.all_gather(x, "rep", axis=0, tiled=False)


class Near(Plain):
    def __init__(self, R, C):
        super().__init__(R, C)
        self.ctx = lax.axis_index("ctx")
        self.rep = lax.axis_index("rep")
        self.order = jnp.arange(C, dtype=jnp.int32) ^ self.ctx

    def over(self, x, d):
        return lax.ppermute(x, "ctx", [(i, i ^ d) for i in range(4)])

    def x(self, x):
        return lax.ppermute(x, "rep", [(0, 1), (1, 0)])

    def y(self, x):
        return self.over(x, 2)

    def core(self, x):
        return self.over(x, 1)

    def gather(self, x):
        half = x.shape[0] // 2
        from_x, from_y = self.x(x), self.y(x)
        far = jnp.concatenate([self.y(from_x[:half]), self.x(from_y[half:])], axis=0)
        quads = [x, from_y, from_x, far]
        return jnp.stack([piece for quad in quads for piece in (quad, self.core(quad))])

    def scatter(self, parts):
        sums = [parts[2 * i].astype(F32) + self.core(parts[2 * i + 1].astype(BF)).astype(F32) for i in range(4)]
        near, by_y, by_x, far = sums
        half = far.shape[0] // 2
        far = far.astype(BF)
        to_y = self.y(far[:half]).astype(F32)
        to_x = self.x(far[half:]).astype(F32)
        by_x = jnp.concatenate([by_x[:half] + to_y, by_x[half:]], axis=0)
        by_y = jnp.concatenate([by_y[:half], by_y[half:] + to_x], axis=0)
        return near + self.x(by_x.astype(BF)).astype(F32) + self.y(by_y.astype(BF)).astype(F32)

    def swap(self, parts):
        pairs = [[(i, i ^ d) for i in range(self.N)] for d in range(self.N)]
        moved = [lax.ppermute(parts[d], self.axes, pairs[d]) for d in range(1, self.N)]
        return jnp.stack([parts[0]] + moved)

    def swap_ctx(self, blocks):
        out = blocks
        for d in range(1, 4):
            moved = self.over(lax.dynamic_index_in_dim(blocks, self.ctx ^ d, 0, keepdims=False), d)
            out = lax.dynamic_update_index_in_dim(out, moved, self.ctx ^ d, 0)
        return out

    def prefixes(self, prefix):
        return jnp.concatenate([prefix, self.x(prefix)])

    def both_reps(self, x):
        other = self.x(x)
        first = self.rep == 0
        return jnp.stack([jnp.where(first, x, other), jnp.where(first, other, x)])


def gather_shifts(x, axis, size):
    me = lax.axis_index(axis)
    out = lax.dynamic_update_index_in_dim(jnp.zeros((size,) + x.shape, x.dtype), x, me, 0)
    for s in range(1, size):
        moved = lax.ppermute(x, axis, [(i, (i + s) % size) for i in range(size)])
        out = lax.dynamic_update_index_in_dim(out, moved, lax.rem(me - s + size, size), 0)
    return out


def scatter_shifts(x, axis, size):
    me = lax.axis_index(axis)
    total = lax.dynamic_index_in_dim(x, me, 0, keepdims=False)
    for s in range(1, size):
        mine = lax.dynamic_index_in_dim(x, lax.rem(me + s, size), 0, keepdims=False)
        total = total + lax.ppermute(mine, axis, [(i, (i + s) % size) for i in range(size)])
    return total


def shards(
    sizes,
    inputs,
    prefix,
    joined_weight,
    query_bias,
    value_bias,
    dense_weight,
    dense_bias,
    expand_weight,
    expand_bias,
    shrink_weight,
    shrink_bias,
    first_gain,
    first_shift,
    second_gain,
    second_shift,
    cotangent,
):
    R, F, C = sizes
    N = R * C
    rep = lax.axis_index("rep")
    ctx = lax.axis_index("ctx")
    S, T, D = inputs.shape
    t = S * T
    B = joined_weight.shape[0]
    FFB = shrink_weight.shape[0]
    FF = FFB * F * C
    E = FFB // R
    W = D // N
    aligned = (B // R) % HD == 0
    near = aligned and S == 1 and R == 2 and C == 4
    tp = Near(R, C) if near else Plain(R, C)

    def split_columns(weight, groups):
        n = weight.shape[1] // groups
        if aligned or groups == 1:
            pieces = weight.reshape(B, groups, F, C, R, n // (F * C * R))
            mine = lax.dynamic_index_in_dim(pieces, rep, 4, keepdims=False)
            mine = mine.transpose(3, 0, 1, 2, 4)
        else:
            pieces = weight.reshape(B, groups, R, C, n // (C * R))
            mine = lax.dynamic_index_in_dim(pieces, rep, 2, keepdims=False)
            mine = mine.transpose(2, 0, 1, 3)
        return mine.reshape(C, B, groups * n // N)

    def columns(weight, groups):
        blocks = tp.swap_ctx(split_columns(weight, groups))
        return lax.all_gather(blocks.reshape(C * B, -1), "fsdp", axis=0, tiled=True)

    def join_columns(grad, groups):
        part = lax.psum_scatter(grad.astype(BF), "fsdp", scatter_dimension=0, tiled=True)
        both = tp.both_reps(tp.swap_ctx(part.reshape(C, B, -1)))
        if aligned or groups == 1:
            both = both.reshape(R, C, B, groups, F, -1).transpose(2, 3, 4, 1, 0, 5)
        else:
            both = both.reshape(R, C, B, groups, -1).transpose(2, 3, 0, 1, 4)
        return both.reshape(B, -1).astype(F32)

    def half_rows(weight):
        n = weight.shape[0] // R
        return lax.dynamic_slice_in_dim(weight, rep * n, n, 0)

    def join_rows(part):
        both = tp.both_reps(part)
        return both.reshape(-1, both.shape[-1]).astype(F32)

    small = jnp.concatenate(
        [first_gain, first_shift, second_gain, second_shift, dense_bias, shrink_bias, query_bias, value_bias, expand_bias]
    )
    small = gather_shifts(gather_shifts(small, "ctx", C), "fsdp", F)
    small = small.reshape(F * C, -1).astype(F32)
    gain_one, shift_one, gain_two, shift_two, dbias, sbias, qbias, vbias = [
        small[:, i * B : (i + 1) * B].reshape(D) for i in range(8)
    ]
    ebias = small[:, 8 * B :].reshape(F, C, R, E)
    ebias = lax.dynamic_index_in_dim(lax.dynamic_index_in_dim(ebias, ctx, 1, False), rep, 1, False).reshape(F * E)

    def my_features(vector):
        if aligned:
            v = vector.reshape(F, C, R, -1)
            return lax.dynamic_index_in_dim(lax.dynamic_index_in_dim(v, ctx, 1, False), rep, 1, False).reshape(W)
        return lax.dynamic_slice_in_dim(vector, (rep * C + ctx) * W, W, 0)

    my_heads = my_features(jnp.repeat(jnp.arange(H, dtype=jnp.int32), HD)).reshape(-1, HD)[:, 0]
    slopes = jnp.exp2(-8.0 * (my_heads.astype(F32) + 1.0) / H)
    prefixes = tp.prefixes(prefix)

    joined_cols = columns(joined_weight, 3)
    if aligned:
        dense_all = tp.gather(lax.all_gather(half_rows(dense_weight), "fsdp", axis=0, tiled=True)).reshape(D, D)
    else:
        dense_all = lax.all_gather(dense_weight, ("fsdp", "ctx"), axis=0, tiled=True)
    expand_cols = columns(expand_weight, 1)
    shrink_rows = lax.all_gather(half_rows(shrink_weight), "fsdp", axis=0, tiled=True)

    def to_sequences(a):
        return a.reshape(R, C, S, T, -1).transpose(0, 2, 1, 3, 4).reshape(R * S, C, T, -1)

    def from_sequences(a):
        return a.reshape(R, S, C, T, -1).transpose(0, 2, 1, 3, 4).reshape(N, t, -1)

    start = inputs.astype(F32).reshape(t, D)
    n1, inv1 = norm_stats(start)
    a1 = (n1 * gain_one + shift_one).astype(BF)
    a1_all = tp.gather(a1).reshape(N * t, D)
    g = cotangent.reshape(t, D)
    g_all = tp.gather(g).reshape(N * t, D)
    qkv_bias = jnp.concatenate([my_features(qbias), jnp.zeros((W,), F32), my_features(vbias)])
    qkv = (dot(a1_all, joined_cols, 1, 0) + qkv_bias).astype(BF)
    qkv = to_sequences(qkv)
    out = attention_forward(tp.order, prefixes, slopes, qkv)
    o = tp.swap(from_sequences(out))
    o = o.transpose(1, 0, 2).reshape(t, D)
    midway = start + dot(o, dense_all, 1, 0) + dbias

    n2, inv2 = norm_stats(midway)
    a2 = (n2 * gain_two + shift_two).astype(BF)
    a2_all = tp.gather(a2).reshape(N * t, D)
    expanded = dot(a2_all, expand_cols, 1, 0) + ebias
    act = gelu(expanded).astype(BF)
    branch = tp.scatter(dot(act, shrink_rows, 1, 0).reshape(N, t, D))
    layer_output = midway + branch + sbias

    g_float = g.astype(F32)
    d_act = dot(g_all, shrink_rows, 1, 1)
    d_exp = (d_act * gelu_slope(expanded)).astype(BF)
    d_a2 = tp.scatter(dot(d_exp, expand_cols, 1, 1).reshape(N, t, D))
    shrink_grad = dot(act, g_all, 0, 0).astype(BF)
    expand_grad = dot(a2_all, d_exp, 0, 0)
    ebias_grad = jnp.sum(d_exp.astype(F32), axis=0)
    sbias_grad = jnp.sum(g_float, axis=0)
    d_mid = g_float + norm_back(n2, inv2, gain_two, d_a2)
    gain_two_grad = jnp.sum(d_a2 * n2, axis=0)
    shift_two_grad = jnp.sum(d_a2, axis=0)
    d_att = d_mid.astype(BF)

    dense_grad = dot(o, d_att, 0, 0)
    dbias_grad = jnp.sum(d_att.astype(F32), axis=0)
    d_o = dot(d_att, dense_all, 1, 1).astype(BF)
    d_o = tp.swap(d_o.reshape(t, N, W).transpose(1, 0, 2))
    d_qkv = attention_backward(tp.order, prefixes, slopes, qkv, to_sequences(d_o))
    d_qkv = from_sequences(d_qkv).reshape(N * t, 3 * W)
    d_a1 = tp.scatter(dot(d_qkv, joined_cols, 1, 1).reshape(N, t, D))
    joined_grad = dot(a1_all, d_qkv, 0, 0)
    qkv_bias_grad = jnp.sum(d_qkv.astype(F32), axis=0)
    input_gradient = d_mid + norm_back(n1, inv1, gain_one, d_a1)
    gain_one_grad = jnp.sum(d_a1 * n1, axis=0)
    shift_one_grad = jnp.sum(d_a1, axis=0)

    shrink_out = join_rows(lax.psum_scatter(shrink_grad, "fsdp", scatter_dimension=0, tiled=True))
    expand_out = join_columns(expand_grad, 1)
    if aligned:
        part = tp.scatter(dense_grad.reshape(N, W, D)).astype(BF)
        dense_out = join_rows(lax.psum_scatter(part, "fsdp", scatter_dimension=0, tiled=True))
    else:
        part = lax.psum_scatter(dense_grad.astype(BF), ("fsdp", "ctx"), scatter_dimension=0, tiled=True)
        dense_out = lax.psum(part, "rep").astype(F32)
    joined_out = join_columns(joined_grad, 3)

    tokens = jnp.stack([gain_one_grad, shift_one_grad, gain_two_grad, shift_two_grad, dbias_grad, sbias_grad])
    if near:
        tokens = tokens + tp.x(tokens)
        tokens = tokens + tp.y(tokens)
        tokens = tokens + tp.core(tokens)
    else:
        tokens = lax.psum(tokens, ("rep", "ctx"))
    tokens = lax.dynamic_index_in_dim(tokens.reshape(6, F, C, B), ctx, 2, keepdims=False)
    tokens = tokens.transpose(1, 0, 2).reshape(F, 6 * B)
    if aligned:
        own = [a.reshape(F, -1) for a in (qkv_bias_grad[:W], qkv_bias_grad[2 * W :], ebias_grad)]
    else:
        spread = jnp.zeros((2, N, W), F32)
        mine = jnp.stack([qkv_bias_grad[:W], qkv_bias_grad[2 * W :]])[:, None]
        spread = lax.psum(lax.dynamic_update_slice(spread, mine, (0, rep * C + ctx, 0)), ("rep", "ctx"))
        spread = lax.dynamic_index_in_dim(spread.reshape(2, F, C, R, -1), ctx, 2, keepdims=False)
        spread = lax.dynamic_index_in_dim(spread, rep, 2, keepdims=False)
        own = [spread[0], spread[1], ebias_grad.reshape(F, -1)]
    little = scatter_shifts(jnp.concatenate([tokens] + own, axis=1), "fsdp", F)
    gain_one_out, shift_one_out, gain_two_out, shift_two_out, dbias_out, sbias_out = [
        little[i * B : (i + 1) * B] for i in range(6)
    ]
    own = tp.both_reps(little[6 * B :])
    n = B // R
    qbias_out = own[:, :n].reshape(B)
    vbias_out = own[:, n : 2 * n].reshape(B)
    ebias_out = own[:, 2 * n :].reshape(FFB)

    return (
        layer_output.reshape(S, T, D),
        input_gradient.reshape(S, T, D),
        joined_out,
        qbias_out,
        vbias_out,
        dense_out,
        dbias_out,
        expand_out,
        ebias_out,
        shrink_out,
        sbias_out,
        gain_one_out,
        shift_one_out,
        gain_two_out,
        shift_two_out,
    )


def solution(mesh):
    sizes = (mesh.shape["rep"], mesh.shape["fsdp"], mesh.shape["ctx"])
    tokens = P(("rep", "fsdp"), "ctx", None)
    matrix = P(("fsdp", "ctx"), None)
    vector = P(("fsdp", "ctx"))
    weights = (matrix, vector, vector, matrix, vector, matrix, vector, matrix, vector, vector, vector, vector, vector)
    in_specs = (tokens, P(("rep", "fsdp")), *weights, tokens)
    out_specs = (tokens, tokens, *weights)

    def step(*arrays):
        return shards(sizes, *arrays)

    return jax.shard_map(step, mesh=mesh, in_specs=in_specs, out_specs=out_specs, check_vma=False)
```

```python
import functools

import jax
import jax.numpy as jnp
from jax import lax
from jax.experimental import pallas as pl
from jax.experimental.pallas import tpu as pltpu
from jax.sharding import PartitionSpec as P

H = 32
HD = 64
BF = jnp.bfloat16
F32 = jnp.float32
LONGEST = 512
CHEAP = pl.CostEstimate(flops=1, transcendentals=0, bytes_accessed=1)


def dot(a, b, ca, cb):
    return lax.dot_general(a, b, (((ca,), (cb,)), ((), ())), preferred_element_type=F32)


def head_probs(query, key, slope, place, prefix, lanes):
    raw = dot(jnp.where(lanes, query, jnp.zeros_like(query)), key, 1, 1)
    row = place + lax.broadcasted_iota(jnp.int32, raw.shape, 0)
    column = lax.broadcasted_iota(jnp.int32, raw.shape, 1)
    distance = jnp.abs(row - column).astype(F32)
    allowed = column <= jnp.maximum(row, prefix - 1)
    logits = jnp.where(allowed, raw - slope * distance, -1e30)
    largest = jnp.max(logits, axis=-1, keepdims=True)
    exponent = jnp.exp(logits - largest)
    return exponent * (1.0 / jnp.sum(exponent, axis=-1, keepdims=True))


def forward_kernel(order_ref, prefix_ref, slope_ref, qkv_ref, out_ref):
    C, T = qkv_ref.shape[0] * qkv_ref.shape[2], qkv_ref.shape[3]
    seq, pair = pl.program_id(0), pl.program_id(1)
    at = lambda part: slice(part * 128, part * 128 + 128)
    first = lax.broadcasted_iota(jnp.int32, (T, 128), 1) < HD
    prefix = prefix_ref[seq]
    key = [qkv_ref[order_ref[0, c], 0, order_ref[1, c], :, at(1)] for c in range(C)]
    value = [qkv_ref[order_ref[0, c], 0, order_ref[1, c], :, at(2)] for c in range(C)]
    for c in range(C):
        n = min(C, max(c + 1, -(-LONGEST // T)))
        keys = jnp.concatenate(key[:n], axis=0)
        values = jnp.concatenate(value[:n], axis=0)
        query = qkv_ref[order_ref[0, c], 0, order_ref[1, c], :, at(0)] * 0.125
        out = []
        for h in range(2):
            probs = head_probs(query, keys, slope_ref[2 * pair + h], c * T, prefix, first if h == 0 else ~first)
            out.append(dot(probs.astype(BF), values, 1, 0))
        out_ref[0, c] = jnp.where(first, out[0], out[1]).astype(BF)


def backward_kernel(order_ref, prefix_ref, slope_ref, qkv_ref, d_out_ref, d_qkv_ref, d_key, d_value):
    C, T = qkv_ref.shape[0] * qkv_ref.shape[2], qkv_ref.shape[3]
    seq, pair = pl.program_id(0), pl.program_id(1)
    at = lambda part: slice(part * 128, part * 128 + 128)
    first = lax.broadcasted_iota(jnp.int32, (T, 128), 1) < HD
    prefix = prefix_ref[seq]
    d_key[...] = jnp.zeros_like(d_key)
    d_value[...] = jnp.zeros_like(d_value)
    key = [qkv_ref[order_ref[0, c], 0, order_ref[1, c], :, at(1)] for c in range(C)]
    value = [qkv_ref[order_ref[0, c], 0, order_ref[1, c], :, at(2)] for c in range(C)]
    for c in range(C):
        n = min(C, max(c + 1, -(-LONGEST // T)))
        keys = jnp.concatenate(key[:n], axis=0)
        values = jnp.concatenate(value[:n], axis=0)
        query = qkv_ref[order_ref[0, c], 0, order_ref[1, c], :, at(0)]
        d_out = d_out_ref[0, c]
        d_query = []
        for h in range(2):
            lanes = first if h == 0 else ~first
            probs = head_probs(query * 0.125, keys, slope_ref[2 * pair + h], c * T, prefix, lanes)
            mine = jnp.where(lanes, d_out, jnp.zeros_like(d_out))
            d_probs = dot(mine, values, 1, 1)
            weighted = jnp.sum(probs * d_probs, axis=-1, keepdims=True)
            d_raw = (probs * (d_probs - weighted) * 0.125).astype(BF)
            d_query.append(dot(d_raw, keys, 1, 0))
            d_value[: n * T] += dot(probs.astype(BF), mine, 0, 0)
            d_key[: n * T] += dot(d_raw, jnp.where(lanes, query, jnp.zeros_like(query)), 0, 0)
        d_qkv_ref[order_ref[0, c], 0, order_ref[1, c], :, at(0)] = jnp.where(first, d_query[0], d_query[1]).astype(BF)
    for c in range(C):
        d_qkv_ref[order_ref[0, c], 0, order_ref[1, c], :, at(1)] = d_key[c * T : (c + 1) * T].astype(BF)
        d_qkv_ref[order_ref[0, c], 0, order_ref[1, c], :, at(2)] = d_value[c * T : (c + 1) * T].astype(BF)


def attention_specs(order_ndim, K, n, Y, C, T, pair):
    near = pl.BlockSpec((K, 1, Y, T, 384), lambda s, p, *_: (0, s, 0, 0, p + pair))
    true = pl.BlockSpec((1, C, T, 128), lambda s, p, order, *_: (s ^ order[2, 0], 0, 0, p + pair))
    return near, true


def attention_forward(order, prefix, slopes, qkv):
    K, n, Y, T = qkv.shape[:4]
    C, pairs = K * Y, qkv.shape[4] // 384
    near, true = attention_specs(0, K, n, Y, C, T, 0)
    return pl.pallas_call(
        forward_kernel,
        out_shape=jax.ShapeDtypeStruct((n, C, T, pairs * 128), BF),
        grid_spec=pltpu.PrefetchScalarGridSpec(num_scalar_prefetch=3, grid=(n, pairs), in_specs=[near], out_specs=true),
        compiler_params=vmem(32),
        cost_estimate=CHEAP,
    )(order, prefix, slopes, qkv)


def attention_backward(pair, order, prefix, slopes, qkv, d_out, before=None):
    K, n, Y, T = qkv.shape[:4]
    C = K * Y
    near, true = attention_specs(0, K, n, Y, C, T, pair)
    kernel = backward_kernel
    more, aliases = [], {}
    if before is not None:
        kernel = lambda a, b, c, d, e, _, *rest: backward_kernel(a, b, c, d, e, *rest)
        more, aliases = [before], {5: 0}
    return pl.pallas_call(
        kernel,
        out_shape=jax.ShapeDtypeStruct(qkv.shape, BF),
        grid_spec=pltpu.PrefetchScalarGridSpec(
            num_scalar_prefetch=3,
            grid=(n, 1),
            in_specs=[near, true] + [pl.BlockSpec(memory_space=pl.ANY)] * len(more),
            out_specs=near,
            scratch_shapes=[pltpu.VMEM((C * T, 128), F32), pltpu.VMEM((C * T, 128), F32)],
        ),
        input_output_aliases=aliases,
        compiler_params=vmem(32),
        cost_estimate=CHEAP,
    )(order, prefix, slopes, qkv, d_out, *more)


def whole(shape):
    return pl.BlockSpec(shape, lambda *_: (0,) * len(shape))


def vmem(megabytes):
    return pltpu.CompilerParams(vmem_limit_bytes=megabytes * 1024 * 1024)


def half_turn(tile):
    return jnp.concatenate([tile[:, 64:], tile[:, :64]], axis=1)


def pack_kernel(F, C, rep_ref, joined_ref, expand_ref, out_ref):
    B = joined_ref.shape[0]
    E = expand_ref.shape[1] // (2 * F * C)
    D = joined_ref.shape[1] // 3
    first = lax.broadcasted_iota(jnp.int32, (B, 128), 1) < HD
    rep = rep_ref[0]
    keep = first == (rep == 0)
    for c in range(C):
        for p in range(F // 2):
            for q in range(3):
                one, two = [joined_ref[:, q * D + (f * C + c) * 128 :][:, :128] for f in (2 * p, 2 * p + 1)]
                mine = jnp.where(keep, jnp.where(first, one, two), half_turn(jnp.where(first, two, one)))
                out_ref[c, :, (p * 3 + q) * 128 : (p * 3 + q + 1) * 128] = mine
        for f in range(F):
            from_ = pl.multiple_of((f * C + c) * 2 * E + rep * E, 128)
            to = 3 * F * 64 + f * E
            out_ref[c, :, to : to + E] = expand_ref[:, pl.ds(from_, E)]


def pack(F, C, rep, joined, expand):
    B = joined.shape[0]
    width = 3 * F * 64 + expand.shape[1] // (2 * C)
    return pl.pallas_call(
        functools.partial(pack_kernel, F, C),
        out_shape=jax.ShapeDtypeStruct((C, B, width), BF),
        grid_spec=pltpu.PrefetchScalarGridSpec(
            num_scalar_prefetch=1,
            grid=(1,),
            in_specs=[whole(joined.shape), whole(expand.shape)],
            out_specs=whole((C, B, width)),
        ),
        compiler_params=vmem(24),
        cost_estimate=CHEAP,
    )(rep.reshape(1), joined, expand)


def unpack_joined_kernel(F, rep_ref, own_ref, other_ref, out_ref):
    C, B = own_ref.shape[:2]
    D = out_ref.shape[1] // 3
    first = lax.broadcasted_iota(jnp.int32, (B, 128), 1) < HD
    swap = rep_ref[0] == 1
    for c in range(C):
        for p in range(F // 2):
            for q in range(3):
                at = slice((p * 3 + q) * 128, (p * 3 + q + 1) * 128)
                own, other = own_ref[c, :, at].astype(F32), other_ref[c, :, at].astype(F32)
                one, two = jnp.where(swap, other, own), jnp.where(swap, own, other)
                for i, f in enumerate((2 * p, 2 * p + 1)):
                    if i == 0:
                        tile = jnp.where(first, one, half_turn(two))
                    else:
                        tile = jnp.where(first, half_turn(one), two)
                    out_ref[:, q * D + (f * C + c) * 128 : q * D + (f * C + c + 1) * 128] = tile


def unpack_expand_kernel(F, rep_ref, own_ref, other_ref, out_ref):
    C = own_ref.shape[0]
    E = own_ref.shape[2] // F
    for c in range(C):
        for f in range(F):
            at = (f * C + c) * 2 * E
            mine = pl.multiple_of(at + rep_ref[0] * E, 128)
            theirs = pl.multiple_of(at + (1 - rep_ref[0]) * E, 128)
            out_ref[:, pl.ds(mine, E)] = own_ref[c, :, f * E : (f + 1) * E].astype(F32)
            out_ref[:, pl.ds(theirs, E)] = other_ref[c, :, f * E : (f + 1) * E].astype(F32)


def unpack(kernel, F, rep, own, other):
    C, B, width = own.shape
    return pl.pallas_call(
        functools.partial(kernel, F),
        out_shape=jax.ShapeDtypeStruct((B, 2 * C * width), F32),
        grid_spec=pltpu.PrefetchScalarGridSpec(
            num_scalar_prefetch=1,
            grid=(1,),
            in_specs=[whole(own.shape), whole(own.shape)],
            out_specs=whole((B, 2 * C * width)),
        ),
        compiler_params=vmem(32),
        cost_estimate=CHEAP,
    )(rep.reshape(1), own, other)


def normed(values):
    average = jnp.mean(values, axis=-1, keepdims=True)
    centred = values - average
    variance = jnp.mean(centred * centred, axis=-1, keepdims=True)
    inverse = lax.rsqrt(variance + 1e-05)
    return centred * inverse, inverse


def norm_kernel(x_ref, gain_ref, shift_ref, out_ref):
    n, _ = normed(x_ref[...].astype(F32))
    out_ref[...] = (n * gain_ref[...] + shift_ref[...]).astype(BF)


def norm(x, gain, shift):
    rows, D = x.shape
    step = min(rows, 256)
    return pl.pallas_call(
        norm_kernel,
        out_shape=jax.ShapeDtypeStruct((rows, D), BF),
        grid=(rows // step,),
        in_specs=[pl.BlockSpec((step, D), lambda i: (i, 0)), whole((1, D)), whole((1, D))],
        out_specs=pl.BlockSpec((step, D), lambda i: (i, 0)),
        compiler_params=vmem(24),
        cost_estimate=CHEAP,
    )(x, gain.reshape(1, D), shift.reshape(1, D))


def attended_kernel(table_ref, o_ref, w_ref, v_ref, x_ref, bias_ref, gain_ref, shift_ref, mid_ref, out_ref):
    d = pl.program_id(0)
    half = pl.num_programs(0) // 2
    weight = jnp.where(d < half, w_ref[0], v_ref[0])
    product = dot(o_ref[0], weight, 1, 0)

    @pl.when(d == 0)
    def _():
        mid_ref[...] = product + x_ref[...].astype(F32) + bias_ref[...]

    @pl.when(d > 0)
    def _():
        mid_ref[...] += product

    @pl.when(d == pl.num_programs(0) - 1)
    def _():
        n, _ = normed(mid_ref[...])
        out_ref[...] = (n * gain_ref[...] + shift_ref[...]).astype(BF)


def attended(table, o, weights, x, bias, gain, shift):
    N, t, W = o.shape
    D = x.shape[1]
    half = N // 2
    weights = [w.reshape(half, W, D) for w in weights]
    return pl.pallas_call(
        attended_kernel,
        out_shape=(jax.ShapeDtypeStruct((t, D), F32), jax.ShapeDtypeStruct((t, D), BF)),
        grid_spec=pltpu.PrefetchScalarGridSpec(
            num_scalar_prefetch=1,
            grid=(N,),
            in_specs=[
                pl.BlockSpec((1, t, W), lambda d, table: (table[d], 0, 0)),
                pl.BlockSpec((1, W, D), lambda d, table: (jnp.minimum(d, half - 1), 0, 0)),
                pl.BlockSpec((1, W, D), lambda d, table: (jnp.maximum(d - half, 0), 0, 0)),
                whole((t, D)),
                whole((1, D)),
                whole((1, D)),
                whole((1, D)),
            ],
            out_specs=(whole((t, D)), whole((t, D))),
        ),
        compiler_params=vmem(32),
        cost_estimate=CHEAP,
    )(table, o, *weights, x, bias.reshape(1, D), gain.reshape(1, D), shift.reshape(1, D))


def turned_kernel(table_ref, a_ref, b_ref, c_ref, mid_ref, g_ref, gain_ref, w_ref, v_ref, d_mid_ref, d_att_ref, sums_ref, d_o_ref):
    d = pl.program_id(0)
    half = pl.num_programs(0) // 2

    @pl.when(d == 0)
    def _():
        grad = a_ref[...] + b_ref[...].astype(F32) + c_ref[...].astype(F32)
        n, inverse = normed(mid_ref[...])
        g = g_ref[...].astype(F32)
        u = grad * gain_ref[...]
        mean_u = jnp.mean(u, axis=-1, keepdims=True)
        mean_un = jnp.mean(u * n, axis=-1, keepdims=True)
        d_mid = g + (u - mean_u - n * mean_un) * inverse
        d_att = d_mid.astype(BF)
        d_mid_ref[...] = d_mid
        d_att_ref[...] = d_att
        rows = (grad * n, grad, d_att.astype(F32), g)
        for i, row in enumerate(rows):
            sums_ref[i : i + 1] = jnp.sum(row, axis=0, keepdims=True)

    weight = jnp.where(d < half, w_ref[0], v_ref[0])
    d_o_ref[0] = dot(d_att_ref[...], weight, 1, 1).astype(BF)


def turned(table, parts, mid, g, gain, weights):
    t, D = mid.shape
    N = table.shape[0]
    half = N // 2
    W = D // N
    weights = [w.reshape(half, W, D) for w in weights]
    full = whole((t, D))
    return pl.pallas_call(
        turned_kernel,
        out_shape=(
            jax.ShapeDtypeStruct((t, D), F32),
            jax.ShapeDtypeStruct((t, D), BF),
            jax.ShapeDtypeStruct((4, D), F32),
            jax.ShapeDtypeStruct((N, t, W), BF),
        ),
        grid_spec=pltpu.PrefetchScalarGridSpec(
            num_scalar_prefetch=1,
            grid=(N,),
            in_specs=[
                full,
                full,
                full,
                full,
                full,
                whole((1, D)),
                pl.BlockSpec((1, W, D), lambda d, table: (jnp.minimum(d, half - 1), 0, 0)),
                pl.BlockSpec((1, W, D), lambda d, table: (jnp.maximum(d - half, 0), 0, 0)),
            ],
            out_specs=(full, full, whole((4, D)), pl.BlockSpec((1, t, W), lambda d, table: (table[d], 0, 0))),
        ),
        compiler_params=vmem(48),
        cost_estimate=CHEAP,
    )(table, *parts, mid, g, gain.reshape(1, D), *weights)


def outer_kernel(table_ref, o_ref, d_att_ref, own_ref, oth_ref):
    d = pl.program_id(0)
    product = dot(o_ref[0], d_att_ref[...], 0, 0).astype(BF)

    @pl.when(d < pl.num_programs(0) // 2)
    def _():
        own_ref[0] = product

    @pl.when(d >= pl.num_programs(0) // 2)
    def _():
        oth_ref[0] = product


def outer(table, o, d_att):
    N, t, W = o.shape
    D = d_att.shape[1]
    half = N // 2
    return pl.pallas_call(
        outer_kernel,
        out_shape=(jax.ShapeDtypeStruct((half, W, D), BF), jax.ShapeDtypeStruct((half, W, D), BF)),
        grid_spec=pltpu.PrefetchScalarGridSpec(
            num_scalar_prefetch=1,
            grid=(N,),
            in_specs=[pl.BlockSpec((1, t, W), lambda d, table: (table[d], 0, 0)), whole((t, D))],
            out_specs=(
                pl.BlockSpec((1, W, D), lambda d, table: (jnp.minimum(d, half - 1), 0, 0)),
                pl.BlockSpec((1, W, D), lambda d, table: (jnp.maximum(d - half, 0), 0, 0)),
            ),
        ),
        compiler_params=vmem(24),
        cost_estimate=CHEAP,
    )(table, o, d_att)


def last_kernel(a_ref, b_ref, c_ref, x_ref, d_mid_ref, gain_ref, out_ref):
    grad = a_ref[...] + b_ref[...].astype(F32) + c_ref[...].astype(F32)
    n, inverse = normed(x_ref[...].astype(F32))
    u = grad * gain_ref[...]
    mean_u = jnp.mean(u, axis=-1, keepdims=True)
    mean_un = jnp.mean(u * n, axis=-1, keepdims=True)
    out_ref[...] = d_mid_ref[...] + (u - mean_u - n * mean_un) * inverse


def last(parts, x, d_mid, gain):
    t, D = x.shape
    full = whole((t, D))
    return pl.pallas_call(
        last_kernel,
        out_shape=jax.ShapeDtypeStruct((t, D), F32),
        grid=(1,),
        in_specs=[full] * 5 + [whole((1, D))],
        out_specs=full,
        compiler_params=vmem(48),
        cost_estimate=CHEAP,
    )(*parts, x, d_mid, gain.reshape(1, D))


def pair_up_kernel(rep_ref, own_ref, other_ref, out_ref):
    m = own_ref.shape[0]
    mine = pl.multiple_of(rep_ref[0] * m, 8)
    theirs = pl.multiple_of((1 - rep_ref[0]) * m, 8)
    out_ref[pl.ds(mine, m)] = own_ref[...].astype(F32)
    out_ref[pl.ds(theirs, m)] = other_ref[...].astype(F32)


def pair_up(rep, own, other):
    m, D = own.shape
    return pl.pallas_call(
        pair_up_kernel,
        out_shape=jax.ShapeDtypeStruct((2 * m, D), F32),
        grid_spec=pltpu.PrefetchScalarGridSpec(
            num_scalar_prefetch=1,
            grid=(1,),
            in_specs=[whole((m, D)), whole((m, D))],
            out_specs=whole((2 * m, D)),
        ),
        compiler_params=vmem(24),
        cost_estimate=CHEAP,
    )(rep.reshape(1), own, other)


def columns_kernel(count, *refs):
    grads, w_ref, sums_ref, gain_ref, shift_ref, rest_ref, out_ref = refs[:count], *refs[count:]
    width = grads[0].shape[1]
    by_d = jnp.zeros((w_ref.shape[0], 1), F32)
    by_g = jnp.zeros((w_ref.shape[0], 1), F32)
    for p, grad_ref in enumerate(grads):
        w = w_ref[:, p * width : (p + 1) * width].astype(F32)
        by_d += jnp.sum(w * sums_ref[:, p * width : (p + 1) * width], axis=1, keepdims=True)
        by_g += jnp.sum(w * grad_ref[...].astype(F32), axis=1, keepdims=True)
    by_n = (by_g - shift_ref[:, :1] * by_d) / gain_ref[:, :1]
    lane = lax.broadcasted_iota(jnp.int32, (w_ref.shape[0], 128), 1)
    small = jnp.where(lane == 0, by_n, jnp.where(lane == 1, by_d, rest_ref[...]))
    out_ref[:, :width] = grads[-1][...]
    out_ref[:, width:] = small.astype(BF)


def with_columns(grads, weight, sums, gain, shift, rest):
    D, width = grads[0].shape
    step = 512
    rows = lambda w: pl.BlockSpec((step, w), lambda i: (i, 0))
    return pl.pallas_call(
        functools.partial(columns_kernel, len(grads)),
        out_shape=jax.ShapeDtypeStruct((D, width + 128), BF),
        grid=(D // step,),
        in_specs=[rows(width)] * len(grads) + [rows(weight.shape[1]), whole(sums.shape), rows(128), rows(128), rows(128)],
        out_specs=rows(width + 128),
        compiler_params=vmem(32),
        cost_estimate=CHEAP,
    )(*grads, weight, sums, gain, shift, rest)


def part_weights_kernel(m, rows, early_ref, late_ref, expand_ref, shrink_ref):
    half = shrink_ref.shape[0] // 2
    width = late_ref.shape[2]
    expand_ref[...] = late_ref[0, :rows]
    shrink_ref[:half] = early_ref[0, m : m + half]
    shrink_ref[half:, :width] = late_ref[0, rows : rows + half]
    shrink_ref[half:, width:] = late_ref[0, rows + half : rows + 2 * half]


def part_weights(early, late, m, rows):
    F, _, D = early.shape
    width = late.shape[2]
    half = (late.shape[1] - rows) // 2
    return pl.pallas_call(
        functools.partial(part_weights_kernel, m, rows),
        out_shape=(jax.ShapeDtypeStruct((F * rows, width), BF), jax.ShapeDtypeStruct((F * 2 * half, D), BF)),
        grid=(F,),
        in_specs=[
            pl.BlockSpec((1,) + early.shape[1:], lambda f: (f, 0, 0)),
            pl.BlockSpec((1,) + late.shape[1:], lambda f: (f, 0, 0)),
        ],
        out_specs=(pl.BlockSpec((rows, width), lambda f: (f, 0)), pl.BlockSpec((2 * half, D), lambda f: (f, 0))),
        compiler_params=vmem(32),
        cost_estimate=CHEAP,
    )(early, late)


def gelu_and_slope(values):
    half = 0.5 + 0.5 * lax.erf(values * 0.7071067811865476)
    density = jnp.exp(values * values * -0.5) * 0.3989422804014327
    return (values * half).astype(BF), (half + values * density).astype(BF)


def together(*values):
    return lax.optimization_barrier(values)


class Plain:
    def __init__(self, R, C):
        self.R, self.C, self.N = R, C, R * C
        self.axes = ("rep", "ctx")
        self.groups = (1, R, C)
        place = jnp.arange(C, dtype=jnp.int32)
        self.order = jnp.stack([place * 0, place, place * 0])
        self.table = jnp.arange(self.N, dtype=jnp.int32)

    def gather(self, x, beside=()):
        out, beside = together(lax.all_gather(x, self.axes, axis=0, tiled=True), beside)
        return [out], beside

    def scatter_core(self, rows, part):
        return part(0, 0, self.N * rows).astype(BF)

    def scatter_far(self, state):
        return state

    def scatter_near(self, state):
        return lax.psum_scatter(state, self.axes, scatter_dimension=0, tiled=True)

    def scatter_end(self, state):
        return state.astype(F32), jnp.zeros_like(state), jnp.zeros_like(state)

    def swap(self, parts):
        return lax.all_to_all(parts, self.axes, 0, 0, tiled=True)

    def swap_ctx(self, blocks):
        return lax.all_to_all(blocks, "ctx", 0, 0, tiled=True)

    def prefixes(self, prefix):
        return lax.all_gather(prefix, "rep", axis=0, tiled=True)


class Near(Plain):
    def __init__(self, R, F, C):
        super().__init__(R, C)
        self.F = F
        self.ctx = lax.axis_index("ctx")
        self.rep = lax.axis_index("rep")
        self.fsdp = lax.axis_index("fsdp")
        self.groups = (2, 2, 2)
        place = jnp.arange(C, dtype=jnp.int32) ^ self.ctx
        self.order = jnp.stack([place & 1, place >> 1, place * 0 + self.rep])
        d = jnp.arange(8, dtype=jnp.int32)
        self.table = (self.rep * 4 + self.ctx) ^ ((d & 2) * 2 + (d & 1) * 2 + (d >> 2))

    def over(self, x, d):
        return lax.ppermute(x, "ctx", [(i, i ^ d) for i in range(4)])

    def x(self, x):
        return lax.ppermute(x, "rep", [(0, 1), (1, 0)])

    def y(self, x):
        return self.over(x, 2)

    def core(self, x):
        return self.over(x, 1)

    def gather(self, x, beside=()):
        half = x.shape[0] // 2
        from_x, from_y = self.x(x), self.y(x)
        if beside:
            from_x, from_y, beside = together(from_x, from_y, beside)
        own = jnp.concatenate([x, from_y, from_x, self.y(from_x[:half]), self.x(from_y[half:])], axis=0)
        return [own, self.core(own)], beside

    def scatter_core(self, rows, part):
        far_x = part(1, 2 * rows, 4 * rows).astype(BF)
        near_x = part(1, 0, 2 * rows).astype(BF)
        far_x = part(0, 2 * rows, 4 * rows) + self.core(far_x).astype(F32)
        near_x = part(0, 0, 2 * rows) + self.core(near_x).astype(F32)
        return far_x, near_x

    def scatter_given(self, own, oth):
        total = (own.astype(F32) + self.core(oth).astype(F32)).astype(BF)
        return total[total.shape[0] // 2 :], total[: total.shape[0] // 2]

    def scatter_far(self, state):
        far_x, near_x = state
        rows = far_x.shape[0] // 2
        far = far_x[rows:].astype(BF)
        return far_x[:rows].astype(F32), near_x.astype(F32), self.y(far[: rows // 2]), self.x(far[rows // 2 :])

    def scatter_near(self, state):
        by_x, near_x, to_y, to_x = state
        rows = by_x.shape[0]
        half = rows // 2
        by_x = jnp.concatenate([by_x[:half] + to_y.astype(F32), by_x[half:]], axis=0)
        by_y = jnp.concatenate([near_x[rows : rows + half], near_x[rows + half :] + to_x.astype(F32)], axis=0)
        return near_x[:rows], self.x(by_x.astype(BF)), self.y(by_y.astype(BF))

    def scatter_end(self, state):
        return state

    def prefixes(self, prefix):
        return jnp.concatenate([prefix, self.x(prefix)])

    def gather_ctx(self, x):
        x = jnp.stack([x, self.y(x)])
        x = jnp.stack([x, self.core(x)], axis=1).reshape(4, *x.shape[1:])
        x = jnp.take(x, jnp.arange(4) ^ self.ctx, axis=0)
        return x.transpose(1, 0, 2).reshape(-1, x.shape[2])


def added(parts):
    return sum(a.astype(F32) for a in parts)


def scatter_shifts(x, axis, size):
    me = lax.axis_index(axis)
    total = lax.dynamic_index_in_dim(x, me, 0, keepdims=False)
    for s in range(1, size):
        mine = lax.dynamic_index_in_dim(x, lax.rem(me + s, size), 0, keepdims=False)
        total = total.astype(F32) + lax.ppermute(mine, axis, [(i, (i + s) % size) for i in range(size)]).astype(F32)
    return total.astype(x.dtype)


def shards(
    sizes,
    inputs,
    prefix,
    joined_weight,
    query_bias,
    value_bias,
    dense_weight,
    dense_bias,
    expand_weight,
    expand_bias,
    shrink_weight,
    shrink_bias,
    first_gain,
    first_shift,
    second_gain,
    second_shift,
    cotangent,
):
    R, F, C = sizes
    N = R * C
    rep = lax.axis_index("rep")
    ctx = lax.axis_index("ctx")
    S, t, D = inputs.shape
    assert S == 1
    B = joined_weight.shape[0]
    FFB = shrink_weight.shape[0]
    FF = FFB * F * C
    E = FFB // R
    W = D // N
    near = R == 2 and C == 4 and B == 2 * HD
    tp = Near(R, F, C) if near else Plain(R, C)
    K, _, Y = tp.groups
    G = range(K)
    n = N // K
    pairs = W // 128

    def half_rows(weight):
        m = weight.shape[0] // R
        return lax.dynamic_slice_in_dim(weight, rep * m, m, 0)

    def widen(blocks):
        return lax.all_gather(blocks.reshape(C * B, -1), "fsdp", axis=0, tiled=True)

    def over_rep(x):
        return lax.ppermute(x, "rep", [(0, 1), (1, 0)])

    x = inputs.reshape(t, D)
    g = cotangent.reshape(t, D)
    small = jnp.concatenate(
        [first_gain, first_shift, second_gain, second_shift, dense_bias, shrink_bias, query_bias, value_bias, expand_bias]
    )
    if near:
        low, high = jnp.split(half_rows(shrink_weight), 2)
        m = B // R
        small = jnp.pad(small.reshape(1, -1), ((0, 15), (0, D - small.shape[0])))
        early = lax.all_gather(jnp.concatenate([half_rows(dense_weight), low, small]), "fsdp", axis=0, tiled=False)
        dense_rows = early[:, :m].reshape(F * m, D)
        small = tp.gather_ctx(early[:, m + low.shape[0], : 8 * B + FFB])
        blocks = lax.all_to_all(pack(F, C, rep, joined_weight, expand_weight), "ctx", 0, 0, tiled=True)
        joined_blocks, expand_blocks = blocks[:, :, : 3 * W], blocks[:, :, 3 * W :]
    else:
        dense_rows = lax.all_gather(dense_weight, ("fsdp", "ctx"), axis=0, tiled=True)
        small = lax.all_gather(small, ("fsdp", "ctx"), axis=0, tiled=False)
        pieces = joined_weight.reshape(B, 3, R, C, pairs, 128)
        pieces = lax.dynamic_index_in_dim(pieces, rep, 2, keepdims=False).transpose(2, 0, 3, 1, 4)
        joined_blocks = lax.all_to_all(pieces.reshape(C, B, 3 * W), "ctx", 0, 0, tiled=True)
        pieces = expand_weight.reshape(B, F, C, R, E)
        pieces = lax.dynamic_index_in_dim(pieces, rep, 3, keepdims=False).transpose(2, 0, 1, 3)
        expand_blocks = lax.all_to_all(pieces.reshape(C, B, F * E), "ctx", 0, 0, tiled=True)
    joined_cols = widen(joined_blocks)
    if near:
        late = jnp.concatenate([expand_blocks.reshape(C * B, -1), high[:, : D // 2], high[:, D // 2 :]])
        late = lax.all_gather(late, "fsdp", axis=0, tiled=False)
        expand_cols, shrink_rows = part_weights(early, late, m, C * B)
    else:
        expand_cols = widen(expand_blocks)
        shrink_rows = lax.all_gather(half_rows(shrink_weight), "fsdp", axis=0, tiled=True)
    prefixes = tp.prefixes(prefix)
    x_all, _ = tp.gather(x)

    small = small.astype(F32)
    gain_one, shift_one, gain_two, shift_two, dbias, sbias, qbias, vbias = [
        small[:, i * B : (i + 1) * B].reshape(D) for i in range(8)
    ]
    ebias = small[:, 8 * B :].reshape(F, C, R, E)
    ebias = lax.dynamic_index_in_dim(lax.dynamic_index_in_dim(ebias, ctx, 1, False), rep, 1, False)
    ebias = ebias.reshape(F * E)

    def my_features(vector):
        if near:
            v = vector.reshape(F, C, R, -1)
            return lax.dynamic_index_in_dim(lax.dynamic_index_in_dim(v, ctx, 1, False), rep, 1, False).reshape(W)
        return lax.dynamic_slice_in_dim(vector, (rep * C + ctx) * W, W, 0)

    my_heads = my_features(jnp.repeat(jnp.arange(H, dtype=jnp.int32), HD)).reshape(-1, HD)[:, 0]
    slopes = jnp.exp2(-8.0 * (my_heads.astype(F32) + 1.0) / H)

    a1_all = [norm(a, gain_one, shift_one) for a in x_all]
    if near:
        a1_all, dense_rows = together(a1_all, dense_rows)
        dense_all, _ = tp.gather(dense_rows)
        own, g = together(dense_all[0], g)
        dense_all[0] = own
    else:
        dense_all = [dense_rows[: D // 2], dense_rows[D // 2 :]]
    g_all, _ = tp.gather(g)
    qkv_bias = jnp.stack([my_features(qbias), jnp.zeros((W,), F32), my_features(vbias)])
    qkv_bias = qkv_bias.reshape(3, pairs, 128).transpose(1, 0, 2).reshape(3 * W)
    qkv = jnp.stack([(dot(a, joined_cols, 1, 0) + qkv_bias).astype(BF) for a in a1_all])
    qkv = qkv.reshape(K, R, Y, t, 3 * W)
    out = attention_forward(tp.order, prefixes, slopes, qkv)
    o = tp.swap(out.reshape(N, t, W))
    o, g_all = together(o, g_all)
    midway, a2 = attended(tp.table, o, dense_all, x, dbias, gain_two, shift_two)

    a2_all, _ = tp.gather(a2)
    act, slope = zip(*[gelu_and_slope(dot(a, expand_cols, 1, 0) + ebias) for a in a2_all])
    shrink_grad = sum(dot(act[i], g_all[i], 0, 0) for i in G).astype(BF)
    slope, shrink_grad, act = together(slope, shrink_grad, act)
    shrink_part = lax.psum_scatter(shrink_grad, "fsdp", scatter_dimension=0, tiled=True)
    d_exp = [(dot(g_all[i], shrink_rows, 1, 1) * slope[i].astype(F32)).astype(BF) for i in G]

    d_a2 = tp.scatter_core(t, lambda i, a, b: dot(d_exp[i][a:b], expand_cols, 1, 1))
    d_a2, d_exp = together(tp.scatter_far(d_a2), d_exp)
    d_a2 = tp.scatter_near(d_a2)
    expand_grad = sum(dot(a2_all[i], d_exp[i], 0, 0) for i in G).astype(BF)
    d_a2, expand_grad = together(d_a2, expand_grad)
    d_mid, d_att, sums_two, d_o = turned(tp.table, tp.scatter_end(d_a2), midway, g, gain_two, dense_all)
    d_o, expand_grad, shrink_part = together(d_o, expand_grad, shrink_part)
    expand_part = lax.psum_scatter(expand_grad, "fsdp", scatter_dimension=0, tiled=True)

    d_o = tp.swap(d_o).reshape(R, C, t, W)
    shrink_other = over_rep(shrink_part)
    dense_part = outer(tp.table, o, d_att) if near else ()
    d_o, dense_part = together(d_o, dense_part)
    if near:
        dense_part = tp.scatter_given(*[a.reshape(n * W, D) for a in dense_part])
    d_qkv, joined_grad = None, []
    for p in range(pairs):
        d_qkv = attention_backward(p, tp.order, prefixes, slopes[2 * p : 2 * p + 2], qkv, d_o, d_qkv)
        mine = d_qkv.reshape(K, n * t, 3 * W)[:, :, 384 * p : 384 * (p + 1)]
        grad = sum(dot(a1_all[i], mine[i], 0, 0) for i in G).astype(BF)
        d_qkv, grad, d_o, act, dense_part = together(d_qkv, grad, d_o, act, dense_part)
        joined_grad.append(grad)
        if p == 0 and near:
            dense_part = tp.scatter_far(dense_part)
    d_qkv = d_qkv.reshape(K, n * t, 3 * W)

    d_qkv_sum = jnp.sum(d_qkv.astype(F32), axis=(0, 1))
    d_exp_sum = sum(jnp.sum(d.astype(F32), axis=0) for d in d_exp)

    def place(vector, width):
        if near or width != D:
            full = jnp.zeros((F, C, R, width // (F * C * R)), F32)
            full = lax.dynamic_update_slice(full, vector.reshape(F, 1, 1, -1), (0, ctx, rep, 0))
            return full.reshape(F * C, width // D, B).transpose(0, 2, 1).reshape(D, width // D)
        return lax.dynamic_update_slice_in_dim(jnp.zeros((width,), F32), vector, (rep * C + ctx) * W, 0).reshape(D, 1)

    by_part = d_qkv_sum.reshape(pairs, 3, 128)
    rest = [jnp.zeros((D, 2), F32), sums_two.T, place(by_part[:, 0].reshape(W), D), place(by_part[:, 2].reshape(W), D)]
    rest.append(place(d_exp_sum, FF))
    rest = jnp.concatenate(rest, axis=1)
    used = rest.shape[1]
    rest = jnp.pad(rest, ((0, 0), (0, 128 - used)))
    lanes = lambda a: jnp.broadcast_to(a[:, None], (D, 128))
    grad = with_columns(joined_grad, joined_cols, d_qkv_sum.reshape(1, 3 * W), lanes(gain_one), lanes(shift_one), rest)
    expand_part, shrink_other, joined_grad = together(expand_part, shrink_other, joined_grad[:-1] + [grad])
    joined_part = [lax.psum_scatter(a, "fsdp", scatter_dimension=0, tiled=True) for a in joined_grad]
    expand_own = lax.all_to_all(expand_part.reshape(C, B, -1), "ctx", 0, 0, tiled=True)

    d_a1 = tp.scatter_core(t, lambda i, a, b: dot(d_qkv[i, a:b], joined_cols, 1, 1))
    if near:
        dense_part = tp.scatter_near(dense_part)
    d_a1, expand_own, dense_part, act = together(d_a1, expand_own, dense_part, act)
    d_a1 = tp.scatter_far(d_a1)
    expand_other = over_rep(expand_own)
    if near:
        shrink_out = pair_up(rep, shrink_part, shrink_other)
        dense_part = added(tp.scatter_end(dense_part)).astype(BF).reshape(F, W // F, D)
        dense_part = scatter_shifts(dense_part, "fsdp", F)

    branch = tp.scatter_core(t, lambda i, a, b: dot(act[i][a:b], shrink_rows, 1, 0))
    d_a1, branch, dense_part = together(d_a1, branch, dense_part)
    d_a1 = tp.scatter_near(d_a1)
    branch = tp.scatter_far(branch)
    d_a1, branch, expand_other = together(d_a1, branch, expand_other)
    if near:
        expand_out = unpack(unpack_expand_kernel, F, rep, expand_own, expand_other)
    branch = tp.scatter_near(branch)
    input_gradient = last(tp.scatter_end(d_a1), x, d_mid, gain_one)
    branch, input_gradient = together(branch, input_gradient)
    layer_output = midway + added(tp.scatter_end(branch)) + sbias

    def both_reps(own, other):
        first = rep == 0
        return jnp.stack([jnp.where(first, own, other), jnp.where(first, other, own)])

    joined_own = [lax.all_to_all(a.reshape(C, B, -1), "ctx", 0, 0, tiled=True) for a in joined_part]
    joined_other = [over_rep(a) for a in joined_own]
    little = jnp.sum((joined_own[-1][:, :, 384:].astype(F32) + joined_other[-1][:, :, 384:].astype(F32)), axis=0).T
    joined_own = jnp.concatenate([a[:, :, :384] for a in joined_own], axis=2)
    joined_other = jnp.concatenate([a[:, :, :384] for a in joined_other], axis=2)
    if near:
        joined_out = unpack(unpack_joined_kernel, F, rep, joined_own, joined_other)
        dense_out = pair_up(rep, dense_part, over_rep(dense_part))
    else:
        both = both_reps(expand_own, expand_other).reshape(R, C, B, F, E).transpose(2, 3, 1, 0, 4)
        expand_out = both.reshape(B, FF).astype(F32)
        both = both_reps(joined_own, joined_other).reshape(R, C, B, pairs, 3, 128).transpose(2, 4, 0, 1, 3, 5)
        joined_out = both.reshape(B, 3 * D).astype(F32)
        shrink_out = both_reps(shrink_part, shrink_other).reshape(FFB, D).astype(F32)
        part = dot(o.transpose(1, 0, 2).reshape(t, D), d_att, 0, 0).astype(BF)
        part = lax.psum_scatter(part, ("fsdp", "ctx"), scatter_dimension=0, tiled=True)
        dense_out = lax.psum(part, "rep").astype(F32)
    gain_one_out, shift_one_out, gain_two_out, shift_two_out, dbias_out, sbias_out, qbias_out, vbias_out = [
        little[i] for i in range(8)
    ]
    ebias_out = little[8:used].reshape(FFB)

    return (
        layer_output.reshape(S, t, D),
        input_gradient.reshape(S, t, D),
        joined_out,
        qbias_out,
        vbias_out,
        dense_out,
        dbias_out,
        expand_out,
        ebias_out,
        shrink_out,
        sbias_out,
        gain_one_out,
        shift_one_out,
        gain_two_out,
        shift_two_out,
    )


def solution(mesh):
    sizes = (mesh.shape["rep"], mesh.shape["fsdp"], mesh.shape["ctx"])
    tokens = P(("rep", "fsdp"), "ctx", None)
    matrix = P(("fsdp", "ctx"), None)
    vector = P(("fsdp", "ctx"))
    weights = (matrix, vector, vector, matrix, vector, matrix, vector, matrix, vector, vector, vector, vector, vector)
    in_specs = (tokens, P(("rep", "fsdp")), *weights, tokens)
    out_specs = (tokens, tokens, *weights)

    def step(*arrays):
        return shards(sizes, *arrays)

    return jax.shard_map(step, mesh=mesh, in_specs=in_specs, out_specs=out_specs, check_vma=False)
```

```python
import functools

import jax
import jax.numpy as jnp
from jax import lax
from jax.experimental import pallas as pl
from jax.experimental.pallas import tpu as pltpu
from jax.sharding import PartitionSpec as P

H = 32
HD = 64
BF = jnp.bfloat16
F32 = jnp.float32
LONGEST = 512
CHEAP = pl.CostEstimate(flops=1, transcendentals=0, bytes_accessed=1)


def dot(a, b, ca, cb):
    return lax.dot_general(a, b, (((ca,), (cb,)), ((), ())), preferred_element_type=F32)


def places(c, n, T, prefix):
    before = lax.broadcasted_iota(jnp.int32, (1, c * T), 1).astype(F32) - c * T if c else None
    row = lax.broadcasted_iota(jnp.int32, (T, (n - c) * T), 0)
    column = lax.broadcasted_iota(jnp.int32, (T, (n - c) * T), 1)
    allowed = column <= jnp.maximum(row, prefix - 1 - c * T)
    return before, jnp.minimum(column, 2 * row - column).astype(F32), allowed


def head_probs(query, key, slope, place, lanes):
    before, near, allowed = place
    raw = dot(jnp.where(lanes, query, jnp.zeros_like(query)), key, 1, 1)
    split = raw.shape[1] - near.shape[1]
    logits = jnp.where(allowed, raw[:, split:] + slope * near, -1e30)
    if split:
        logits = jnp.concatenate([raw[:, :split] + slope * before, logits], axis=1)
    largest = jnp.max(logits, axis=-1, keepdims=True)
    exponent = jnp.exp(logits - largest)
    return exponent * (1.0 / jnp.sum(exponent, axis=-1, keepdims=True))


def forward_kernel(order_ref, prefix_ref, slope_ref, qkv_ref, out_ref):
    C, T = qkv_ref.shape[0] * qkv_ref.shape[2], qkv_ref.shape[3]
    seq, pair = pl.program_id(0), pl.program_id(1)
    at = lambda part: slice(part * 128, part * 128 + 128)
    first = lax.broadcasted_iota(jnp.int32, (T, 128), 1) < HD
    key = [qkv_ref[order_ref[0, c], 0, order_ref[1, c], :, at(1)] for c in range(C)]
    value = [qkv_ref[order_ref[0, c], 0, order_ref[1, c], :, at(2)] for c in range(C)]
    for c in range(C):
        n = min(C, max(c + 1, -(-LONGEST // T)))
        keys = jnp.concatenate(key[:n], axis=0)
        values = jnp.concatenate(value[:n], axis=0)
        query = qkv_ref[order_ref[0, c], 0, order_ref[1, c], :, at(0)] * 0.125
        place = places(c, n, T, prefix_ref[seq])
        out = []
        for h in range(2):
            probs = head_probs(query, keys, slope_ref[2 * pair + h], place, first if h == 0 else ~first)
            out.append(dot(probs.astype(BF), values, 1, 0))
        out_ref[0, c] = jnp.where(first, out[0], out[1]).astype(BF)


def backward_kernel(order_ref, prefix_ref, slope_ref, qkv_ref, d_out_ref, d_qkv_ref, d_key, d_value):
    C, T = qkv_ref.shape[0] * qkv_ref.shape[2], qkv_ref.shape[3]
    seq, pair = pl.program_id(0), pl.program_id(1)
    at = lambda part: slice(part * 128, part * 128 + 128)
    first = lax.broadcasted_iota(jnp.int32, (T, 128), 1) < HD
    d_key[...] = jnp.zeros_like(d_key)
    d_value[...] = jnp.zeros_like(d_value)
    key = [qkv_ref[order_ref[0, c], 0, order_ref[1, c], :, at(1)] for c in range(C)]
    value = [qkv_ref[order_ref[0, c], 0, order_ref[1, c], :, at(2)] for c in range(C)]
    for c in range(C):
        n = min(C, max(c + 1, -(-LONGEST // T)))
        keys = jnp.concatenate(key[:n], axis=0)
        values = jnp.concatenate(value[:n], axis=0)
        query = qkv_ref[order_ref[0, c], 0, order_ref[1, c], :, at(0)]
        d_out = d_out_ref[0, c]
        place = places(c, n, T, prefix_ref[seq])
        d_query = []
        for h in range(2):
            lanes = first if h == 0 else ~first
            probs = head_probs(query * 0.125, keys, slope_ref[2 * pair + h], place, lanes)
            mine = jnp.where(lanes, d_out, jnp.zeros_like(d_out))
            d_probs = dot(mine, values, 1, 1)
            weighted = jnp.sum(probs * d_probs, axis=-1, keepdims=True)
            d_raw = (probs * (d_probs - weighted) * 0.125).astype(BF)
            d_query.append(dot(d_raw, keys, 1, 0))
            d_value[: n * T] += dot(probs.astype(BF), mine, 0, 0)
            d_key[: n * T] += dot(d_raw, jnp.where(lanes, query, jnp.zeros_like(query)), 0, 0)
        d_qkv_ref[order_ref[0, c], 0, order_ref[1, c], :, at(0)] = jnp.where(first, d_query[0], d_query[1]).astype(BF)
    for c in range(C):
        d_qkv_ref[order_ref[0, c], 0, order_ref[1, c], :, at(1)] = d_key[c * T : (c + 1) * T].astype(BF)
        d_qkv_ref[order_ref[0, c], 0, order_ref[1, c], :, at(2)] = d_value[c * T : (c + 1) * T].astype(BF)


def attention_specs(order_ndim, K, n, Y, C, T, pair):
    near = pl.BlockSpec((K, 1, Y, T, 384), lambda s, p, *_: (0, s, 0, 0, p + pair))
    true = pl.BlockSpec((1, C, T, 128), lambda s, p, order, *_: (s ^ order[2, 0], 0, 0, p + pair))
    return near, true


def attention_forward(order, prefix, slopes, qkv):
    K, n, Y, T = qkv.shape[:4]
    C, pairs = K * Y, qkv.shape[4] // 384
    near, true = attention_specs(0, K, n, Y, C, T, 0)
    return pl.pallas_call(
        forward_kernel,
        out_shape=jax.ShapeDtypeStruct((n, C, T, pairs * 128), BF),
        grid_spec=pltpu.PrefetchScalarGridSpec(num_scalar_prefetch=3, grid=(n, pairs), in_specs=[near], out_specs=true),
        compiler_params=vmem(32),
        cost_estimate=pl.CostEstimate(flops=12 * 10**9, transcendentals=0, bytes_accessed=1),
    )(order, prefix, slopes, qkv)


def attention_backward(pair, order, prefix, slopes, qkv, d_out, before=None):
    K, n, Y, T = qkv.shape[:4]
    C = K * Y
    near, true = attention_specs(0, K, n, Y, C, T, pair)
    kernel = backward_kernel
    more, aliases = [], {}
    if before is not None:
        kernel = lambda a, b, c, d, e, _, *rest: backward_kernel(a, b, c, d, e, *rest)
        more, aliases = [before], {5: 0}
    return pl.pallas_call(
        kernel,
        out_shape=jax.ShapeDtypeStruct(qkv.shape, BF),
        grid_spec=pltpu.PrefetchScalarGridSpec(
            num_scalar_prefetch=3,
            grid=(n, 1),
            in_specs=[near, true] + [pl.BlockSpec(memory_space=pl.ANY)] * len(more),
            out_specs=near,
            scratch_shapes=[pltpu.VMEM((C * T, 128), F32), pltpu.VMEM((C * T, 128), F32)],
        ),
        input_output_aliases=aliases,
        compiler_params=vmem(32),
        cost_estimate=pl.CostEstimate(flops=12 * 10**9, transcendentals=0, bytes_accessed=1),
    )(order, prefix, slopes, qkv, d_out, *more)


def whole(shape):
    return pl.BlockSpec(shape, lambda *_: (0,) * len(shape))


def vmem(megabytes):
    return pltpu.CompilerParams(vmem_limit_bytes=megabytes * 1024 * 1024)


def half_turn(tile):
    return jnp.concatenate([tile[:, 64:], tile[:, :64]], axis=1)


def pack_kernel(F, C, rep_ref, joined_ref, expand_ref, out_ref):
    B = joined_ref.shape[0]
    E = expand_ref.shape[1] // (2 * F * C)
    D = joined_ref.shape[1] // 3
    first = lax.broadcasted_iota(jnp.int32, (B, 128), 1) < HD
    rep = rep_ref[0]
    keep = first == (rep == 0)
    for c in range(C):
        for p in range(F // 2):
            for q in range(3):
                one, two = [joined_ref[:, q * D + (f * C + c) * 128 :][:, :128] for f in (2 * p, 2 * p + 1)]
                mine = jnp.where(keep, jnp.where(first, one, two), half_turn(jnp.where(first, two, one)))
                out_ref[c, :, (p * 3 + q) * 128 : (p * 3 + q + 1) * 128] = mine
        for f in range(F):
            from_ = pl.multiple_of((f * C + c) * 2 * E + rep * E, 128)
            to = 3 * F * 64 + f * E
            out_ref[c, :, to : to + E] = expand_ref[:, pl.ds(from_, E)]


def pack(F, C, rep, joined, expand):
    B = joined.shape[0]
    width = 3 * F * 64 + expand.shape[1] // (2 * C)
    return pl.pallas_call(
        functools.partial(pack_kernel, F, C),
        out_shape=jax.ShapeDtypeStruct((C, B, width), BF),
        grid_spec=pltpu.PrefetchScalarGridSpec(
            num_scalar_prefetch=1,
            grid=(1,),
            in_specs=[whole(joined.shape), whole(expand.shape)],
            out_specs=whole((C, B, width)),
        ),
        compiler_params=vmem(24),
        cost_estimate=CHEAP,
    )(rep.reshape(1), joined, expand)


def unpack_joined_kernel(F, ref, out_ref):
    C, B = ref.shape[1:3]
    D = out_ref.shape[1] // 3
    first = lax.broadcasted_iota(jnp.int32, (B, 128), 1) < HD
    for c in range(C):
        for p in range(F // 2):
            for q in range(3):
                at = slice((p * 3 + q) * 128, (p * 3 + q + 1) * 128)
                one, two = ref[0, c, :, at].astype(F32), ref[1, c, :, at].astype(F32)
                for i, f in enumerate((2 * p, 2 * p + 1)):
                    tile = jnp.where(first, half_turn(one) if i else one, two if i else half_turn(two))
                    out_ref[:, q * D + (f * C + c) * 128 : q * D + (f * C + c + 1) * 128] = tile


def unpack_expand_kernel(F, ref, out_ref):
    C = ref.shape[1]
    E = ref.shape[3] // F
    for c in range(C):
        for f in range(F):
            for r in range(2):
                at = ((f * C + c) * 2 + r) * E
                out_ref[:, at : at + E] = ref[r, c, :, f * E : (f + 1) * E].astype(F32)


def unpack(kernel, F, parts, extra=0):
    R, C, B, width = parts.shape
    width -= extra
    return pl.pallas_call(
        functools.partial(kernel, F),
        out_shape=jax.ShapeDtypeStruct((B, R * C * width), F32),
        grid=(1,),
        in_specs=[whole((R, C, B, width))],
        out_specs=whole((B, R * C * width)),
        compiler_params=vmem(32),
        cost_estimate=CHEAP,
    )(parts)


def normed(values):
    average = jnp.mean(values, axis=-1, keepdims=True)
    centred = values - average
    variance = jnp.mean(centred * centred, axis=-1, keepdims=True)
    inverse = lax.rsqrt(variance + 1e-05)
    return centred * inverse, inverse


def norm_kernel(x_ref, gain_ref, shift_ref, out_ref):
    n, _ = normed(x_ref[...].astype(F32))
    out_ref[...] = (n * gain_ref[...] + shift_ref[...]).astype(BF)


def norm(x, gain, shift):
    rows, D = x.shape
    step = min(rows, 256)
    return pl.pallas_call(
        norm_kernel,
        out_shape=jax.ShapeDtypeStruct((rows, D), BF),
        grid=(rows // step,),
        in_specs=[pl.BlockSpec((step, D), lambda i: (i, 0)), whole((1, D)), whole((1, D))],
        out_specs=pl.BlockSpec((step, D), lambda i: (i, 0)),
        compiler_params=vmem(24),
        cost_estimate=CHEAP,
    )(x, gain.reshape(1, D), shift.reshape(1, D))


def attended_kernel(table_ref, o_ref, w_ref, v_ref, x_ref, bias_ref, gain_ref, shift_ref, mid_ref, out_ref):
    d = pl.program_id(0)
    half = pl.num_programs(0) // 2
    weight = jnp.where(d < half, w_ref[0], v_ref[0])
    product = dot(o_ref[0], weight, 1, 0)

    @pl.when(d == 0)
    def _():
        mid_ref[...] = product + x_ref[...].astype(F32) + bias_ref[...]

    @pl.when(d > 0)
    def _():
        mid_ref[...] += product

    @pl.when(d == pl.num_programs(0) - 1)
    def _():
        n, _ = normed(mid_ref[...])
        out_ref[...] = (n * gain_ref[...] + shift_ref[...]).astype(BF)


def attended(table, o, weights, x, bias, gain, shift):
    N, t, W = o.shape
    D = x.shape[1]
    half = N // 2
    weights = [w.reshape(half, W, D) for w in weights]
    return pl.pallas_call(
        attended_kernel,
        out_shape=(jax.ShapeDtypeStruct((t, D), F32), jax.ShapeDtypeStruct((t, D), BF)),
        grid_spec=pltpu.PrefetchScalarGridSpec(
            num_scalar_prefetch=1,
            grid=(N,),
            in_specs=[
                pl.BlockSpec((1, t, W), lambda d, table: (table[d], 0, 0)),
                pl.BlockSpec((1, W, D), lambda d, table: (jnp.minimum(d, half - 1), 0, 0)),
                pl.BlockSpec((1, W, D), lambda d, table: (jnp.maximum(d - half, 0), 0, 0)),
                whole((t, D)),
                whole((1, D)),
                whole((1, D)),
                whole((1, D)),
            ],
            out_specs=(whole((t, D)), whole((t, D))),
        ),
        compiler_params=vmem(32),
        cost_estimate=CHEAP,
    )(table, o, *weights, x, bias.reshape(1, D), gain.reshape(1, D), shift.reshape(1, D))


def turned_kernel(table_ref, a_ref, b_ref, c_ref, mid_ref, g_ref, gain_ref, w_ref, v_ref, d_mid_ref, d_att_ref, sums_ref, d_o_ref):
    d = pl.program_id(0)
    half = pl.num_programs(0) // 2

    @pl.when(d == 0)
    def _():
        grad = a_ref[...] + b_ref[...].astype(F32) + c_ref[...].astype(F32)
        n, inverse = normed(mid_ref[...])
        g = g_ref[...].astype(F32)
        u = grad * gain_ref[...]
        mean_u = jnp.mean(u, axis=-1, keepdims=True)
        mean_un = jnp.mean(u * n, axis=-1, keepdims=True)
        d_mid = g + (u - mean_u - n * mean_un) * inverse
        d_att = d_mid.astype(BF)
        d_mid_ref[...] = d_mid
        d_att_ref[...] = d_att
        rows = (grad * n, grad, d_att.astype(F32), g)
        for i, row in enumerate(rows):
            sums_ref[i : i + 1] = jnp.sum(row, axis=0, keepdims=True)

    weight = jnp.where(d < half, w_ref[0], v_ref[0])
    d_o_ref[0] = dot(d_att_ref[...], weight, 1, 1).astype(BF)


def turned(table, parts, mid, g, gain, weights):
    t, D = mid.shape
    N = table.shape[0]
    half = N // 2
    W = D // N
    weights = [w.reshape(half, W, D) for w in weights]
    full = whole((t, D))
    return pl.pallas_call(
        turned_kernel,
        out_shape=(
            jax.ShapeDtypeStruct((t, D), F32),
            jax.ShapeDtypeStruct((t, D), BF),
            jax.ShapeDtypeStruct((4, D), F32),
            jax.ShapeDtypeStruct((N, t, W), BF),
        ),
        grid_spec=pltpu.PrefetchScalarGridSpec(
            num_scalar_prefetch=1,
            grid=(N,),
            in_specs=[
                full,
                full,
                full,
                full,
                full,
                whole((1, D)),
                pl.BlockSpec((1, W, D), lambda d, table: (jnp.minimum(d, half - 1), 0, 0)),
                pl.BlockSpec((1, W, D), lambda d, table: (jnp.maximum(d - half, 0), 0, 0)),
            ],
            out_specs=(full, full, whole((4, D)), pl.BlockSpec((1, t, W), lambda d, table: (table[d], 0, 0))),
        ),
        compiler_params=vmem(48),
        cost_estimate=CHEAP,
    )(table, *parts, mid, g, gain.reshape(1, D), *weights)


def outer_kernel(table_ref, o_ref, d_att_ref, own_ref, oth_ref):
    d = pl.program_id(0)
    product = dot(o_ref[0], d_att_ref[...], 0, 0).astype(BF)

    @pl.when(d < pl.num_programs(0) // 2)
    def _():
        own_ref[0] = product

    @pl.when(d >= pl.num_programs(0) // 2)
    def _():
        oth_ref[0] = product


def outer(table, o, d_att):
    N, t, W = o.shape
    D = d_att.shape[1]
    half = N // 2
    return pl.pallas_call(
        outer_kernel,
        out_shape=(jax.ShapeDtypeStruct((half, W, D), BF), jax.ShapeDtypeStruct((half, W, D), BF)),
        grid_spec=pltpu.PrefetchScalarGridSpec(
            num_scalar_prefetch=1,
            grid=(N,),
            in_specs=[pl.BlockSpec((1, t, W), lambda d, table: (table[d], 0, 0)), whole((t, D))],
            out_specs=(
                pl.BlockSpec((1, W, D), lambda d, table: (jnp.minimum(d, half - 1), 0, 0)),
                pl.BlockSpec((1, W, D), lambda d, table: (jnp.maximum(d - half, 0), 0, 0)),
            ),
        ),
        compiler_params=vmem(24),
        cost_estimate=CHEAP,
    )(table, o, d_att)


def last_kernel(a_ref, b_ref, c_ref, x_ref, d_mid_ref, gain_ref, out_ref):
    grad = a_ref[...] + b_ref[...].astype(F32) + c_ref[...].astype(F32)
    n, inverse = normed(x_ref[...].astype(F32))
    u = grad * gain_ref[...]
    mean_u = jnp.mean(u, axis=-1, keepdims=True)
    mean_un = jnp.mean(u * n, axis=-1, keepdims=True)
    out_ref[...] = d_mid_ref[...] + (u - mean_u - n * mean_un) * inverse


def last(parts, x, d_mid, gain):
    t, D = x.shape
    full = whole((t, D))
    return pl.pallas_call(
        last_kernel,
        out_shape=jax.ShapeDtypeStruct((t, D), F32),
        grid=(1,),
        in_specs=[full] * 5 + [whole((1, D))],
        out_specs=full,
        compiler_params=vmem(48),
        cost_estimate=pl.CostEstimate(flops=4 * 10**9, transcendentals=0, bytes_accessed=1),
    )(*parts, x, d_mid, gain.reshape(1, D))


def pair_up_kernel(rep_ref, own_ref, other_ref, out_ref):
    m = own_ref.shape[0]
    mine = pl.multiple_of(rep_ref[0] * m, 8)
    theirs = pl.multiple_of((1 - rep_ref[0]) * m, 8)
    out_ref[pl.ds(mine, m)] = own_ref[...].astype(F32)
    out_ref[pl.ds(theirs, m)] = other_ref[...].astype(F32)


def pair_up(rep, own, other):
    m, D = own.shape
    return pl.pallas_call(
        pair_up_kernel,
        out_shape=jax.ShapeDtypeStruct((2 * m, D), F32),
        grid_spec=pltpu.PrefetchScalarGridSpec(
            num_scalar_prefetch=1,
            grid=(1,),
            in_specs=[whole((m, D)), whole((m, D))],
            out_specs=whole((2 * m, D)),
        ),
        compiler_params=vmem(24),
        cost_estimate=CHEAP,
    )(rep.reshape(1), own, other)


def columns_kernel(count, *refs):
    grads, w_ref, sums_ref, gain_ref, shift_ref, rest_ref, out_ref = refs[:count], *refs[count:]
    width = grads[0].shape[1]
    by_d = jnp.zeros((w_ref.shape[0], 1), F32)
    by_g = jnp.zeros((w_ref.shape[0], 1), F32)
    for p, grad_ref in enumerate(grads):
        w = w_ref[:, p * width : (p + 1) * width].astype(F32)
        by_d += jnp.sum(w * sums_ref[:, p * width : (p + 1) * width], axis=1, keepdims=True)
        by_g += jnp.sum(w * grad_ref[...].astype(F32), axis=1, keepdims=True)
    by_n = (by_g - shift_ref[:, :1] * by_d) / gain_ref[:, :1]
    lane = lax.broadcasted_iota(jnp.int32, (w_ref.shape[0], 128), 1)
    small = jnp.where(lane == 0, by_n, jnp.where(lane == 1, by_d, rest_ref[...]))
    out_ref[:, :width] = grads[-1][...]
    out_ref[:, width:] = small.astype(BF)


def with_columns(grads, weight, sums, gain, shift, rest):
    D, width = grads[0].shape
    step = 512
    rows = lambda w: pl.BlockSpec((step, w), lambda i: (i, 0))
    return pl.pallas_call(
        functools.partial(columns_kernel, len(grads)),
        out_shape=jax.ShapeDtypeStruct((D, width + 128), BF),
        grid=(D // step,),
        in_specs=[rows(width)] * len(grads) + [rows(weight.shape[1]), whole(sums.shape), rows(128), rows(128), rows(128)],
        out_specs=rows(width + 128),
        compiler_params=vmem(32),
        cost_estimate=CHEAP,
    )(*grads, weight, sums, gain, shift, rest)


def part_weights_kernel(m, rows, early_ref, late_ref, expand_ref, shrink_ref):
    half = shrink_ref.shape[0] // 2
    width = late_ref.shape[2]
    expand_ref[...] = late_ref[0, :rows]
    shrink_ref[:half] = early_ref[0, m : m + half]
    shrink_ref[half:, :width] = late_ref[0, rows : rows + half]
    shrink_ref[half:, width:] = late_ref[0, rows + half : rows + 2 * half]


def part_weights(early, late, m, rows):
    F, _, D = early.shape
    width = late.shape[2]
    half = (late.shape[1] - rows) // 2
    return pl.pallas_call(
        functools.partial(part_weights_kernel, m, rows),
        out_shape=(jax.ShapeDtypeStruct((F * rows, width), BF), jax.ShapeDtypeStruct((F * 2 * half, D), BF)),
        grid=(F,),
        in_specs=[
            pl.BlockSpec((1,) + early.shape[1:], lambda f: (f, 0, 0)),
            pl.BlockSpec((1,) + late.shape[1:], lambda f: (f, 0, 0)),
        ],
        out_specs=(pl.BlockSpec((rows, width), lambda f: (f, 0)), pl.BlockSpec((2 * half, D), lambda f: (f, 0))),
        compiler_params=vmem(32),
        cost_estimate=CHEAP,
    )(early, late)


def gelu_and_slope(values):
    half = 0.5 + 0.5 * lax.erf(values * 0.7071067811865476)
    density = jnp.exp(values * values * -0.5) * 0.3989422804014327
    return (values * half).astype(BF), (half + values * density).astype(BF)


def together(*values):
    return lax.optimization_barrier(values)


class Plain:
    def __init__(self, R, C):
        self.R, self.C, self.N = R, C, R * C
        self.axes = ("rep", "ctx")
        self.groups = (1, R, C)
        place = jnp.arange(C, dtype=jnp.int32)
        self.order = jnp.stack([place * 0, place, place * 0])
        self.table = jnp.arange(self.N, dtype=jnp.int32)

    def gather(self, x):
        return [lax.all_gather(x, self.axes, axis=0, tiled=True)]

    def gather_two(self, x, g, ready):
        return self.gather(x), self.gather(g), ready

    def scatter_core(self, rows, part, ready=None):
        out = part(0, 0, self.N * rows).astype(BF)
        return out if ready is None else (out, ready)

    def scatter_far(self, state):
        return state

    def scatter_near(self, state):
        return lax.psum_scatter(state, self.axes, scatter_dimension=0, tiled=True)

    def scatter_end(self, state):
        return state.astype(F32), jnp.zeros_like(state), jnp.zeros_like(state)

    def swap(self, parts):
        return lax.all_to_all(parts, self.axes, 0, 0, tiled=True)

    def swap_ctx(self, blocks):
        return lax.all_to_all(blocks, "ctx", 0, 0, tiled=True)

    def prefixes(self, prefix):
        return lax.all_gather(prefix, "rep", axis=0, tiled=True)


class Near(Plain):
    def __init__(self, R, F, C):
        super().__init__(R, C)
        self.F = F
        self.ctx = lax.axis_index("ctx")
        self.rep = lax.axis_index("rep")
        self.fsdp = lax.axis_index("fsdp")
        self.groups = (2, 2, 2)
        place = jnp.arange(C, dtype=jnp.int32) ^ self.ctx
        self.order = jnp.stack([place & 1, place >> 1, place * 0 + self.rep])
        d = jnp.arange(8, dtype=jnp.int32)
        self.table = (self.rep * 4 + self.ctx) ^ ((d & 2) * 2 + (d & 1) * 2 + (d >> 2))

    def over(self, x, d):
        return lax.ppermute(x, "ctx", [(i, i ^ d) for i in range(4)])

    def x(self, x):
        return lax.ppermute(x, "rep", [(0, 1), (1, 0)])

    def y(self, x):
        return self.over(x, 2)

    def core(self, x):
        return self.over(x, 1)

    def gather(self, x):
        return self.gather_core(self.gather_far(x, self.x(x), self.y(x)))

    def gather_far(self, x, from_x, from_y):
        half = x.shape[0] // 2
        return x, from_y, from_x, self.y(from_x[:half]), self.x(from_y[half:])

    def gather_core(self, pieces):
        own = jnp.concatenate(pieces, axis=0)
        return [own, self.core(own)]

    def gather_two(self, x, g, ready):
        t = x.shape[0]
        both = jnp.concatenate([x, g], axis=0)
        from_x = self.x(both)
        both, ready = together(both, ready)
        from_y = self.y(both)
        far_x, far_g = together(self.y(from_x[:t]), self.x(from_y[t:]))
        x = jnp.concatenate([x, from_y[:t], from_x[:t], far_x], axis=0)
        g = jnp.concatenate([g, from_y[t:], from_x[t:], far_g], axis=0)
        return [x, self.core(x)], [g, self.core(g)], ready

    def scatter_core(self, rows, part, ready=None):
        far_x = part(1, 2 * rows, 4 * rows).astype(BF)
        near_x = part(1, 0, 2 * rows).astype(BF)
        far_x, near_x, halfway = together(far_x, near_x, () if ready is None else ready)
        far_x = part(0, 2 * rows, 4 * rows) + self.core(far_x).astype(F32)
        near_x = part(0, 0, 2 * rows) + self.core(near_x).astype(F32)
        return (far_x, near_x) if ready is None else ((far_x, near_x), halfway)

    def scatter_given(self, own, oth):
        total = (own.astype(F32) + self.core(oth).astype(F32)).astype(BF)
        return total[total.shape[0] // 2 :], total[: total.shape[0] // 2]

    def scatter_far(self, state):
        far_x, near_x = state
        rows = far_x.shape[0] // 2
        far = far_x[rows:].astype(BF)
        return far_x, near_x, self.y(far[: rows // 2]), self.x(far[rows // 2 :])

    def scatter_near(self, state):
        far_x, near_x, to_y, to_x = state
        rows = far_x.shape[0] // 2
        half = rows // 2
        by_x, near_y = far_x[:rows].astype(F32), near_x[rows:].astype(F32)
        by_x = jnp.concatenate([by_x[:half] + to_y.astype(F32), by_x[half:]], axis=0)
        by_y = jnp.concatenate([near_y[:half], near_y[half:] + to_x.astype(F32)], axis=0)
        return near_x, self.x(by_x.astype(BF)), self.y(by_y.astype(BF))

    def scatter_end(self, state):
        return state

    def prefixes(self, prefix):
        return jnp.concatenate([prefix, self.x(prefix)])

    def gather_ctx(self, x):
        x = jnp.stack([x, self.y(x)])
        x = jnp.stack([x, self.core(x)], axis=1).reshape(4, *x.shape[1:])
        x = jnp.take(x, jnp.arange(4) ^ self.ctx, axis=0)
        return x.transpose(1, 0, 2).reshape(-1, x.shape[2])


def added(parts):
    rows = parts[-1].shape[0]
    return sum(a[:rows].astype(F32) for a in parts)


def scatter_shifts(x, axis, size):
    me = lax.axis_index(axis)
    total = lax.dynamic_index_in_dim(x, me, 0, keepdims=False)
    for s in range(1, size):
        mine = lax.dynamic_index_in_dim(x, lax.rem(me + s, size), 0, keepdims=False)
        total = total.astype(F32) + lax.ppermute(mine, axis, [(i, (i + s) % size) for i in range(size)]).astype(F32)
    return total.astype(x.dtype)


def shards(
    sizes,
    inputs,
    prefix,
    joined_weight,
    query_bias,
    value_bias,
    dense_weight,
    dense_bias,
    expand_weight,
    expand_bias,
    shrink_weight,
    shrink_bias,
    first_gain,
    first_shift,
    second_gain,
    second_shift,
    cotangent,
):
    R, F, C = sizes
    N = R * C
    rep = lax.axis_index("rep")
    ctx = lax.axis_index("ctx")
    S, t, D = inputs.shape
    assert S == 1
    B = joined_weight.shape[0]
    FFB = shrink_weight.shape[0]
    FF = FFB * F * C
    E = FFB // R
    W = D // N
    near = R == 2 and C == 4 and B == 2 * HD
    tp = Near(R, F, C) if near else Plain(R, C)
    K, _, Y = tp.groups
    G = range(K)
    n = N // K
    pairs = W // 128

    def half_rows(weight):
        m = weight.shape[0] // R
        return lax.dynamic_slice_in_dim(weight, rep * m, m, 0)

    def widen(blocks):
        return lax.all_gather(blocks.reshape(C * B, -1), "fsdp", axis=0, tiled=True)

    def to_owners(part):
        blocks = jnp.concatenate([part.reshape(C, B, -1)] * R)
        return lax.all_to_all(blocks, ("rep", "ctx"), 0, 0, tiled=True).reshape(R, C, B, -1)

    def over_rep(x):
        return lax.ppermute(x, "rep", [(0, 1), (1, 0)])

    x = inputs.reshape(t, D)
    g = cotangent.reshape(t, D)
    small = jnp.concatenate(
        [first_gain, first_shift, second_gain, second_shift, dense_bias, shrink_bias, query_bias, value_bias, expand_bias]
    )
    if near:
        low, high = jnp.split(half_rows(shrink_weight), 2)
        m = B // R
        small = jnp.pad(small.reshape(1, -1), ((0, 15), (0, D - small.shape[0])))
        early = lax.all_gather(jnp.concatenate([half_rows(dense_weight), low, small]), "fsdp", axis=0, tiled=False)
        dense_rows = early[:, :m].reshape(F * m, D)
        small = tp.gather_ctx(early[:, m + low.shape[0], : 8 * B + FFB])
        blocks = lax.all_to_all(pack(F, C, rep, joined_weight, expand_weight), "ctx", 0, 0, tiled=True)
        joined_blocks, expand_blocks = blocks[:, :, : 3 * W], blocks[:, :, 3 * W :]
    else:
        dense_rows = lax.all_gather(dense_weight, ("fsdp", "ctx"), axis=0, tiled=True)
        small = lax.all_gather(small, ("fsdp", "ctx"), axis=0, tiled=False)
        pieces = joined_weight.reshape(B, 3, R, C, pairs, 128)
        pieces = lax.dynamic_index_in_dim(pieces, rep, 2, keepdims=False).transpose(2, 0, 3, 1, 4)
        joined_blocks = lax.all_to_all(pieces.reshape(C, B, 3 * W), "ctx", 0, 0, tiled=True)
        pieces = expand_weight.reshape(B, F, C, R, E)
        pieces = lax.dynamic_index_in_dim(pieces, rep, 3, keepdims=False).transpose(2, 0, 1, 3)
        expand_blocks = lax.all_to_all(pieces.reshape(C, B, F * E), "ctx", 0, 0, tiled=True)
    x_all, g_all, (joined_blocks, expand_blocks) = tp.gather_two(x, g, (joined_blocks, expand_blocks))
    joined_cols = widen(joined_blocks)
    if near:
        late = jnp.concatenate([expand_blocks.reshape(C * B, -1), high[:, : D // 2], high[:, D // 2 :]])
        late = lax.all_gather(late, "fsdp", axis=0, tiled=False)
    else:
        expand_cols = widen(expand_blocks)
        shrink_rows = lax.all_gather(half_rows(shrink_weight), "fsdp", axis=0, tiled=True)
    prefixes = tp.prefixes(prefix)

    small = small.astype(F32)
    gain_one, shift_one, gain_two, shift_two, dbias, sbias, qbias, vbias = [
        small[:, i * B : (i + 1) * B].reshape(D) for i in range(8)
    ]
    ebias = small[:, 8 * B :].reshape(F, C, R, E)
    ebias = lax.dynamic_index_in_dim(lax.dynamic_index_in_dim(ebias, ctx, 1, False), rep, 1, False)
    ebias = ebias.reshape(F * E)

    def my_features(vector):
        if near:
            v = vector.reshape(F, C, R, -1)
            return lax.dynamic_index_in_dim(lax.dynamic_index_in_dim(v, ctx, 1, False), rep, 1, False).reshape(W)
        return lax.dynamic_slice_in_dim(vector, (rep * C + ctx) * W, W, 0)

    my_heads = my_features(jnp.repeat(jnp.arange(H, dtype=jnp.int32), HD)).reshape(-1, HD)[:, 0]
    slopes = jnp.exp2(-8.0 * (my_heads.astype(F32) + 1.0) / H)

    if near:
        own, dense_rows = together(x_all[0], dense_rows)
        x_all[0] = own
    a1_all = [norm(a, gain_one, shift_one) for a in x_all]
    if near:
        a1_all, joined_cols = together(a1_all, joined_cols)
    else:
        dense_all = [dense_rows[: D // 2], dense_rows[D // 2 :]]
    qkv_bias = jnp.stack([my_features(qbias), jnp.zeros((W,), F32), my_features(vbias)])
    qkv_bias = qkv_bias.reshape(3, pairs, 128).transpose(1, 0, 2).reshape(3 * W)
    qkv = jnp.stack([(dot(a, joined_cols, 1, 0) + qkv_bias).astype(BF) for a in a1_all])
    qkv = qkv.reshape(K, R, Y, t, 3 * W)
    if near:
        from_x, from_y, qkv = together(tp.x(dense_rows), tp.y(dense_rows), qkv)
        dense_all = tp.gather_far(dense_rows, from_x, from_y)
    out = attention_forward(tp.order, prefixes, slopes, qkv)
    out, g_all, dense_all = together(out, g_all, dense_all)
    if near:
        dense_all = tp.gather_core(dense_all)
    o = tp.swap(out.reshape(N, t, W))
    midway, a2 = attended(tp.table, o, dense_all, x, dbias, gain_two, shift_two)

    if near:
        pieces, late = together(tp.gather_far(a2, tp.x(a2), tp.y(a2)), late)
        a2_all = tp.gather_core(pieces)
        expand_cols, shrink_rows = part_weights(early, late, m, C * B)
    else:
        a2_all = tp.gather(a2)
    act, slope = [], []
    for i in G:
        got = gelu_and_slope(dot(a2_all[i], expand_cols, 1, 0) + ebias)
        if i + 1 < K:
            got, a2_all[i + 1] = together(got, a2_all[i + 1])
        act.append(got[0])
        slope.append(got[1])
    shrink_grad = sum(dot(act[i], g_all[i], 0, 0) for i in G).astype(BF)
    slope, shrink_grad, act = together(slope, shrink_grad, act)
    shrink_part = lax.psum_scatter(shrink_grad, "fsdp", scatter_dimension=0, tiled=True)
    d_exp = [(dot(g_all[i], shrink_rows, 1, 1) * slope[i].astype(F32)).astype(BF) for i in G]

    d_a2 = tp.scatter_core(t, lambda i, a, b: dot(d_exp[i][a:b], expand_cols, 1, 1))
    d_a2, act = together(d_a2, act)
    d_a2 = tp.scatter_far(d_a2)
    branch = tp.scatter_core(t, lambda i, a, b: dot(act[i][a:b], shrink_rows, 1, 0))
    d_a2, d_exp, branch = together(d_a2, d_exp, branch)
    d_a2 = tp.scatter_near(d_a2)
    expand_grad = sum(dot(a2_all[i], d_exp[i], 0, 0) for i in G).astype(BF)
    d_a2, expand_grad, branch = together(d_a2, expand_grad, branch)
    expand_part = lax.psum_scatter(expand_grad, "fsdp", scatter_dimension=0, tiled=True)
    branch = tp.scatter_far(branch)
    d_mid, d_att, sums_two, d_o = turned(tp.table, tp.scatter_end(d_a2), midway, g, gain_two, dense_all)

    d_o, shrink_part, branch = together(d_o, shrink_part, branch)
    d_o = tp.swap(d_o).reshape(R, C, t, W)
    dense_part = outer(tp.table, o, d_att) if near else ()
    d_o, dense_part, branch, shrink_part = together(d_o, dense_part, branch, shrink_part)
    branch = tp.scatter_near(branch)
    shrink_other = over_rep(shrink_part)
    if near:
        dense_part = tp.scatter_given(*[a.reshape(n * W, D) for a in dense_part])
    d_qkv, joined_grad, expand_all = None, [], ()
    for p in range(pairs):
        d_qkv = attention_backward(p, tp.order, prefixes, slopes[2 * p : 2 * p + 2], qkv, d_o, d_qkv)
        d_qkv, dense_part, branch, expand_all = together(d_qkv, dense_part, branch, expand_all)
        mine = d_qkv.reshape(K, n * t, 3 * W)[:, :, 384 * p : 384 * (p + 1)]
        grad = sum(dot(a1_all[i], mine[i], 0, 0) for i in G).astype(BF)
        d_qkv, grad, d_o, expand_part, shrink_other = together(d_qkv, grad, d_o, expand_part, shrink_other)
        joined_grad.append(grad)
        if p == 0:
            expand_all = to_owners(expand_part)
            if near:
                dense_part = tp.scatter_far(dense_part)
    d_qkv = d_qkv.reshape(K, n * t, 3 * W)
    layer_output = midway + added(tp.scatter_end(branch)) + sbias

    d_qkv_sum = jnp.sum(d_qkv.astype(F32), axis=(0, 1))
    d_exp_sum = sum(jnp.sum(d.astype(F32), axis=0) for d in d_exp)

    def place(vector, width):
        if near or width != D:
            full = jnp.zeros((F, C, R, width // (F * C * R)), F32)
            full = lax.dynamic_update_slice(full, vector.reshape(F, 1, 1, -1), (0, ctx, rep, 0))
            return full.reshape(F * C, width // D, B).transpose(0, 2, 1).reshape(D, width // D)
        return lax.dynamic_update_slice_in_dim(jnp.zeros((width,), F32), vector, (rep * C + ctx) * W, 0).reshape(D, 1)

    by_part = d_qkv_sum.reshape(pairs, 3, 128)
    rest = [jnp.zeros((D, 2), F32), sums_two.T, place(by_part[:, 0].reshape(W), D), place(by_part[:, 2].reshape(W), D)]
    rest.append(place(d_exp_sum, FF))
    rest = jnp.concatenate(rest, axis=1)
    used = rest.shape[1]
    rest = jnp.pad(rest, ((0, 0), (0, 128 - used)))
    lanes = lambda a: jnp.broadcast_to(a[:, None], (D, 128))
    grad = with_columns(joined_grad, joined_cols, d_qkv_sum.reshape(1, 3 * W), lanes(gain_one), lanes(shift_one), rest)
    joined_part = [lax.psum_scatter(a, "fsdp", scatter_dimension=0, tiled=True) for a in joined_grad[:-1]]
    grad, joined_part = together(grad, joined_part)
    joined_part.append(lax.psum_scatter(grad, "fsdp", scatter_dimension=0, tiled=True))
    if near:
        dense_part = tp.scatter_near(dense_part)
    d_a1, dense_part = tp.scatter_core(t, lambda i, a, b: dot(d_qkv[i, a:b], joined_cols, 1, 1), dense_part)
    expand_out = shrink_out = ()
    if near:
        shrink_out = pair_up(rep, shrink_part, shrink_other)
        expand_out = unpack(unpack_expand_kernel, F, expand_all)
        dense_part = added(tp.scatter_end(dense_part)).astype(BF).reshape(F, W // F, D)
    d_a1, shrink_out, expand_out, layer_output, dense_part, joined_part = together(
        d_a1, shrink_out, expand_out, layer_output, dense_part, joined_part
    )
    if near:
        dense_part = scatter_shifts(dense_part, "fsdp", F)
    d_a1 = together(*tp.scatter_far(d_a1)) if near else d_a1
    joined_all = to_owners(jnp.concatenate(joined_part, axis=1))
    d_a1 = tp.scatter_near(d_a1)
    d_a1, dense_part = together(d_a1, dense_part)
    dense_other = over_rep(dense_part) if near else ()
    input_gradient = last(tp.scatter_end(d_a1), x, d_mid, gain_one)
    if near:
        dense_out = pair_up(rep, dense_part, dense_other)
        input_gradient, dense_out, joined_all = together(input_gradient, dense_out, joined_all)

    def both_reps(own, other):
        first = rep == 0
        return jnp.stack([jnp.where(first, own, other), jnp.where(first, other, own)])

    little = jnp.sum(joined_all[:, :, :, 3 * W :].astype(F32), axis=(0, 1)).T
    if near:
        joined_out = unpack(unpack_joined_kernel, F, joined_all, 128)
    else:
        expand_out = expand_all.reshape(R, C, B, F, E).transpose(2, 3, 1, 0, 4).reshape(B, FF).astype(F32)
        both = joined_all[:, :, :, : 3 * W].reshape(R, C, B, pairs, 3, 128).transpose(2, 4, 0, 1, 3, 5)
        joined_out = both.reshape(B, 3 * D).astype(F32)
        shrink_out = both_reps(shrink_part, shrink_other).reshape(FFB, D).astype(F32)
        part = dot(o.transpose(1, 0, 2).reshape(t, D), d_att, 0, 0).astype(BF)
        part = lax.psum_scatter(part, ("fsdp", "ctx"), scatter_dimension=0, tiled=True)
        dense_out = lax.psum(part, "rep").astype(F32)
    gain_one_out, shift_one_out, gain_two_out, shift_two_out, dbias_out, sbias_out, qbias_out, vbias_out = [
        little[i] for i in range(8)
    ]
    ebias_out = little[8:used].reshape(FFB)

    return (
        layer_output.reshape(S, t, D),
        input_gradient.reshape(S, t, D),
        joined_out,
        qbias_out,
        vbias_out,
        dense_out,
        dbias_out,
        expand_out,
        ebias_out,
        shrink_out,
        sbias_out,
        gain_one_out,
        shift_one_out,
        gain_two_out,
        shift_two_out,
    )


def solution(mesh):
    sizes = (mesh.shape["rep"], mesh.shape["fsdp"], mesh.shape["ctx"])
    tokens = P(("rep", "fsdp"), "ctx", None)
    matrix = P(("fsdp", "ctx"), None)
    vector = P(("fsdp", "ctx"))
    weights = (matrix, vector, vector, matrix, vector, matrix, vector, matrix, vector, vector, vector, vector, vector)
    in_specs = (tokens, P(("rep", "fsdp")), *weights, tokens)
    out_specs = (tokens, tokens, *weights)

    def step(*arrays):
        return shards(sizes, *arrays)

    return jax.shard_map(step, mesh=mesh, in_specs=in_specs, out_specs=out_specs, check_vma=False)
```

```python
import functools

import jax
import jax.numpy as jnp
from jax import lax
from jax.experimental import pallas as pl
from jax.experimental.pallas import tpu as pltpu
from jax.sharding import PartitionSpec as P

H = 32
HD = 64
BF = jnp.bfloat16
F32 = jnp.float32
LONGEST = 512
CHEAP = pl.CostEstimate(flops=1, transcendentals=0, bytes_accessed=1)


def dot(a, b, ca, cb):
    return lax.dot_general(a, b, (((ca,), (cb,)), ((), ())), preferred_element_type=F32)


def places(c, n, T, prefix):
    before = lax.broadcasted_iota(jnp.int32, (1, c * T), 1).astype(F32) - c * T if c else None
    row = lax.broadcasted_iota(jnp.int32, (T, (n - c) * T), 0)
    column = lax.broadcasted_iota(jnp.int32, (T, (n - c) * T), 1)
    allowed = column <= jnp.maximum(row, prefix - 1 - c * T)
    return before, jnp.minimum(column, 2 * row - column).astype(F32), allowed


def head_probs(query, key, slope, place, lanes):
    before, near, allowed = place
    raw = dot(jnp.where(lanes, query, jnp.zeros_like(query)), key, 1, 1)
    split = raw.shape[1] - near.shape[1]
    logits = jnp.where(allowed, raw[:, split:] + slope * near, -1e30)
    if split:
        logits = jnp.concatenate([raw[:, :split] + slope * before, logits], axis=1)
    largest = jnp.max(logits, axis=-1, keepdims=True)
    exponent = jnp.exp(logits - largest)
    return exponent * (1.0 / jnp.sum(exponent, axis=-1, keepdims=True))


def forward_kernel(order_ref, prefix_ref, slope_ref, qkv_ref, out_ref):
    C, T = qkv_ref.shape[0] * qkv_ref.shape[2], qkv_ref.shape[3]
    seq, pair = pl.program_id(0), pl.program_id(1)
    at = lambda part: slice(part * 128, part * 128 + 128)
    first = lax.broadcasted_iota(jnp.int32, (T, 128), 1) < HD
    key = [qkv_ref[order_ref[0, c], 0, order_ref[1, c], :, at(1)] for c in range(C)]
    value = [qkv_ref[order_ref[0, c], 0, order_ref[1, c], :, at(2)] for c in range(C)]
    for c in range(C):
        n = min(C, max(c + 1, -(-LONGEST // T)))
        keys = jnp.concatenate(key[:n], axis=0)
        values = jnp.concatenate(value[:n], axis=0)
        query = qkv_ref[order_ref[0, c], 0, order_ref[1, c], :, at(0)] * 0.125
        place = places(c, n, T, prefix_ref[seq])
        out = []
        for h in range(2):
            probs = head_probs(query, keys, slope_ref[2 * pair + h], place, first if h == 0 else ~first)
            out.append(dot(probs.astype(BF), values, 1, 0))
        out_ref[0, c] = jnp.where(first, out[0], out[1]).astype(BF)


def backward_kernel(order_ref, prefix_ref, slope_ref, qkv_ref, d_out_ref, d_qkv_ref, d_key, d_value):
    C, T = qkv_ref.shape[0] * qkv_ref.shape[2], qkv_ref.shape[3]
    seq, pair = pl.program_id(0), pl.program_id(1)
    at = lambda part: slice(part * 128, part * 128 + 128)
    first = lax.broadcasted_iota(jnp.int32, (T, 128), 1) < HD
    d_key[...] = jnp.zeros_like(d_key)
    d_value[...] = jnp.zeros_like(d_value)
    key = [qkv_ref[order_ref[0, c], 0, order_ref[1, c], :, at(1)] for c in range(C)]
    value = [qkv_ref[order_ref[0, c], 0, order_ref[1, c], :, at(2)] for c in range(C)]
    for c in range(C):
        n = min(C, max(c + 1, -(-LONGEST // T)))
        keys = jnp.concatenate(key[:n], axis=0)
        values = jnp.concatenate(value[:n], axis=0)
        query = qkv_ref[order_ref[0, c], 0, order_ref[1, c], :, at(0)]
        d_out = d_out_ref[0, c]
        place = places(c, n, T, prefix_ref[seq])
        d_query = []
        for h in range(2):
            lanes = first if h == 0 else ~first
            probs = head_probs(query * 0.125, keys, slope_ref[2 * pair + h], place, lanes)
            mine = jnp.where(lanes, d_out, jnp.zeros_like(d_out))
            d_probs = dot(mine, values, 1, 1)
            weighted = jnp.sum(probs * d_probs, axis=-1, keepdims=True)
            d_raw = (probs * (d_probs - weighted) * 0.125).astype(BF)
            d_query.append(dot(d_raw, keys, 1, 0))
            d_value[: n * T] += dot(probs.astype(BF), mine, 0, 0)
            d_key[: n * T] += dot(d_raw, jnp.where(lanes, query, jnp.zeros_like(query)), 0, 0)
        d_qkv_ref[order_ref[0, c], 0, order_ref[1, c], :, at(0)] = jnp.where(first, d_query[0], d_query[1]).astype(BF)
    for c in range(C):
        d_qkv_ref[order_ref[0, c], 0, order_ref[1, c], :, at(1)] = d_key[c * T : (c + 1) * T].astype(BF)
        d_qkv_ref[order_ref[0, c], 0, order_ref[1, c], :, at(2)] = d_value[c * T : (c + 1) * T].astype(BF)


def attention_specs(order_ndim, K, n, Y, C, T, pair):
    near = pl.BlockSpec((K, 1, Y, T, 384), lambda s, p, *_: (0, s, 0, 0, p + pair))
    true = pl.BlockSpec((1, C, T, 128), lambda s, p, order, *_: (s ^ order[2, 0], 0, 0, p + pair))
    return near, true


def attention_forward(order, prefix, slopes, qkv):
    K, n, Y, T = qkv.shape[:4]
    C, pairs = K * Y, qkv.shape[4] // 384
    near, true = attention_specs(0, K, n, Y, C, T, 0)
    return pl.pallas_call(
        forward_kernel,
        out_shape=jax.ShapeDtypeStruct((n, C, T, pairs * 128), BF),
        grid_spec=pltpu.PrefetchScalarGridSpec(num_scalar_prefetch=3, grid=(n, pairs), in_specs=[near], out_specs=true),
        compiler_params=vmem(32),
        cost_estimate=pl.CostEstimate(flops=12 * 10**9, transcendentals=0, bytes_accessed=1),
    )(order, prefix, slopes, qkv)


def attention_backward(pair, order, prefix, slopes, qkv, d_out, before=None):
    K, n, Y, T = qkv.shape[:4]
    C = K * Y
    near, true = attention_specs(0, K, n, Y, C, T, pair)
    kernel = backward_kernel
    more, aliases = [], {}
    if before is not None:
        kernel = lambda a, b, c, d, e, _, *rest: backward_kernel(a, b, c, d, e, *rest)
        more, aliases = [before], {5: 0}
    return pl.pallas_call(
        kernel,
        out_shape=jax.ShapeDtypeStruct(qkv.shape, BF),
        grid_spec=pltpu.PrefetchScalarGridSpec(
            num_scalar_prefetch=3,
            grid=(n, 1),
            in_specs=[near, true] + [pl.BlockSpec(memory_space=pl.ANY)] * len(more),
            out_specs=near,
            scratch_shapes=[pltpu.VMEM((C * T, 128), F32), pltpu.VMEM((C * T, 128), F32)],
        ),
        input_output_aliases=aliases,
        compiler_params=vmem(32),
        cost_estimate=pl.CostEstimate(flops=12 * 10**9, transcendentals=0, bytes_accessed=1),
    )(order, prefix, slopes, qkv, d_out, *more)


def whole(shape):
    return pl.BlockSpec(shape, lambda *_: (0,) * len(shape))


def vmem(megabytes):
    return pltpu.CompilerParams(vmem_limit_bytes=megabytes * 1024 * 1024)


def half_turn(tile):
    return jnp.concatenate([tile[:, 64:], tile[:, :64]], axis=1)


def pack_kernel(F, C, rep_ref, joined_ref, expand_ref, out_ref):
    B = joined_ref.shape[0]
    E = expand_ref.shape[1] // (2 * F * C)
    D = joined_ref.shape[1] // 3
    first = lax.broadcasted_iota(jnp.int32, (B, 128), 1) < HD
    rep = rep_ref[0]
    keep = first == (rep == 0)
    for c in range(C):
        for p in range(F // 2):
            for q in range(3):
                one, two = [joined_ref[:, q * D + (f * C + c) * 128 :][:, :128] for f in (2 * p, 2 * p + 1)]
                mine = jnp.where(keep, jnp.where(first, one, two), half_turn(jnp.where(first, two, one)))
                out_ref[c, :, (p * 3 + q) * 128 : (p * 3 + q + 1) * 128] = mine
        for f in range(F):
            from_ = pl.multiple_of((f * C + c) * 2 * E + rep * E, 128)
            to = 3 * F * 64 + f * E
            out_ref[c, :, to : to + E] = expand_ref[:, pl.ds(from_, E)]


def pack(F, C, rep, joined, expand):
    B = joined.shape[0]
    width = 3 * F * 64 + expand.shape[1] // (2 * C)
    return pl.pallas_call(
        functools.partial(pack_kernel, F, C),
        out_shape=jax.ShapeDtypeStruct((C, B, width), BF),
        grid_spec=pltpu.PrefetchScalarGridSpec(
            num_scalar_prefetch=1,
            grid=(1,),
            in_specs=[whole(joined.shape), whole(expand.shape)],
            out_specs=whole((C, B, width)),
        ),
        compiler_params=vmem(24),
        cost_estimate=CHEAP,
    )(rep.reshape(1), joined, expand)


def unpack_joined_kernel(F, ref, out_ref):
    C, B = ref.shape[1:3]
    D = out_ref.shape[1] // 3
    first = lax.broadcasted_iota(jnp.int32, (B, 128), 1) < HD
    for c in range(C):
        for p in range(F // 2):
            for q in range(3):
                at = slice((p * 3 + q) * 128, (p * 3 + q + 1) * 128)
                one, two = ref[0, c, :, at].astype(F32), ref[1, c, :, at].astype(F32)
                for i, f in enumerate((2 * p, 2 * p + 1)):
                    tile = jnp.where(first, half_turn(one) if i else one, two if i else half_turn(two))
                    out_ref[:, q * D + (f * C + c) * 128 : q * D + (f * C + c + 1) * 128] = tile


def unpack_expand_kernel(F, ref, out_ref):
    C = ref.shape[1]
    E = ref.shape[3] // F
    for c in range(C):
        for f in range(F):
            for r in range(2):
                at = ((f * C + c) * 2 + r) * E
                out_ref[:, at : at + E] = ref[r, c, :, f * E : (f + 1) * E].astype(F32)


def unpack(kernel, F, parts, extra=0):
    R, C, B, width = parts.shape
    width -= extra
    return pl.pallas_call(
        functools.partial(kernel, F),
        out_shape=jax.ShapeDtypeStruct((B, R * C * width), F32),
        grid=(1,),
        in_specs=[whole((R, C, B, width))],
        out_specs=whole((B, R * C * width)),
        compiler_params=vmem(32),
        cost_estimate=CHEAP,
    )(parts)


def normed(values):
    average = jnp.mean(values, axis=-1, keepdims=True)
    centred = values - average
    variance = jnp.mean(centred * centred, axis=-1, keepdims=True)
    inverse = lax.rsqrt(variance + 1e-05)
    return centred * inverse, inverse


def norm_kernel(x_ref, gain_ref, shift_ref, out_ref):
    n, _ = normed(x_ref[...].astype(F32))
    out_ref[...] = (n * gain_ref[...] + shift_ref[...]).astype(BF)


def norm(x, gain, shift):
    rows, D = x.shape
    step = min(rows, 256)
    return pl.pallas_call(
        norm_kernel,
        out_shape=jax.ShapeDtypeStruct((rows, D), BF),
        grid=(rows // step,),
        in_specs=[pl.BlockSpec((step, D), lambda i: (i, 0)), whole((1, D)), whole((1, D))],
        out_specs=pl.BlockSpec((step, D), lambda i: (i, 0)),
        compiler_params=vmem(24),
        cost_estimate=CHEAP,
    )(x, gain.reshape(1, D), shift.reshape(1, D))


def attended_kernel(table_ref, o_ref, w_ref, v_ref, x_ref, bias_ref, gain_ref, shift_ref, mid_ref, out_ref):
    d = pl.program_id(0)
    half = pl.num_programs(0) // 2
    weight = jnp.where(d < half, w_ref[0], v_ref[0])
    product = dot(o_ref[0], weight, 1, 0)

    @pl.when(d == 0)
    def _():
        mid_ref[...] = product + x_ref[...].astype(F32) + bias_ref[...]

    @pl.when(d > 0)
    def _():
        mid_ref[...] += product

    @pl.when(d == pl.num_programs(0) - 1)
    def _():
        n, _ = normed(mid_ref[...])
        out_ref[...] = (n * gain_ref[...] + shift_ref[...]).astype(BF)


def attended(table, o, weights, x, bias, gain, shift):
    N, t, W = o.shape
    D = x.shape[1]
    half = N // 2
    weights = [w.reshape(half, W, D) for w in weights]
    return pl.pallas_call(
        attended_kernel,
        out_shape=(jax.ShapeDtypeStruct((t, D), F32), jax.ShapeDtypeStruct((t, D), BF)),
        grid_spec=pltpu.PrefetchScalarGridSpec(
            num_scalar_prefetch=1,
            grid=(N,),
            in_specs=[
                pl.BlockSpec((1, t, W), lambda d, table: (table[d], 0, 0)),
                pl.BlockSpec((1, W, D), lambda d, table: (jnp.minimum(d, half - 1), 0, 0)),
                pl.BlockSpec((1, W, D), lambda d, table: (jnp.maximum(d - half, 0), 0, 0)),
                whole((t, D)),
                whole((1, D)),
                whole((1, D)),
                whole((1, D)),
            ],
            out_specs=(whole((t, D)), whole((t, D))),
        ),
        compiler_params=vmem(32),
        cost_estimate=CHEAP,
    )(table, o, *weights, x, bias.reshape(1, D), gain.reshape(1, D), shift.reshape(1, D))


def turned_kernel(table_ref, a_ref, b_ref, c_ref, mid_ref, g_ref, gain_ref, w_ref, v_ref, d_mid_ref, d_att_ref, sums_ref, d_o_ref):
    d = pl.program_id(0)
    half = pl.num_programs(0) // 2

    @pl.when(d == 0)
    def _():
        grad = a_ref[...] + b_ref[...].astype(F32) + c_ref[...].astype(F32)
        n, inverse = normed(mid_ref[...])
        g = g_ref[...].astype(F32)
        u = grad * gain_ref[...]
        mean_u = jnp.mean(u, axis=-1, keepdims=True)
        mean_un = jnp.mean(u * n, axis=-1, keepdims=True)
        d_mid = g + (u - mean_u - n * mean_un) * inverse
        d_att = d_mid.astype(BF)
        d_mid_ref[...] = d_mid
        d_att_ref[...] = d_att
        rows = (grad * n, grad, d_att.astype(F32), g)
        for i, row in enumerate(rows):
            sums_ref[i : i + 1] = jnp.sum(row, axis=0, keepdims=True)

    weight = jnp.where(d < half, w_ref[0], v_ref[0])
    d_o_ref[0] = dot(d_att_ref[...], weight, 1, 1).astype(BF)


def turned(table, parts, mid, g, gain, weights):
    t, D = mid.shape
    N = table.shape[0]
    half = N // 2
    W = D // N
    weights = [w.reshape(half, W, D) for w in weights]
    full = whole((t, D))
    return pl.pallas_call(
        turned_kernel,
        out_shape=(
            jax.ShapeDtypeStruct((t, D), F32),
            jax.ShapeDtypeStruct((t, D), BF),
            jax.ShapeDtypeStruct((4, D), F32),
            jax.ShapeDtypeStruct((N, t, W), BF),
        ),
        grid_spec=pltpu.PrefetchScalarGridSpec(
            num_scalar_prefetch=1,
            grid=(N,),
            in_specs=[
                full,
                full,
                full,
                full,
                full,
                whole((1, D)),
                pl.BlockSpec((1, W, D), lambda d, table: (jnp.minimum(d, half - 1), 0, 0)),
                pl.BlockSpec((1, W, D), lambda d, table: (jnp.maximum(d - half, 0), 0, 0)),
            ],
            out_specs=(full, full, whole((4, D)), pl.BlockSpec((1, t, W), lambda d, table: (table[d], 0, 0))),
        ),
        compiler_params=vmem(48),
        cost_estimate=CHEAP,
    )(table, *parts, mid, g, gain.reshape(1, D), *weights)


def outer_kernel(table_ref, o_ref, d_att_ref, own_ref, oth_ref):
    d = pl.program_id(0)
    product = dot(o_ref[0], d_att_ref[...], 0, 0).astype(BF)

    @pl.when(d < pl.num_programs(0) // 2)
    def _():
        own_ref[0] = product

    @pl.when(d >= pl.num_programs(0) // 2)
    def _():
        oth_ref[0] = product


def outer(table, o, d_att):
    N, t, W = o.shape
    D = d_att.shape[1]
    half = N // 2
    return pl.pallas_call(
        outer_kernel,
        out_shape=(jax.ShapeDtypeStruct((half, W, D), BF), jax.ShapeDtypeStruct((half, W, D), BF)),
        grid_spec=pltpu.PrefetchScalarGridSpec(
            num_scalar_prefetch=1,
            grid=(N,),
            in_specs=[pl.BlockSpec((1, t, W), lambda d, table: (table[d], 0, 0)), whole((t, D))],
            out_specs=(
                pl.BlockSpec((1, W, D), lambda d, table: (jnp.minimum(d, half - 1), 0, 0)),
                pl.BlockSpec((1, W, D), lambda d, table: (jnp.maximum(d - half, 0), 0, 0)),
            ),
        ),
        compiler_params=vmem(24),
        cost_estimate=CHEAP,
    )(table, o, d_att)


def last_kernel(a_ref, b_ref, c_ref, x_ref, d_mid_ref, gain_ref, out_ref):
    grad = a_ref[...] + b_ref[...].astype(F32) + c_ref[...].astype(F32)
    n, inverse = normed(x_ref[...].astype(F32))
    u = grad * gain_ref[...]
    mean_u = jnp.mean(u, axis=-1, keepdims=True)
    mean_un = jnp.mean(u * n, axis=-1, keepdims=True)
    out_ref[...] = d_mid_ref[...] + (u - mean_u - n * mean_un) * inverse


def last(parts, x, d_mid, gain):
    t, D = x.shape
    full = whole((t, D))
    return pl.pallas_call(
        last_kernel,
        out_shape=jax.ShapeDtypeStruct((t, D), F32),
        grid=(1,),
        in_specs=[full] * 5 + [whole((1, D))],
        out_specs=full,
        compiler_params=vmem(48),
        cost_estimate=pl.CostEstimate(flops=4 * 10**9, transcendentals=0, bytes_accessed=1),
    )(*parts, x, d_mid, gain.reshape(1, D))


def pair_up_kernel(rep_ref, own_ref, other_ref, out_ref):
    m = own_ref.shape[0]
    mine = pl.multiple_of(rep_ref[0] * m, 8)
    theirs = pl.multiple_of((1 - rep_ref[0]) * m, 8)
    out_ref[pl.ds(mine, m)] = own_ref[...].astype(F32)
    out_ref[pl.ds(theirs, m)] = other_ref[...].astype(F32)


def pair_up(rep, own, other):
    m, D = own.shape
    return pl.pallas_call(
        pair_up_kernel,
        out_shape=jax.ShapeDtypeStruct((2 * m, D), F32),
        grid_spec=pltpu.PrefetchScalarGridSpec(
            num_scalar_prefetch=1,
            grid=(1,),
            in_specs=[whole((m, D)), whole((m, D))],
            out_specs=whole((2 * m, D)),
        ),
        compiler_params=vmem(24),
        cost_estimate=CHEAP,
    )(rep.reshape(1), own, other)


def columns_kernel(count, *refs):
    grads, w_ref, sums_ref, gain_ref, shift_ref, rest_ref, out_ref = refs[:count], *refs[count:]
    width = grads[0].shape[1]
    by_d = jnp.zeros((w_ref.shape[0], 1), F32)
    by_g = jnp.zeros((w_ref.shape[0], 1), F32)
    for p, grad_ref in enumerate(grads):
        w = w_ref[:, p * width : (p + 1) * width].astype(F32)
        by_d += jnp.sum(w * sums_ref[:, p * width : (p + 1) * width], axis=1, keepdims=True)
        by_g += jnp.sum(w * grad_ref[...].astype(F32), axis=1, keepdims=True)
    by_n = (by_g - shift_ref[:, :1] * by_d) / gain_ref[:, :1]
    lane = lax.broadcasted_iota(jnp.int32, (w_ref.shape[0], 128), 1)
    small = jnp.where(lane == 0, by_n, jnp.where(lane == 1, by_d, rest_ref[...]))
    out_ref[:, :width] = grads[-1][...]
    out_ref[:, width:] = small.astype(BF)


def with_columns(grads, weight, sums, gain, shift, rest):
    D, width = grads[0].shape
    step = 512
    rows = lambda w: pl.BlockSpec((step, w), lambda i: (i, 0))
    return pl.pallas_call(
        functools.partial(columns_kernel, len(grads)),
        out_shape=jax.ShapeDtypeStruct((D, width + 128), BF),
        grid=(D // step,),
        in_specs=[rows(width)] * len(grads) + [rows(weight.shape[1]), whole(sums.shape), rows(128), rows(128), rows(128)],
        out_specs=rows(width + 128),
        compiler_params=vmem(32),
        cost_estimate=CHEAP,
    )(*grads, weight, sums, gain, shift, rest)


def part_weights_kernel(m, rows, early_ref, late_ref, expand_ref, shrink_ref):
    half = shrink_ref.shape[0] // 2
    width = late_ref.shape[2]
    expand_ref[...] = late_ref[0, :rows]
    shrink_ref[:half] = early_ref[0, m : m + half]
    shrink_ref[half:, :width] = late_ref[0, rows : rows + half]
    shrink_ref[half:, width:] = late_ref[0, rows + half : rows + 2 * half]


def part_weights(early, late, m, rows):
    F, _, D = early.shape
    width = late.shape[2]
    half = (late.shape[1] - rows) // 2
    return pl.pallas_call(
        functools.partial(part_weights_kernel, m, rows),
        out_shape=(jax.ShapeDtypeStruct((F * rows, width), BF), jax.ShapeDtypeStruct((F * 2 * half, D), BF)),
        grid=(F,),
        in_specs=[
            pl.BlockSpec((1,) + early.shape[1:], lambda f: (f, 0, 0)),
            pl.BlockSpec((1,) + late.shape[1:], lambda f: (f, 0, 0)),
        ],
        out_specs=(pl.BlockSpec((rows, width), lambda f: (f, 0)), pl.BlockSpec((2 * half, D), lambda f: (f, 0))),
        compiler_params=vmem(32),
        cost_estimate=CHEAP,
    )(early, late)


def gelu_and_slope(values):
    half = 0.5 + 0.5 * lax.erf(values * 0.7071067811865476)
    density = jnp.exp(values * values * -0.5) * 0.3989422804014327
    return (values * half).astype(BF), (half + values * density).astype(BF)


def together(*values):
    return lax.optimization_barrier(values)


class Plain:
    def __init__(self, R, C):
        self.R, self.C, self.N = R, C, R * C
        self.axes = ("rep", "ctx")
        self.groups = (1, R, C)
        place = jnp.arange(C, dtype=jnp.int32)
        self.order = jnp.stack([place * 0, place, place * 0])
        self.table = jnp.arange(self.N, dtype=jnp.int32)

    def gather(self, x):
        return [lax.all_gather(x, self.axes, axis=0, tiled=True)]

    def gather_two(self, x, g, ready):
        return self.gather(x), self.gather(g), ready

    def scatter_core(self, rows, part, ready=None):
        out = part(0, 0, self.N * rows).astype(BF)
        return out if ready is None else (out, ready)

    def scatter_far(self, state):
        return state

    def scatter_near(self, state):
        return lax.psum_scatter(state, self.axes, scatter_dimension=0, tiled=True)

    def scatter_end(self, state):
        return state.astype(F32), jnp.zeros_like(state), jnp.zeros_like(state)

    def swap(self, parts):
        return lax.all_to_all(parts, self.axes, 0, 0, tiled=True)

    def swap_ctx(self, blocks):
        return lax.all_to_all(blocks, "ctx", 0, 0, tiled=True)

    def prefixes(self, prefix):
        return lax.all_gather(prefix, "rep", axis=0, tiled=True)


class Near(Plain):
    def __init__(self, R, F, C):
        super().__init__(R, C)
        self.F = F
        self.ctx = lax.axis_index("ctx")
        self.rep = lax.axis_index("rep")
        self.fsdp = lax.axis_index("fsdp")
        self.groups = (2, 2, 2)
        place = jnp.arange(C, dtype=jnp.int32) ^ self.ctx
        self.order = jnp.stack([place & 1, place >> 1, place * 0 + self.rep])
        d = jnp.arange(8, dtype=jnp.int32)
        self.table = (self.rep * 4 + self.ctx) ^ ((d & 2) * 2 + (d & 1) * 2 + (d >> 2))

    def over(self, x, d):
        return lax.ppermute(x, "ctx", [(i, i ^ d) for i in range(4)])

    def x(self, x):
        return lax.ppermute(x, "rep", [(0, 1), (1, 0)])

    def y(self, x):
        return self.over(x, 2)

    def core(self, x):
        return self.over(x, 1)

    def gather(self, x):
        return self.gather_core(self.gather_far(x, self.x(x), self.y(x)))

    def gather_far(self, x, from_x, from_y):
        half = x.shape[0] // 2
        near = jnp.concatenate([x, from_y, from_x, jnp.zeros_like(x)], axis=0)
        return near, self.y(from_x[:half]), self.x(from_y[half:])

    def gather_core(self, pieces):
        own, low, high = pieces
        at = own.shape[0] - 2 * low.shape[0]
        own = lax.dynamic_update_slice_in_dim(own, low, at, 0)
        own = lax.dynamic_update_slice_in_dim(own, high, at + low.shape[0], 0)
        return [own, self.core(own)]

    def gather_two(self, x, g, ready):
        t = x.shape[0]
        both = jnp.concatenate([x, g], axis=0)
        from_x = self.x(both)
        both, ready = together(both, ready)
        from_y = self.y(both)
        far_x, far_g = together(self.y(from_x[:t]), self.x(from_y[t:]))
        x = jnp.concatenate([x, from_y[:t], from_x[:t], far_x], axis=0)
        g = jnp.concatenate([g, from_y[t:], from_x[t:], far_g], axis=0)
        return [x, self.core(x)], [g, self.core(g)], ready

    def scatter_core(self, rows, part, ready=None):
        far_x = part(1, 2 * rows, 4 * rows).astype(BF)
        near_x = part(1, 0, 2 * rows).astype(BF)
        far_x, near_x, halfway = together(far_x, near_x, () if ready is None else ready)
        far_x = part(0, 2 * rows, 4 * rows) + self.core(far_x).astype(F32)
        near_x = part(0, 0, 2 * rows) + self.core(near_x).astype(F32)
        return (far_x, near_x) if ready is None else ((far_x, near_x), halfway)

    def scatter_given(self, own, oth):
        total = (own.astype(F32) + self.core(oth).astype(F32)).astype(BF)
        return total[total.shape[0] // 2 :], total[: total.shape[0] // 2]

    def scatter_far(self, state):
        far_x, near_x = state
        rows = far_x.shape[0] // 2
        far = far_x[rows:].astype(BF)
        return far_x, near_x, self.y(far[: rows // 2]), self.x(far[rows // 2 :])

    def scatter_near(self, state):
        far_x, near_x, to_y, to_x = state
        rows = far_x.shape[0] // 2
        half = rows // 2
        by_x, near_y = far_x[:rows].astype(F32), near_x[rows:].astype(F32)
        by_x = jnp.concatenate([by_x[:half] + to_y.astype(F32), by_x[half:]], axis=0)
        by_y = jnp.concatenate([near_y[:half], near_y[half:] + to_x.astype(F32)], axis=0)
        return near_x, self.x(by_x.astype(BF)), self.y(by_y.astype(BF))

    def scatter_end(self, state):
        return state

    def prefixes(self, prefix):
        return jnp.concatenate([prefix, self.x(prefix)])

    def gather_ctx(self, x):
        x = jnp.stack([x, self.y(x)])
        x = jnp.stack([x, self.core(x)], axis=1).reshape(4, *x.shape[1:])
        x = jnp.take(x, jnp.arange(4) ^ self.ctx, axis=0)
        return x.transpose(1, 0, 2).reshape(-1, x.shape[2])


def added(parts):
    rows = parts[-1].shape[0]
    return sum(a[:rows].astype(F32) for a in parts)


def scatter_shifts(x, axis, size):
    me = lax.axis_index(axis)
    total = lax.dynamic_index_in_dim(x, me, 0, keepdims=False)
    for s in range(1, size):
        mine = lax.dynamic_index_in_dim(x, lax.rem(me + s, size), 0, keepdims=False)
        total = total.astype(F32) + lax.ppermute(mine, axis, [(i, (i + s) % size) for i in range(size)]).astype(F32)
    return total.astype(x.dtype)


def shards(
    sizes,
    inputs,
    prefix,
    joined_weight,
    query_bias,
    value_bias,
    dense_weight,
    dense_bias,
    expand_weight,
    expand_bias,
    shrink_weight,
    shrink_bias,
    first_gain,
    first_shift,
    second_gain,
    second_shift,
    cotangent,
):
    R, F, C = sizes
    N = R * C
    rep = lax.axis_index("rep")
    ctx = lax.axis_index("ctx")
    S, t, D = inputs.shape
    assert S == 1
    B = joined_weight.shape[0]
    FFB = shrink_weight.shape[0]
    FF = FFB * F * C
    E = FFB // R
    W = D // N
    near = R == 2 and C == 4 and B == 2 * HD
    tp = Near(R, F, C) if near else Plain(R, C)
    K, _, Y = tp.groups
    G = range(K)
    n = N // K
    pairs = W // 128

    def half_rows(weight):
        m = weight.shape[0] // R
        return lax.dynamic_slice_in_dim(weight, rep * m, m, 0)

    def widen(blocks):
        return lax.all_gather(blocks.reshape(C * B, -1), "fsdp", axis=0, tiled=True)

    def to_owners(part):
        blocks = jnp.concatenate([part.reshape(C, B, -1)] * R)
        return lax.all_to_all(blocks, ("rep", "ctx"), 0, 0, tiled=True).reshape(R, C, B, -1)

    def over_rep(x):
        return lax.ppermute(x, "rep", [(0, 1), (1, 0)])

    x = inputs.reshape(t, D)
    g = cotangent.reshape(t, D)
    small = jnp.concatenate(
        [first_gain, first_shift, second_gain, second_shift, dense_bias, shrink_bias, query_bias, value_bias, expand_bias]
    )
    if near:
        low, high = jnp.split(half_rows(shrink_weight), 2)
        m = B // R
        small = jnp.pad(small.reshape(1, -1), ((0, 15), (0, D - small.shape[0])))
        early = lax.all_gather(jnp.concatenate([half_rows(dense_weight), low, small]), "fsdp", axis=0, tiled=False)
        dense_rows = early[:, :m].reshape(F * m, D)
        small = tp.gather_ctx(early[:, m + low.shape[0], : 8 * B + FFB])
        blocks = lax.all_to_all(pack(F, C, rep, joined_weight, expand_weight), "ctx", 0, 0, tiled=True)
        joined_blocks, expand_blocks = blocks[:, :, : 3 * W], blocks[:, :, 3 * W :]
    else:
        dense_rows = lax.all_gather(dense_weight, ("fsdp", "ctx"), axis=0, tiled=True)
        small = lax.all_gather(small, ("fsdp", "ctx"), axis=0, tiled=False)
        pieces = joined_weight.reshape(B, 3, R, C, pairs, 128)
        pieces = lax.dynamic_index_in_dim(pieces, rep, 2, keepdims=False).transpose(2, 0, 3, 1, 4)
        joined_blocks = lax.all_to_all(pieces.reshape(C, B, 3 * W), "ctx", 0, 0, tiled=True)
        pieces = expand_weight.reshape(B, F, C, R, E)
        pieces = lax.dynamic_index_in_dim(pieces, rep, 3, keepdims=False).transpose(2, 0, 1, 3)
        expand_blocks = lax.all_to_all(pieces.reshape(C, B, F * E), "ctx", 0, 0, tiled=True)
    x_all, g_all, (joined_blocks, expand_blocks) = tp.gather_two(x, g, (joined_blocks, expand_blocks))
    joined_cols = widen(joined_blocks)
    if near:
        late = jnp.concatenate([expand_blocks.reshape(C * B, -1), high[:, : D // 2], high[:, D // 2 :]])
        late = lax.all_gather(late, "fsdp", axis=0, tiled=False)
    else:
        expand_cols = widen(expand_blocks)
        shrink_rows = lax.all_gather(half_rows(shrink_weight), "fsdp", axis=0, tiled=True)
    prefixes = tp.prefixes(prefix)

    small = small.astype(F32)
    gain_one, shift_one, gain_two, shift_two, dbias, sbias, qbias, vbias = [
        small[:, i * B : (i + 1) * B].reshape(D) for i in range(8)
    ]
    ebias = small[:, 8 * B :].reshape(F, C, R, E)
    ebias = lax.dynamic_index_in_dim(lax.dynamic_index_in_dim(ebias, ctx, 1, False), rep, 1, False)
    ebias = ebias.reshape(F * E)

    def my_features(vector):
        if near:
            v = vector.reshape(F, C, R, -1)
            return lax.dynamic_index_in_dim(lax.dynamic_index_in_dim(v, ctx, 1, False), rep, 1, False).reshape(W)
        return lax.dynamic_slice_in_dim(vector, (rep * C + ctx) * W, W, 0)

    my_heads = my_features(jnp.repeat(jnp.arange(H, dtype=jnp.int32), HD)).reshape(-1, HD)[:, 0]
    slopes = jnp.exp2(-8.0 * (my_heads.astype(F32) + 1.0) / H)

    if near:
        own, dense_rows = together(x_all[0], dense_rows)
        x_all[0] = own
    a1_all = [norm(a, gain_one, shift_one) for a in x_all]
    if near:
        a1_all, joined_cols = together(a1_all, joined_cols)
    else:
        dense_all = [dense_rows[: D // 2], dense_rows[D // 2 :]]
    qkv_bias = jnp.stack([my_features(qbias), jnp.zeros((W,), F32), my_features(vbias)])
    qkv_bias = qkv_bias.reshape(3, pairs, 128).transpose(1, 0, 2).reshape(3 * W)
    qkv = jnp.stack([(dot(a, joined_cols, 1, 0) + qkv_bias).astype(BF) for a in a1_all])
    qkv = qkv.reshape(K, R, Y, t, 3 * W)
    if near:
        from_x, from_y, qkv = together(tp.x(dense_rows), tp.y(dense_rows), qkv)
        dense_all = tp.gather_far(dense_rows, from_x, from_y)
    out = attention_forward(tp.order, prefixes, slopes, qkv)
    out, g_all, dense_all = together(out, g_all, dense_all)
    if near:
        dense_all = tp.gather_core(dense_all)
    o = tp.swap(out.reshape(N, t, W))
    midway, a2 = attended(tp.table, o, dense_all, x, dbias, gain_two, shift_two)

    if near:
        pieces, late = together(tp.gather_far(a2, tp.x(a2), tp.y(a2)), late)
        expand_cols, shrink_rows = part_weights(early, late, m, C * B)
        a2_all = tp.gather_core(pieces)
    else:
        a2_all = tp.gather(a2)
    act, slope = [], []
    for i in G:
        got = gelu_and_slope(dot(a2_all[i], expand_cols, 1, 0) + ebias)
        if i + 1 < K:
            got, a2_all[i + 1] = together(got, a2_all[i + 1])
        act.append(got[0])
        slope.append(got[1])
    shrink_grad = sum(dot(act[i], g_all[i], 0, 0) for i in G).astype(BF)
    slope, shrink_grad, act = together(slope, shrink_grad, act)
    shrink_part = lax.psum_scatter(shrink_grad, "fsdp", scatter_dimension=0, tiled=True)
    d_exp = [(dot(g_all[i], shrink_rows, 1, 1) * slope[i].astype(F32)).astype(BF) for i in G]
    d_exp_sum = sum(jnp.sum(d.astype(F32), axis=0) for d in d_exp)

    d_a2 = tp.scatter_core(t, lambda i, a, b: dot(d_exp[i][a:b], expand_cols, 1, 1))
    d_a2, act = together(d_a2, act)
    d_a2 = tp.scatter_far(d_a2)
    branch = tp.scatter_core(t, lambda i, a, b: dot(act[i][a:b], shrink_rows, 1, 0))
    d_a2, d_exp, branch = together(d_a2, d_exp, branch)
    d_a2 = tp.scatter_near(d_a2)
    expand_grad = sum(dot(a2_all[i], d_exp[i], 0, 0) for i in G).astype(BF)
    d_a2, expand_grad, branch = together(d_a2, expand_grad, branch)
    expand_part = lax.psum_scatter(expand_grad, "fsdp", scatter_dimension=0, tiled=True)
    branch = tp.scatter_far(branch)
    d_mid, d_att, sums_two, d_o = turned(tp.table, tp.scatter_end(d_a2), midway, g, gain_two, dense_all)

    d_o, shrink_part, branch = together(d_o, shrink_part, branch)
    d_o = tp.swap(d_o).reshape(R, C, t, W)
    dense_part = outer(tp.table, o, d_att) if near else ()
    d_o, dense_part, branch, shrink_part = together(d_o, dense_part, branch, shrink_part)
    branch = tp.scatter_near(branch)
    shrink_other = over_rep(shrink_part)
    if near:
        dense_part = tp.scatter_given(*[a.reshape(n * W, D) for a in dense_part])
    d_qkv, joined_grad, expand_all = None, [], ()
    for p in range(pairs):
        d_qkv = attention_backward(p, tp.order, prefixes, slopes[2 * p : 2 * p + 2], qkv, d_o, d_qkv)
        d_qkv, dense_part, branch = together(d_qkv, dense_part, branch)
        if p == 0 and near:
            dense_part = tp.scatter_far(dense_part)
        if p == pairs - 1:
            d_qkv, expand_part, shrink_other = together(d_qkv, expand_part, shrink_other)
            expand_all = to_owners(expand_part)
        mine = d_qkv.reshape(K, n * t, 3 * W)[:, :, 384 * p : 384 * (p + 1)]
        grad = sum(dot(a1_all[i], mine[i], 0, 0) for i in G).astype(BF)
        d_qkv, grad, d_o = together(d_qkv, grad, d_o)
        joined_grad.append(grad)
    d_qkv = d_qkv.reshape(K, n * t, 3 * W)
    layer_output = midway + added(tp.scatter_end(branch)) + sbias

    d_qkv_sum = jnp.sum(d_qkv.astype(F32), axis=(0, 1))

    def place(vector, width):
        if near or width != D:
            full = jnp.zeros((F, C, R, width // (F * C * R)), F32)
            full = lax.dynamic_update_slice(full, vector.reshape(F, 1, 1, -1), (0, ctx, rep, 0))
            return full.reshape(F * C, width // D, B).transpose(0, 2, 1).reshape(D, width // D)
        return lax.dynamic_update_slice_in_dim(jnp.zeros((width,), F32), vector, (rep * C + ctx) * W, 0).reshape(D, 1)

    by_part = d_qkv_sum.reshape(pairs, 3, 128)
    rest = [jnp.zeros((D, 2), F32), sums_two.T, place(by_part[:, 0].reshape(W), D), place(by_part[:, 2].reshape(W), D)]
    rest.append(place(d_exp_sum, FF))
    rest = jnp.concatenate(rest, axis=1)
    used = rest.shape[1]
    rest = jnp.pad(rest, ((0, 0), (0, 128 - used)))
    lanes = lambda a: jnp.broadcast_to(a[:, None], (D, 128))
    grad = with_columns(joined_grad, joined_cols, d_qkv_sum.reshape(1, 3 * W), lanes(gain_one), lanes(shift_one), rest)
    joined_part = [lax.psum_scatter(a, "fsdp", scatter_dimension=0, tiled=True) for a in joined_grad[:-1]]
    grad, joined_part, expand_all = together(grad, joined_part, expand_all)
    joined_part.append(lax.psum_scatter(grad, "fsdp", scatter_dimension=0, tiled=True))
    if near:
        dense_part = tp.scatter_near(dense_part)
    d_a1, dense_part = tp.scatter_core(t, lambda i, a, b: dot(d_qkv[i, a:b], joined_cols, 1, 1), dense_part)
    shrink_out = ()
    if near:
        shrink_out = pair_up(rep, shrink_part, shrink_other)
        dense_part = added(tp.scatter_end(dense_part)).astype(BF).reshape(F, W // F, D)
    d_a1, shrink_out, layer_output, dense_part, joined_part = together(d_a1, shrink_out, layer_output, dense_part, joined_part)
    if near:
        dense_part = scatter_shifts(dense_part, "fsdp", F)
    d_a1 = together(*tp.scatter_far(d_a1)) if near else d_a1
    joined_all = to_owners(jnp.concatenate(joined_part, axis=1))
    d_a1 = tp.scatter_near(d_a1)
    if near:
        expand_out = unpack(unpack_expand_kernel, F, expand_all)
        d_a1, expand_out = together(d_a1, expand_out)
    d_a1, dense_part = together(d_a1, dense_part)
    dense_other = over_rep(dense_part) if near else ()
    input_gradient = last(tp.scatter_end(d_a1), x, d_mid, gain_one)
    if near:
        dense_out = pair_up(rep, dense_part, dense_other)
        input_gradient, dense_out, joined_all = together(input_gradient, dense_out, joined_all)

    def both_reps(own, other):
        first = rep == 0
        return jnp.stack([jnp.where(first, own, other), jnp.where(first, other, own)])

    little = jnp.sum(joined_all[:, :, :, 3 * W :].astype(F32), axis=(0, 1)).T
    if near:
        joined_out = unpack(unpack_joined_kernel, F, joined_all, 128)
    else:
        expand_out = expand_all.reshape(R, C, B, F, E).transpose(2, 3, 1, 0, 4).reshape(B, FF).astype(F32)
        both = joined_all[:, :, :, : 3 * W].reshape(R, C, B, pairs, 3, 128).transpose(2, 4, 0, 1, 3, 5)
        joined_out = both.reshape(B, 3 * D).astype(F32)
        shrink_out = both_reps(shrink_part, shrink_other).reshape(FFB, D).astype(F32)
        part = dot(o.transpose(1, 0, 2).reshape(t, D), d_att, 0, 0).astype(BF)
        part = lax.psum_scatter(part, ("fsdp", "ctx"), scatter_dimension=0, tiled=True)
        dense_out = lax.psum(part, "rep").astype(F32)
    gain_one_out, shift_one_out, gain_two_out, shift_two_out, dbias_out, sbias_out, qbias_out, vbias_out = [
        little[i] for i in range(8)
    ]
    ebias_out = little[8:used].reshape(FFB)

    return (
        layer_output.reshape(S, t, D),
        input_gradient.reshape(S, t, D),
        joined_out,
        qbias_out,
        vbias_out,
        dense_out,
        dbias_out,
        expand_out,
        ebias_out,
        shrink_out,
        sbias_out,
        gain_one_out,
        shift_one_out,
        gain_two_out,
        shift_two_out,
    )


def solution(mesh):
    sizes = (mesh.shape["rep"], mesh.shape["fsdp"], mesh.shape["ctx"])
    tokens = P(("rep", "fsdp"), "ctx", None)
    matrix = P(("fsdp", "ctx"), None)
    vector = P(("fsdp", "ctx"))
    weights = (matrix, vector, vector, matrix, vector, matrix, vector, matrix, vector, vector, vector, vector, vector)
    in_specs = (tokens, P(("rep", "fsdp")), *weights, tokens)
    out_specs = (tokens, tokens, *weights)

    def step(*arrays):
        return shards(sizes, *arrays)

    return jax.shard_map(step, mesh=mesh, in_specs=in_specs, out_specs=out_specs, check_vma=False)
```

```python
import functools

import jax
import jax.numpy as jnp
from jax import lax
from jax.experimental import pallas as pl
from jax.experimental.pallas import tpu as pltpu
from jax.sharding import PartitionSpec as P

H = 32
HD = 64
BF = jnp.bfloat16
F32 = jnp.float32
LONGEST = 512
CHEAP = pl.CostEstimate(flops=1, transcendentals=0, bytes_accessed=1)


def dot(a, b, ca, cb):
    return lax.dot_general(a, b, (((ca,), (cb,)), ((), ())), preferred_element_type=F32)


def places(c, n, T, prefix):
    before = lax.broadcasted_iota(jnp.int32, (1, c * T), 1).astype(F32) - c * T if c else None
    row = lax.broadcasted_iota(jnp.int32, (T, (n - c) * T), 0)
    column = lax.broadcasted_iota(jnp.int32, (T, (n - c) * T), 1)
    allowed = column <= jnp.maximum(row, prefix - 1 - c * T)
    return before, jnp.minimum(column, 2 * row - column).astype(F32), allowed


def head_probs(query, key, slope, place, lanes):
    before, near, allowed = place
    raw = dot(jnp.where(lanes, query, jnp.zeros_like(query)), key, 1, 1)
    split = raw.shape[1] - near.shape[1]
    logits = jnp.where(allowed, raw[:, split:] + slope * near, -1e30)
    if split:
        logits = jnp.concatenate([raw[:, :split] + slope * before, logits], axis=1)
    largest = jnp.max(logits, axis=-1, keepdims=True)
    exponent = jnp.exp(logits - largest)
    return exponent * (1.0 / jnp.sum(exponent, axis=-1, keepdims=True))


def forward_kernel(order_ref, prefix_ref, slope_ref, qkv_ref, out_ref):
    C, T = qkv_ref.shape[0] * qkv_ref.shape[2], qkv_ref.shape[3]
    seq, pair = pl.program_id(0), pl.program_id(1)
    at = lambda part: slice(part * 128, part * 128 + 128)
    first = lax.broadcasted_iota(jnp.int32, (T, 128), 1) < HD
    key = [qkv_ref[order_ref[0, c], 0, order_ref[1, c], :, at(1)] for c in range(C)]
    value = [qkv_ref[order_ref[0, c], 0, order_ref[1, c], :, at(2)] for c in range(C)]
    for c in range(C):
        n = min(C, max(c + 1, -(-LONGEST // T)))
        keys = jnp.concatenate(key[:n], axis=0)
        values = jnp.concatenate(value[:n], axis=0)
        query = qkv_ref[order_ref[0, c], 0, order_ref[1, c], :, at(0)] * 0.125
        place = places(c, n, T, prefix_ref[seq])
        out = []
        for h in range(2):
            probs = head_probs(query, keys, slope_ref[2 * pair + h], place, first if h == 0 else ~first)
            out.append(dot(probs.astype(BF), values, 1, 0))
        out_ref[0, c] = jnp.where(first, out[0], out[1]).astype(BF)


def backward_kernel(order_ref, prefix_ref, slope_ref, qkv_ref, d_out_ref, d_qkv_ref, d_key, d_value):
    C, T = qkv_ref.shape[0] * qkv_ref.shape[2], qkv_ref.shape[3]
    seq, pair = pl.program_id(0), pl.program_id(1)
    at = lambda part: slice(part * 128, part * 128 + 128)
    first = lax.broadcasted_iota(jnp.int32, (T, 128), 1) < HD
    d_key[...] = jnp.zeros_like(d_key)
    d_value[...] = jnp.zeros_like(d_value)
    key = [qkv_ref[order_ref[0, c], 0, order_ref[1, c], :, at(1)] for c in range(C)]
    value = [qkv_ref[order_ref[0, c], 0, order_ref[1, c], :, at(2)] for c in range(C)]
    for c in range(C):
        n = min(C, max(c + 1, -(-LONGEST // T)))
        keys = jnp.concatenate(key[:n], axis=0)
        values = jnp.concatenate(value[:n], axis=0)
        query = qkv_ref[order_ref[0, c], 0, order_ref[1, c], :, at(0)]
        d_out = d_out_ref[0, c]
        place = places(c, n, T, prefix_ref[seq])
        d_query = []
        for h in range(2):
            lanes = first if h == 0 else ~first
            probs = head_probs(query * 0.125, keys, slope_ref[2 * pair + h], place, lanes)
            mine = jnp.where(lanes, d_out, jnp.zeros_like(d_out))
            d_probs = dot(mine, values, 1, 1)
            weighted = jnp.sum(probs * d_probs, axis=-1, keepdims=True)
            d_raw = (probs * (d_probs - weighted) * 0.125).astype(BF)
            d_query.append(dot(d_raw, keys, 1, 0))
            d_value[: n * T] += dot(probs.astype(BF), mine, 0, 0)
            d_key[: n * T] += dot(d_raw, jnp.where(lanes, query, jnp.zeros_like(query)), 0, 0)
        d_qkv_ref[order_ref[0, c], 0, order_ref[1, c], :, at(0)] = jnp.where(first, d_query[0], d_query[1]).astype(BF)
    for c in range(C):
        d_qkv_ref[order_ref[0, c], 0, order_ref[1, c], :, at(1)] = d_key[c * T : (c + 1) * T].astype(BF)
        d_qkv_ref[order_ref[0, c], 0, order_ref[1, c], :, at(2)] = d_value[c * T : (c + 1) * T].astype(BF)


def attention_specs(order_ndim, K, n, Y, C, T, pair):
    near = pl.BlockSpec((K, 1, Y, T, 384), lambda s, p, *_: (0, s, 0, 0, p + pair))
    true = pl.BlockSpec((1, C, T, 128), lambda s, p, order, *_: (s ^ order[2, 0], 0, 0, p + pair))
    return near, true


def attention_forward(order, prefix, slopes, qkv):
    K, n, Y, T = qkv.shape[:4]
    C, pairs = K * Y, qkv.shape[4] // 384
    near, true = attention_specs(0, K, n, Y, C, T, 0)
    return pl.pallas_call(
        forward_kernel,
        out_shape=jax.ShapeDtypeStruct((n, C, T, pairs * 128), BF),
        grid_spec=pltpu.PrefetchScalarGridSpec(num_scalar_prefetch=3, grid=(n, pairs), in_specs=[near], out_specs=true),
        compiler_params=vmem(32),
        cost_estimate=pl.CostEstimate(flops=12 * 10**9, transcendentals=0, bytes_accessed=1),
    )(order, prefix, slopes, qkv)


def attention_backward(pair, order, prefix, slopes, qkv, d_out, before=None):
    K, n, Y, T = qkv.shape[:4]
    C = K * Y
    near, true = attention_specs(0, K, n, Y, C, T, pair)
    kernel = backward_kernel
    more, aliases = [], {}
    if before is not None:
        kernel = lambda a, b, c, d, e, _, *rest: backward_kernel(a, b, c, d, e, *rest)
        more, aliases = [before], {5: 0}
    return pl.pallas_call(
        kernel,
        out_shape=jax.ShapeDtypeStruct(qkv.shape, BF),
        grid_spec=pltpu.PrefetchScalarGridSpec(
            num_scalar_prefetch=3,
            grid=(n, 1),
            in_specs=[near, true] + [pl.BlockSpec(memory_space=pl.ANY)] * len(more),
            out_specs=near,
            scratch_shapes=[pltpu.VMEM((C * T, 128), F32), pltpu.VMEM((C * T, 128), F32)],
        ),
        input_output_aliases=aliases,
        compiler_params=vmem(32),
        cost_estimate=pl.CostEstimate(flops=12 * 10**9, transcendentals=0, bytes_accessed=1),
    )(order, prefix, slopes, qkv, d_out, *more)


def whole(shape):
    return pl.BlockSpec(shape, lambda *_: (0,) * len(shape))


def vmem(megabytes):
    return pltpu.CompilerParams(vmem_limit_bytes=megabytes * 1024 * 1024)


def half_turn(tile):
    return jnp.concatenate([tile[:, 64:], tile[:, :64]], axis=1)


def pack_kernel(F, C, rep_ref, joined_ref, expand_ref, out_ref):
    B = joined_ref.shape[0]
    E = expand_ref.shape[1] // (2 * F * C)
    D = joined_ref.shape[1] // 3
    first = lax.broadcasted_iota(jnp.int32, (B, 128), 1) < HD
    rep = rep_ref[0]
    keep = first == (rep == 0)
    for c in range(C):
        for p in range(F // 2):
            for q in range(3):
                one, two = [joined_ref[:, q * D + (f * C + c) * 128 :][:, :128] for f in (2 * p, 2 * p + 1)]
                mine = jnp.where(keep, jnp.where(first, one, two), half_turn(jnp.where(first, two, one)))
                out_ref[c, :, (p * 3 + q) * 128 : (p * 3 + q + 1) * 128] = mine
        for f in range(F):
            from_ = pl.multiple_of((f * C + c) * 2 * E + rep * E, 128)
            to = 3 * F * 64 + f * E
            out_ref[c, :, to : to + E] = expand_ref[:, pl.ds(from_, E)]


def pack(F, C, rep, joined, expand):
    B = joined.shape[0]
    width = 3 * F * 64 + expand.shape[1] // (2 * C)
    return pl.pallas_call(
        functools.partial(pack_kernel, F, C),
        out_shape=jax.ShapeDtypeStruct((C, B, width), BF),
        grid_spec=pltpu.PrefetchScalarGridSpec(
            num_scalar_prefetch=1,
            grid=(1,),
            in_specs=[whole(joined.shape), whole(expand.shape)],
            out_specs=whole((C, B, width)),
        ),
        compiler_params=vmem(24),
        cost_estimate=CHEAP,
    )(rep.reshape(1), joined, expand)


def unpack_joined_kernel(F, ref, out_ref):
    C, B = ref.shape[1:3]
    D = out_ref.shape[1] // 3
    first = lax.broadcasted_iota(jnp.int32, (B, 128), 1) < HD
    for c in range(C):
        for p in range(F // 2):
            for q in range(3):
                at = slice((p * 3 + q) * 128, (p * 3 + q + 1) * 128)
                one, two = ref[0, c, :, at].astype(F32), ref[1, c, :, at].astype(F32)
                for i, f in enumerate((2 * p, 2 * p + 1)):
                    tile = jnp.where(first, half_turn(one) if i else one, two if i else half_turn(two))
                    out_ref[:, q * D + (f * C + c) * 128 : q * D + (f * C + c + 1) * 128] = tile


def unpack_expand_kernel(F, ref, out_ref):
    C = ref.shape[1]
    E = ref.shape[3] // F
    for c in range(C):
        for f in range(F):
            for r in range(2):
                at = ((f * C + c) * 2 + r) * E
                out_ref[:, at : at + E] = ref[r, c, :, f * E : (f + 1) * E].astype(F32)


def unpack(kernel, F, parts, extra=0):
    R, C, B, width = parts.shape
    width -= extra
    return pl.pallas_call(
        functools.partial(kernel, F),
        out_shape=jax.ShapeDtypeStruct((B, R * C * width), F32),
        grid=(1,),
        in_specs=[whole((R, C, B, width))],
        out_specs=whole((B, R * C * width)),
        compiler_params=vmem(32),
        cost_estimate=CHEAP,
    )(parts)


def normed(values):
    average = jnp.mean(values, axis=-1, keepdims=True)
    centred = values - average
    variance = jnp.mean(centred * centred, axis=-1, keepdims=True)
    inverse = lax.rsqrt(variance + 1e-05)
    return centred * inverse, inverse


def norm_kernel(x_ref, gain_ref, shift_ref, out_ref):
    n, _ = normed(x_ref[...].astype(F32))
    out_ref[...] = (n * gain_ref[...] + shift_ref[...]).astype(BF)


def norm(x, gain, shift):
    rows, D = x.shape
    step = min(rows, 256)
    return pl.pallas_call(
        norm_kernel,
        out_shape=jax.ShapeDtypeStruct((rows, D), BF),
        grid=(rows // step,),
        in_specs=[pl.BlockSpec((step, D), lambda i: (i, 0)), whole((1, D)), whole((1, D))],
        out_specs=pl.BlockSpec((step, D), lambda i: (i, 0)),
        compiler_params=vmem(24),
        cost_estimate=CHEAP,
    )(x, gain.reshape(1, D), shift.reshape(1, D))


def attended_kernel(table_ref, o_ref, w_ref, v_ref, x_ref, bias_ref, gain_ref, shift_ref, mid_ref, out_ref):
    d = pl.program_id(0)
    half = pl.num_programs(0) // 2
    weight = jnp.where(d < half, w_ref[0], v_ref[0])
    product = dot(o_ref[0], weight, 1, 0)

    @pl.when(d == 0)
    def _():
        mid_ref[...] = product + x_ref[...].astype(F32) + bias_ref[...]

    @pl.when(d > 0)
    def _():
        mid_ref[...] += product

    @pl.when(d == pl.num_programs(0) - 1)
    def _():
        n, _ = normed(mid_ref[...])
        out_ref[...] = (n * gain_ref[...] + shift_ref[...]).astype(BF)


def attended(table, o, weights, x, bias, gain, shift):
    N, t, W = o.shape
    D = x.shape[1]
    half = N // 2
    weights = [w.reshape(half, W, D) for w in weights]
    return pl.pallas_call(
        attended_kernel,
        out_shape=(jax.ShapeDtypeStruct((t, D), F32), jax.ShapeDtypeStruct((t, D), BF)),
        grid_spec=pltpu.PrefetchScalarGridSpec(
            num_scalar_prefetch=1,
            grid=(N,),
            in_specs=[
                pl.BlockSpec((1, t, W), lambda d, table: (table[d], 0, 0)),
                pl.BlockSpec((1, W, D), lambda d, table: (jnp.minimum(d, half - 1), 0, 0)),
                pl.BlockSpec((1, W, D), lambda d, table: (jnp.maximum(d - half, 0), 0, 0)),
                whole((t, D)),
                whole((1, D)),
                whole((1, D)),
                whole((1, D)),
            ],
            out_specs=(whole((t, D)), whole((t, D))),
        ),
        compiler_params=vmem(32),
        cost_estimate=CHEAP,
    )(table, o, *weights, x, bias.reshape(1, D), gain.reshape(1, D), shift.reshape(1, D))


def turned_kernel(table_ref, a_ref, b_ref, c_ref, mid_ref, g_ref, gain_ref, w_ref, v_ref, d_mid_ref, d_att_ref, sums_ref, d_o_ref):
    d = pl.program_id(0)
    half = pl.num_programs(0) // 2

    @pl.when(d == 0)
    def _():
        grad = a_ref[...].astype(F32) + b_ref[...].astype(F32) + c_ref[...].astype(F32)
        n, inverse = normed(mid_ref[...])
        g = g_ref[...].astype(F32)
        u = grad * gain_ref[...]
        mean_u = jnp.mean(u, axis=-1, keepdims=True)
        mean_un = jnp.mean(u * n, axis=-1, keepdims=True)
        d_mid = g + (u - mean_u - n * mean_un) * inverse
        d_att = d_mid.astype(BF)
        d_mid_ref[...] = d_mid
        d_att_ref[...] = d_att
        rows = (grad * n, grad, d_att.astype(F32), g)
        for i, row in enumerate(rows):
            sums_ref[i : i + 1] = jnp.sum(row, axis=0, keepdims=True)

    weight = jnp.where(d < half, w_ref[0], v_ref[0])
    d_o_ref[0] = dot(d_att_ref[...], weight, 1, 1).astype(BF)


def turned(table, parts, mid, g, gain, weights):
    t, D = mid.shape
    N = table.shape[0]
    half = N // 2
    W = D // N
    weights = [w.reshape(half, W, D) for w in weights]
    full = whole((t, D))
    return pl.pallas_call(
        turned_kernel,
        out_shape=(
            jax.ShapeDtypeStruct((t, D), F32),
            jax.ShapeDtypeStruct((t, D), BF),
            jax.ShapeDtypeStruct((4, D), F32),
            jax.ShapeDtypeStruct((N, t, W), BF),
        ),
        grid_spec=pltpu.PrefetchScalarGridSpec(
            num_scalar_prefetch=1,
            grid=(N,),
            in_specs=[
                full,
                full,
                full,
                full,
                full,
                whole((1, D)),
                pl.BlockSpec((1, W, D), lambda d, table: (jnp.minimum(d, half - 1), 0, 0)),
                pl.BlockSpec((1, W, D), lambda d, table: (jnp.maximum(d - half, 0), 0, 0)),
            ],
            out_specs=(full, full, whole((4, D)), pl.BlockSpec((1, t, W), lambda d, table: (table[d], 0, 0))),
        ),
        compiler_params=vmem(48),
        cost_estimate=CHEAP,
    )(table, *parts, mid, g, gain.reshape(1, D), *weights)


def outer_kernel(table_ref, o_ref, d_att_ref, own_ref, oth_ref):
    d = pl.program_id(0)
    product = dot(o_ref[0], d_att_ref[...], 0, 0).astype(BF)

    @pl.when(d < pl.num_programs(0) // 2)
    def _():
        own_ref[0] = product

    @pl.when(d >= pl.num_programs(0) // 2)
    def _():
        oth_ref[0] = product


def outer(table, o, d_att):
    N, t, W = o.shape
    D = d_att.shape[1]
    half = N // 2
    return pl.pallas_call(
        outer_kernel,
        out_shape=(jax.ShapeDtypeStruct((half, W, D), BF), jax.ShapeDtypeStruct((half, W, D), BF)),
        grid_spec=pltpu.PrefetchScalarGridSpec(
            num_scalar_prefetch=1,
            grid=(N,),
            in_specs=[pl.BlockSpec((1, t, W), lambda d, table: (table[d], 0, 0)), whole((t, D))],
            out_specs=(
                pl.BlockSpec((1, W, D), lambda d, table: (jnp.minimum(d, half - 1), 0, 0)),
                pl.BlockSpec((1, W, D), lambda d, table: (jnp.maximum(d - half, 0), 0, 0)),
            ),
        ),
        compiler_params=vmem(24),
        cost_estimate=CHEAP,
    )(table, o, d_att)


def last_kernel(a_ref, b_ref, c_ref, x_ref, d_mid_ref, gain_ref, out_ref):
    grad = a_ref[...].astype(F32) + b_ref[...].astype(F32) + c_ref[...].astype(F32)
    n, inverse = normed(x_ref[...].astype(F32))
    u = grad * gain_ref[...]
    mean_u = jnp.mean(u, axis=-1, keepdims=True)
    mean_un = jnp.mean(u * n, axis=-1, keepdims=True)
    out_ref[...] = d_mid_ref[...] + (u - mean_u - n * mean_un) * inverse


def last(parts, x, d_mid, gain):
    t, D = x.shape
    full = whole((t, D))
    return pl.pallas_call(
        last_kernel,
        out_shape=jax.ShapeDtypeStruct((t, D), F32),
        grid=(1,),
        in_specs=[full] * 5 + [whole((1, D))],
        out_specs=full,
        compiler_params=vmem(48),
        cost_estimate=pl.CostEstimate(flops=4 * 10**9, transcendentals=0, bytes_accessed=1),
    )(*parts, x, d_mid, gain.reshape(1, D))


def pair_up_kernel(rep_ref, own_ref, other_ref, out_ref):
    m = own_ref.shape[0]
    mine = pl.multiple_of(rep_ref[0] * m, 8)
    theirs = pl.multiple_of((1 - rep_ref[0]) * m, 8)
    out_ref[pl.ds(mine, m)] = own_ref[...].astype(F32)
    out_ref[pl.ds(theirs, m)] = other_ref[...].astype(F32)


def pair_up(rep, own, other):
    m, D = own.shape
    return pl.pallas_call(
        pair_up_kernel,
        out_shape=jax.ShapeDtypeStruct((2 * m, D), F32),
        grid_spec=pltpu.PrefetchScalarGridSpec(
            num_scalar_prefetch=1,
            grid=(1,),
            in_specs=[whole((m, D)), whole((m, D))],
            out_specs=whole((2 * m, D)),
        ),
        compiler_params=vmem(24),
        cost_estimate=CHEAP,
    )(rep.reshape(1), own, other)


def columns_kernel(count, *refs):
    grads, w_ref, sums_ref, gain_ref, shift_ref, rest_ref, out_ref = refs[:count], *refs[count:]
    width = grads[0].shape[1]
    by_d = jnp.zeros((w_ref.shape[0], 1), F32)
    by_g = jnp.zeros((w_ref.shape[0], 1), F32)
    for p, grad_ref in enumerate(grads):
        w = w_ref[:, p * width : (p + 1) * width].astype(F32)
        by_d += jnp.sum(w * sums_ref[:, p * width : (p + 1) * width], axis=1, keepdims=True)
        by_g += jnp.sum(w * grad_ref[...].astype(F32), axis=1, keepdims=True)
    by_n = (by_g - shift_ref[:, :1] * by_d) / gain_ref[:, :1]
    lane = lax.broadcasted_iota(jnp.int32, (w_ref.shape[0], 128), 1)
    small = jnp.where(lane == 0, by_n, jnp.where(lane == 1, by_d, rest_ref[...]))
    out_ref[:, :width] = grads[-1][...]
    out_ref[:, width:] = small.astype(BF)


def with_columns(grads, weight, sums, gain, shift, rest):
    D, width = grads[0].shape
    step = 512
    rows = lambda w: pl.BlockSpec((step, w), lambda i: (i, 0))
    return pl.pallas_call(
        functools.partial(columns_kernel, len(grads)),
        out_shape=jax.ShapeDtypeStruct((D, width + 128), BF),
        grid=(D // step,),
        in_specs=[rows(width)] * len(grads) + [rows(weight.shape[1]), whole(sums.shape), rows(128), rows(128), rows(128)],
        out_specs=rows(width + 128),
        compiler_params=vmem(32),
        cost_estimate=CHEAP,
    )(*grads, weight, sums, gain, shift, rest)


def part_weights_kernel(m, rows, early_ref, late_ref, expand_ref, shrink_ref):
    half = shrink_ref.shape[0] // 2
    width = late_ref.shape[2]
    expand_ref[...] = late_ref[0, :rows]
    shrink_ref[:half] = early_ref[0, m : m + half]
    shrink_ref[half:, :width] = late_ref[0, rows : rows + half]
    shrink_ref[half:, width:] = late_ref[0, rows + half : rows + 2 * half]


def part_weights(early, late, m, rows):
    F, _, D = early.shape
    width = late.shape[2]
    half = (late.shape[1] - rows) // 2
    return pl.pallas_call(
        functools.partial(part_weights_kernel, m, rows),
        out_shape=(jax.ShapeDtypeStruct((F * rows, width), BF), jax.ShapeDtypeStruct((F * 2 * half, D), BF)),
        grid=(F,),
        in_specs=[
            pl.BlockSpec((1,) + early.shape[1:], lambda f: (f, 0, 0)),
            pl.BlockSpec((1,) + late.shape[1:], lambda f: (f, 0, 0)),
        ],
        out_specs=(pl.BlockSpec((rows, width), lambda f: (f, 0)), pl.BlockSpec((2 * half, D), lambda f: (f, 0))),
        compiler_params=vmem(32),
        cost_estimate=CHEAP,
    )(early, late)


def gelu_and_slope(values):
    half = 0.5 + 0.5 * lax.erf(values * 0.7071067811865476)
    density = jnp.exp(values * values * -0.5) * 0.3989422804014327
    return (values * half).astype(BF), (half + values * density).astype(BF)


def together(*values):
    return lax.optimization_barrier(values)


class Plain:
    def __init__(self, R, C):
        self.R, self.C, self.N = R, C, R * C
        self.axes = ("rep", "ctx")
        self.groups = (1, R, C)
        place = jnp.arange(C, dtype=jnp.int32)
        self.order = jnp.stack([place * 0, place, place * 0])
        self.table = jnp.arange(self.N, dtype=jnp.int32)

    def gather(self, x):
        return [lax.all_gather(x, self.axes, axis=0, tiled=True)]

    def gather_two(self, x, g, ready):
        return self.gather(x), self.gather(g), ready

    def scatter_core(self, rows, part, ready=None):
        out = part(0, 0, self.N * rows).astype(BF)
        return out if ready is None else (out, ready)

    def scatter_far(self, state):
        return state

    def scatter_near(self, state):
        return lax.psum_scatter(state, self.axes, scatter_dimension=0, tiled=True)

    def scatter_end(self, state):
        return state, jnp.zeros_like(state), jnp.zeros_like(state)

    def swap(self, parts):
        return lax.all_to_all(parts, self.axes, 0, 0, tiled=True)

    def swap_ctx(self, blocks):
        return lax.all_to_all(blocks, "ctx", 0, 0, tiled=True)

    def prefixes(self, prefix):
        return lax.all_gather(prefix, "rep", axis=0, tiled=True)


class Near(Plain):
    def __init__(self, R, F, C):
        super().__init__(R, C)
        self.F = F
        self.ctx = lax.axis_index("ctx")
        self.rep = lax.axis_index("rep")
        self.fsdp = lax.axis_index("fsdp")
        self.groups = (2, 2, 2)
        place = jnp.arange(C, dtype=jnp.int32) ^ self.ctx
        self.order = jnp.stack([place & 1, place >> 1, place * 0 + self.rep])
        d = jnp.arange(8, dtype=jnp.int32)
        self.table = (self.rep * 4 + self.ctx) ^ ((d & 2) * 2 + (d & 1) * 2 + (d >> 2))

    def over(self, x, d):
        return lax.ppermute(x, "ctx", [(i, i ^ d) for i in range(4)])

    def x(self, x):
        return lax.ppermute(x, "rep", [(0, 1), (1, 0)])

    def y(self, x):
        return self.over(x, 2)

    def core(self, x):
        return self.over(x, 1)

    def gather(self, x):
        return self.gather_core(self.gather_far(x, self.x(x), self.y(x)))

    def gather_far(self, x, from_x, from_y):
        half = x.shape[0] // 2
        near = jnp.concatenate([x, from_y, from_x, jnp.zeros_like(x)], axis=0)
        return near, self.y(from_x[:half]), self.x(from_y[half:])

    def gather_core(self, pieces):
        own, low, high = pieces
        at = own.shape[0] - 2 * low.shape[0]
        own = lax.dynamic_update_slice_in_dim(own, low, at, 0)
        own = lax.dynamic_update_slice_in_dim(own, high, at + low.shape[0], 0)
        return [own, self.core(own)]

    def gather_two(self, x, g, ready):
        t = x.shape[0]
        both = jnp.concatenate([x, g], axis=0)
        from_x = self.x(both)
        both, ready = together(both, ready)
        from_y = self.y(both)
        far_x, far_g = together(self.y(from_x[:t]), self.x(from_y[t:]))
        x = jnp.concatenate([x, from_y[:t], from_x[:t], far_x], axis=0)
        g = jnp.concatenate([g, from_y[t:], from_x[t:], far_g], axis=0)
        return [x, self.core(x)], [g, self.core(g)], ready

    def scatter_core(self, rows, part, ready=None):
        far_x = part(1, 2 * rows, 4 * rows).astype(BF)
        near_x = part(1, 0, 2 * rows).astype(BF)
        far_x, near_x, halfway = together(far_x, near_x, () if ready is None else ready)
        far_x = (part(0, 2 * rows, 4 * rows) + self.core(far_x).astype(F32)).astype(BF)
        near_x = (part(0, 0, 2 * rows) + self.core(near_x).astype(F32)).astype(BF)
        return (far_x, near_x) if ready is None else ((far_x, near_x), halfway)

    def scatter_given(self, own, oth):
        total = (own.astype(F32) + self.core(oth).astype(F32)).astype(BF)
        return total[total.shape[0] // 2 :], total[: total.shape[0] // 2]

    def scatter_far(self, state):
        far_x, near_x = state
        rows = far_x.shape[0] // 2
        half = rows // 2
        return far_x, near_x, self.y(far_x[rows : rows + half]), self.x(far_x[rows + half :])

    def scatter_near(self, state):
        far_x, near_x, to_y, to_x = state
        rows = far_x.shape[0] // 2
        half = rows // 2
        by_x, near_y = far_x[:rows].astype(F32), near_x[rows:].astype(F32)
        by_x = jnp.concatenate([by_x[:half] + to_y.astype(F32), by_x[half:]], axis=0)
        by_y = jnp.concatenate([near_y[:half], near_y[half:] + to_x.astype(F32)], axis=0)
        return near_x, self.x(by_x.astype(BF)), self.y(by_y.astype(BF))

    def scatter_end(self, state):
        return state

    def prefixes(self, prefix):
        return jnp.concatenate([prefix, self.x(prefix)])

    def gather_ctx(self, x):
        x = jnp.stack([x, self.y(x)])
        x = jnp.stack([x, self.core(x)], axis=1).reshape(4, *x.shape[1:])
        x = jnp.take(x, jnp.arange(4) ^ self.ctx, axis=0)
        return x.transpose(1, 0, 2).reshape(-1, x.shape[2])


def added(parts):
    rows = parts[-1].shape[0]
    return sum(a[:rows].astype(F32) for a in parts)


def scatter_shifts(x, axis, size):
    me = lax.axis_index(axis)
    total = lax.dynamic_index_in_dim(x, me, 0, keepdims=False)
    for s in range(1, size):
        mine = lax.dynamic_index_in_dim(x, lax.rem(me + s, size), 0, keepdims=False)
        total = total.astype(F32) + lax.ppermute(mine, axis, [(i, (i + s) % size) for i in range(size)]).astype(F32)
    return total.astype(x.dtype)


def shards(
    sizes,
    inputs,
    prefix,
    joined_weight,
    query_bias,
    value_bias,
    dense_weight,
    dense_bias,
    expand_weight,
    expand_bias,
    shrink_weight,
    shrink_bias,
    first_gain,
    first_shift,
    second_gain,
    second_shift,
    cotangent,
):
    R, F, C = sizes
    N = R * C
    rep = lax.axis_index("rep")
    ctx = lax.axis_index("ctx")
    S, t, D = inputs.shape
    assert S == 1
    B = joined_weight.shape[0]
    FFB = shrink_weight.shape[0]
    FF = FFB * F * C
    E = FFB // R
    W = D // N
    near = R == 2 and C == 4 and B == 2 * HD
    tp = Near(R, F, C) if near else Plain(R, C)
    K, _, Y = tp.groups
    G = range(K)
    n = N // K
    pairs = W // 128

    def half_rows(weight):
        m = weight.shape[0] // R
        return lax.dynamic_slice_in_dim(weight, rep * m, m, 0)

    def widen(blocks):
        return lax.all_gather(blocks.reshape(C * B, -1), "fsdp", axis=0, tiled=True)

    def to_owners(part):
        blocks = jnp.concatenate([part.reshape(C, B, -1)] * R)
        return lax.all_to_all(blocks, ("rep", "ctx"), 0, 0, tiled=True).reshape(R, C, B, -1)

    def over_rep(x):
        return lax.ppermute(x, "rep", [(0, 1), (1, 0)])

    x = inputs.reshape(t, D)
    g = cotangent.reshape(t, D)
    small = jnp.concatenate(
        [first_gain, first_shift, second_gain, second_shift, dense_bias, shrink_bias, query_bias, value_bias, expand_bias]
    )
    if near:
        low, high = jnp.split(half_rows(shrink_weight), 2)
        m = B // R
        small = jnp.pad(small.reshape(1, -1), ((0, 15), (0, D - small.shape[0])))
        early = lax.all_gather(jnp.concatenate([half_rows(dense_weight), low, small]), "fsdp", axis=0, tiled=False)
        dense_rows = early[:, :m].reshape(F * m, D)
        small = tp.gather_ctx(early[:, m + low.shape[0], : 8 * B + FFB])
        blocks = lax.all_to_all(pack(F, C, rep, joined_weight, expand_weight), "ctx", 0, 0, tiled=True)
        joined_blocks, expand_blocks = blocks[:, :, : 3 * W], blocks[:, :, 3 * W :]
    else:
        dense_rows = lax.all_gather(dense_weight, ("fsdp", "ctx"), axis=0, tiled=True)
        small = lax.all_gather(small, ("fsdp", "ctx"), axis=0, tiled=False)
        pieces = joined_weight.reshape(B, 3, R, C, pairs, 128)
        pieces = lax.dynamic_index_in_dim(pieces, rep, 2, keepdims=False).transpose(2, 0, 3, 1, 4)
        joined_blocks = lax.all_to_all(pieces.reshape(C, B, 3 * W), "ctx", 0, 0, tiled=True)
        pieces = expand_weight.reshape(B, F, C, R, E)
        pieces = lax.dynamic_index_in_dim(pieces, rep, 3, keepdims=False).transpose(2, 0, 1, 3)
        expand_blocks = lax.all_to_all(pieces.reshape(C, B, F * E), "ctx", 0, 0, tiled=True)
    x_all, g_all, (joined_blocks, expand_blocks) = tp.gather_two(x, g, (joined_blocks, expand_blocks))
    joined_cols = widen(joined_blocks)
    if near:
        late = jnp.concatenate([expand_blocks.reshape(C * B, -1), high[:, : D // 2], high[:, D // 2 :]])
        late = lax.all_gather(late, "fsdp", axis=0, tiled=False)
    else:
        expand_cols = widen(expand_blocks)
        shrink_rows = lax.all_gather(half_rows(shrink_weight), "fsdp", axis=0, tiled=True)
    prefixes = tp.prefixes(prefix)

    small = small.astype(F32)
    gain_one, shift_one, gain_two, shift_two, dbias, sbias, qbias, vbias = [
        small[:, i * B : (i + 1) * B].reshape(D) for i in range(8)
    ]
    ebias = small[:, 8 * B :].reshape(F, C, R, E)
    ebias = lax.dynamic_index_in_dim(lax.dynamic_index_in_dim(ebias, ctx, 1, False), rep, 1, False)
    ebias = ebias.reshape(F * E)

    def my_features(vector):
        if near:
            v = vector.reshape(F, C, R, -1)
            return lax.dynamic_index_in_dim(lax.dynamic_index_in_dim(v, ctx, 1, False), rep, 1, False).reshape(W)
        return lax.dynamic_slice_in_dim(vector, (rep * C + ctx) * W, W, 0)

    my_heads = my_features(jnp.repeat(jnp.arange(H, dtype=jnp.int32), HD)).reshape(-1, HD)[:, 0]
    slopes = jnp.exp2(-8.0 * (my_heads.astype(F32) + 1.0) / H)

    if near:
        own, dense_rows = together(x_all[0], dense_rows)
        x_all[0] = own
    a1_all = [norm(a, gain_one, shift_one) for a in x_all]
    if near:
        a1_all, joined_cols = together(a1_all, joined_cols)
    else:
        dense_all = [dense_rows[: D // 2], dense_rows[D // 2 :]]
    qkv_bias = jnp.stack([my_features(qbias), jnp.zeros((W,), F32), my_features(vbias)])
    qkv_bias = qkv_bias.reshape(3, pairs, 128).transpose(1, 0, 2).reshape(3 * W)
    qkv = jnp.stack([(dot(a, joined_cols, 1, 0) + qkv_bias).astype(BF) for a in a1_all])
    qkv = qkv.reshape(K, R, Y, t, 3 * W)
    if near:
        from_x, from_y, qkv = together(tp.x(dense_rows), tp.y(dense_rows), qkv)
        dense_all = tp.gather_far(dense_rows, from_x, from_y)
    out = attention_forward(tp.order, prefixes, slopes, qkv)
    out, g_all, dense_all = together(out, g_all, dense_all)
    if near:
        dense_all = tp.gather_core(dense_all)
    o = tp.swap(out.reshape(N, t, W))
    midway, a2 = attended(tp.table, o, dense_all, x, dbias, gain_two, shift_two)

    if near:
        pieces, late = together(tp.gather_far(a2, tp.x(a2), tp.y(a2)), late)
        expand_cols, shrink_rows = part_weights(early, late, m, C * B)
        a2_all = tp.gather_core(pieces)
    else:
        a2_all = tp.gather(a2)
    act, slope = [], []
    for i in G:
        got = gelu_and_slope(dot(a2_all[i], expand_cols, 1, 0) + ebias)
        if i + 1 < K:
            got, a2_all[i + 1] = together(got, a2_all[i + 1])
        act.append(got[0])
        slope.append(got[1])
    shrink_grad = sum(dot(act[i], g_all[i], 0, 0) for i in G).astype(BF)
    slope, shrink_grad, act = together(slope, shrink_grad, act)
    shrink_part = lax.psum_scatter(shrink_grad, "fsdp", scatter_dimension=0, tiled=True)
    d_exp = [(dot(g_all[i], shrink_rows, 1, 1) * slope[i].astype(F32)).astype(BF) for i in G]
    d_exp_sum = sum(jnp.sum(d.astype(F32), axis=0) for d in d_exp)

    d_a2 = tp.scatter_core(t, lambda i, a, b: dot(d_exp[i][a:b], expand_cols, 1, 1))
    d_a2, act = together(d_a2, act)
    d_a2 = tp.scatter_far(d_a2)
    branch = tp.scatter_core(t, lambda i, a, b: dot(act[i][a:b], shrink_rows, 1, 0))
    d_a2, d_exp, branch = together(d_a2, d_exp, branch)
    d_a2 = tp.scatter_near(d_a2)
    expand_grad = sum(dot(a2_all[i], d_exp[i], 0, 0) for i in G).astype(BF)
    d_a2, expand_grad, branch = together(d_a2, expand_grad, branch)
    expand_part = lax.psum_scatter(expand_grad, "fsdp", scatter_dimension=0, tiled=True)
    branch = tp.scatter_far(branch)
    d_mid, d_att, sums_two, d_o = turned(tp.table, tp.scatter_end(d_a2), midway, g, gain_two, dense_all)

    d_o, shrink_part, branch = together(d_o, shrink_part, branch)
    d_o = tp.swap(d_o).reshape(R, C, t, W)
    dense_part = outer(tp.table, o, d_att) if near else ()
    d_o, dense_part, branch, shrink_part = together(d_o, dense_part, branch, shrink_part)
    branch = tp.scatter_near(branch)
    shrink_other = over_rep(shrink_part)
    if near:
        dense_part = tp.scatter_given(*[a.reshape(n * W, D) for a in dense_part])
    d_qkv, joined_grad, expand_all = None, [], ()
    for p in range(pairs):
        d_qkv = attention_backward(p, tp.order, prefixes, slopes[2 * p : 2 * p + 2], qkv, d_o, d_qkv)
        d_qkv, dense_part, branch = together(d_qkv, dense_part, branch)
        if p == 0 and near:
            dense_part = tp.scatter_far(dense_part)
        if p == pairs - 1:
            d_qkv, expand_part, shrink_other = together(d_qkv, expand_part, shrink_other)
            expand_all = to_owners(expand_part)
        mine = d_qkv.reshape(K, n * t, 3 * W)[:, :, 384 * p : 384 * (p + 1)]
        grad = sum(dot(a1_all[i], mine[i], 0, 0) for i in G).astype(BF)
        d_qkv, grad, d_o = together(d_qkv, grad, d_o)
        joined_grad.append(grad)
    d_qkv = d_qkv.reshape(K, n * t, 3 * W)
    layer_output = midway + added(tp.scatter_end(branch)) + sbias

    d_qkv_sum = jnp.sum(d_qkv.astype(F32), axis=(0, 1))

    def place(vector, width):
        if near or width != D:
            full = jnp.zeros((F, C, R, width // (F * C * R)), F32)
            full = lax.dynamic_update_slice(full, vector.reshape(F, 1, 1, -1), (0, ctx, rep, 0))
            return full.reshape(F * C, width // D, B).transpose(0, 2, 1).reshape(D, width // D)
        return lax.dynamic_update_slice_in_dim(jnp.zeros((width,), F32), vector, (rep * C + ctx) * W, 0).reshape(D, 1)

    by_part = d_qkv_sum.reshape(pairs, 3, 128)
    rest = [jnp.zeros((D, 2), F32), sums_two.T, place(by_part[:, 0].reshape(W), D), place(by_part[:, 2].reshape(W), D)]
    rest.append(place(d_exp_sum, FF))
    rest = jnp.concatenate(rest, axis=1)
    used = rest.shape[1]
    rest = jnp.pad(rest, ((0, 0), (0, 128 - used)))
    lanes = lambda a: jnp.broadcast_to(a[:, None], (D, 128))
    grad = with_columns(joined_grad, joined_cols, d_qkv_sum.reshape(1, 3 * W), lanes(gain_one), lanes(shift_one), rest)
    joined_part = [lax.psum_scatter(a, "fsdp", scatter_dimension=0, tiled=True) for a in joined_grad[:-1]]
    grad, joined_part = together(grad, joined_part)
    joined_part.append(lax.psum_scatter(grad, "fsdp", scatter_dimension=0, tiled=True))
    if near:
        dense_part = tp.scatter_near(dense_part)
    d_a1, expand_all = tp.scatter_core(t, lambda i, a, b: dot(d_qkv[i, a:b], joined_cols, 1, 1), expand_all)
    shrink_out = ()
    if near:
        shrink_out = pair_up(rep, shrink_part, shrink_other)
        dense_part = added(tp.scatter_end(dense_part)).astype(BF).reshape(F, W // F, D)
    d_a1, shrink_out, layer_output, dense_part, joined_part = together(d_a1, shrink_out, layer_output, dense_part, joined_part)
    if near:
        dense_part = scatter_shifts(dense_part, "fsdp", F)
    d_a1 = together(*tp.scatter_far(d_a1)) if near else d_a1
    joined_all = to_owners(jnp.concatenate(joined_part, axis=1))
    d_a1 = tp.scatter_near(d_a1)
    if near:
        expand_out = unpack(unpack_expand_kernel, F, expand_all)
        d_a1, expand_out = together(d_a1, expand_out)
    d_a1, dense_part = together(d_a1, dense_part)
    dense_other = over_rep(dense_part) if near else ()
    input_gradient = last(tp.scatter_end(d_a1), x, d_mid, gain_one)
    if near:
        dense_out = pair_up(rep, dense_part, dense_other)
        input_gradient, dense_out, joined_all = together(input_gradient, dense_out, joined_all)

    def both_reps(own, other):
        first = rep == 0
        return jnp.stack([jnp.where(first, own, other), jnp.where(first, other, own)])

    little = jnp.sum(joined_all[:, :, :, 3 * W :].astype(F32), axis=(0, 1)).T
    if near:
        joined_out = unpack(unpack_joined_kernel, F, joined_all, 128)
    else:
        expand_out = expand_all.reshape(R, C, B, F, E).transpose(2, 3, 1, 0, 4).reshape(B, FF).astype(F32)
        both = joined_all[:, :, :, : 3 * W].reshape(R, C, B, pairs, 3, 128).transpose(2, 4, 0, 1, 3, 5)
        joined_out = both.reshape(B, 3 * D).astype(F32)
        shrink_out = both_reps(shrink_part, shrink_other).reshape(FFB, D).astype(F32)
        part = dot(o.transpose(1, 0, 2).reshape(t, D), d_att, 0, 0).astype(BF)
        part = lax.psum_scatter(part, ("fsdp", "ctx"), scatter_dimension=0, tiled=True)
        dense_out = lax.psum(part, "rep").astype(F32)
    gain_one_out, shift_one_out, gain_two_out, shift_two_out, dbias_out, sbias_out, qbias_out, vbias_out = [
        little[i] for i in range(8)
    ]
    ebias_out = little[8:used].reshape(FFB)

    return (
        layer_output.reshape(S, t, D),
        input_gradient.reshape(S, t, D),
        joined_out,
        qbias_out,
        vbias_out,
        dense_out,
        dbias_out,
        expand_out,
        ebias_out,
        shrink_out,
        sbias_out,
        gain_one_out,
        shift_one_out,
        gain_two_out,
        shift_two_out,
    )


def solution(mesh):
    sizes = (mesh.shape["rep"], mesh.shape["fsdp"], mesh.shape["ctx"])
    tokens = P(("rep", "fsdp"), "ctx", None)
    matrix = P(("fsdp", "ctx"), None)
    vector = P(("fsdp", "ctx"))
    weights = (matrix, vector, vector, matrix, vector, matrix, vector, matrix, vector, vector, vector, vector, vector)
    in_specs = (tokens, P(("rep", "fsdp")), *weights, tokens)
    out_specs = (tokens, tokens, *weights)

    def step(*arrays):
        return shards(sizes, *arrays)

    return jax.shard_map(step, mesh=mesh, in_specs=in_specs, out_specs=out_specs, check_vma=False)
```

```python
import functools

import jax
import jax.numpy as jnp
from jax import lax
from jax.experimental import pallas as pl
from jax.experimental.pallas import tpu as pltpu
from jax.sharding import PartitionSpec as P

H = 32
HD = 64
BF = jnp.bfloat16
F32 = jnp.float32
LONGEST = 512
CHEAP = pl.CostEstimate(flops=1, transcendentals=0, bytes_accessed=1)


def dot(a, b, ca, cb):
    return lax.dot_general(a, b, (((ca,), (cb,)), ((), ())), preferred_element_type=F32)


def places(c, n, T, prefix):
    before = lax.broadcasted_iota(jnp.int32, (1, c * T), 1).astype(F32) - c * T if c else None
    row = lax.broadcasted_iota(jnp.int32, (T, (n - c) * T), 0)
    column = lax.broadcasted_iota(jnp.int32, (T, (n - c) * T), 1)
    allowed = column <= jnp.maximum(row, prefix - 1 - c * T)
    return before, jnp.minimum(column, 2 * row - column).astype(F32), allowed


def head_probs(query, key, slope, place, lanes):
    before, near, allowed = place
    raw = dot(jnp.where(lanes, query, jnp.zeros_like(query)), key, 1, 1)
    split = raw.shape[1] - near.shape[1]
    logits = jnp.where(allowed, raw[:, split:] + slope * near, -1e30)
    if split:
        logits = jnp.concatenate([raw[:, :split] + slope * before, logits], axis=1)
    largest = jnp.max(logits, axis=-1, keepdims=True)
    exponent = jnp.exp(logits - largest)
    return exponent * (1.0 / jnp.sum(exponent, axis=-1, keepdims=True))


def forward_kernel(order_ref, prefix_ref, slope_ref, qkv_ref, out_ref):
    C, T = qkv_ref.shape[0] * qkv_ref.shape[2], qkv_ref.shape[3]
    seq, pair = pl.program_id(0), pl.program_id(1)
    at = lambda part: slice(part * 128, part * 128 + 128)
    first = lax.broadcasted_iota(jnp.int32, (T, 128), 1) < HD
    key = [qkv_ref[order_ref[0, c], 0, order_ref[1, c], :, at(1)] for c in range(C)]
    value = [qkv_ref[order_ref[0, c], 0, order_ref[1, c], :, at(2)] for c in range(C)]
    for c in range(C):
        n = min(C, max(c + 1, -(-LONGEST // T)))
        keys = jnp.concatenate(key[:n], axis=0)
        values = jnp.concatenate(value[:n], axis=0)
        query = qkv_ref[order_ref[0, c], 0, order_ref[1, c], :, at(0)] * 0.125
        place = places(c, n, T, prefix_ref[seq])
        out = []
        for h in range(2):
            probs = head_probs(query, keys, slope_ref[2 * pair + h], place, first if h == 0 else ~first)
            out.append(dot(probs.astype(BF), values, 1, 0))
        out_ref[0, c] = jnp.where(first, out[0], out[1]).astype(BF)


def backward_kernel(order_ref, prefix_ref, slope_ref, qkv_ref, d_out_ref, d_qkv_ref, d_key, d_value):
    C, T = qkv_ref.shape[0] * qkv_ref.shape[2], qkv_ref.shape[3]
    seq, pair = pl.program_id(0), pl.program_id(1)
    at = lambda part: slice(part * 128, part * 128 + 128)
    first = lax.broadcasted_iota(jnp.int32, (T, 128), 1) < HD
    d_key[...] = jnp.zeros_like(d_key)
    d_value[...] = jnp.zeros_like(d_value)
    key = [qkv_ref[order_ref[0, c], 0, order_ref[1, c], :, at(1)] for c in range(C)]
    value = [qkv_ref[order_ref[0, c], 0, order_ref[1, c], :, at(2)] for c in range(C)]
    for c in range(C):
        n = min(C, max(c + 1, -(-LONGEST // T)))
        keys = jnp.concatenate(key[:n], axis=0)
        values = jnp.concatenate(value[:n], axis=0)
        query = qkv_ref[order_ref[0, c], 0, order_ref[1, c], :, at(0)]
        d_out = d_out_ref[0, c]
        place = places(c, n, T, prefix_ref[seq])
        d_query = []
        for h in range(2):
            lanes = first if h == 0 else ~first
            probs = head_probs(query * 0.125, keys, slope_ref[2 * pair + h], place, lanes)
            mine = jnp.where(lanes, d_out, jnp.zeros_like(d_out))
            d_probs = dot(mine, values, 1, 1)
            weighted = jnp.sum(probs * d_probs, axis=-1, keepdims=True)
            d_raw = (probs * (d_probs - weighted) * 0.125).astype(BF)
            d_query.append(dot(d_raw, keys, 1, 0))
            d_value[: n * T] += dot(probs.astype(BF), mine, 0, 0)
            d_key[: n * T] += dot(d_raw, jnp.where(lanes, query, jnp.zeros_like(query)), 0, 0)
        d_qkv_ref[order_ref[0, c], 0, order_ref[1, c], :, at(0)] = jnp.where(first, d_query[0], d_query[1]).astype(BF)
    for c in range(C):
        d_qkv_ref[order_ref[0, c], 0, order_ref[1, c], :, at(1)] = d_key[c * T : (c + 1) * T].astype(BF)
        d_qkv_ref[order_ref[0, c], 0, order_ref[1, c], :, at(2)] = d_value[c * T : (c + 1) * T].astype(BF)


def attention_specs(order_ndim, K, n, Y, C, T, pair):
    near = pl.BlockSpec((K, 1, Y, T, 384), lambda s, p, *_: (0, s, 0, 0, p + pair))
    true = pl.BlockSpec((1, C, T, 128), lambda s, p, order, *_: (s ^ order[2, 0], 0, 0, p + pair))
    return near, true


def attention_forward(order, prefix, slopes, qkv):
    K, n, Y, T = qkv.shape[:4]
    C, pairs = K * Y, qkv.shape[4] // 384
    near, true = attention_specs(0, K, n, Y, C, T, 0)
    return pl.pallas_call(
        forward_kernel,
        out_shape=jax.ShapeDtypeStruct((n, C, T, pairs * 128), BF),
        grid_spec=pltpu.PrefetchScalarGridSpec(num_scalar_prefetch=3, grid=(n, pairs), in_specs=[near], out_specs=true),
        compiler_params=vmem(32),
        cost_estimate=pl.CostEstimate(flops=6 * 10**9, transcendentals=0, bytes_accessed=1),
    )(order, prefix, slopes, qkv)


def attention_backward(pair, order, prefix, slopes, qkv, d_out, before=None):
    K, n, Y, T = qkv.shape[:4]
    C = K * Y
    near, true = attention_specs(0, K, n, Y, C, T, pair)
    kernel = backward_kernel
    more, aliases = [], {}
    if before is not None:
        kernel = lambda a, b, c, d, e, _, *rest: backward_kernel(a, b, c, d, e, *rest)
        more, aliases = [before], {5: 0}
    return pl.pallas_call(
        kernel,
        out_shape=jax.ShapeDtypeStruct(qkv.shape, BF),
        grid_spec=pltpu.PrefetchScalarGridSpec(
            num_scalar_prefetch=3,
            grid=(n, 1),
            in_specs=[near, true] + [pl.BlockSpec(memory_space=pl.ANY)] * len(more),
            out_specs=near,
            scratch_shapes=[pltpu.VMEM((C * T, 128), F32), pltpu.VMEM((C * T, 128), F32)],
        ),
        input_output_aliases=aliases,
        compiler_params=vmem(32),
        cost_estimate=pl.CostEstimate(flops=6 * 10**9, transcendentals=0, bytes_accessed=1),
    )(order, prefix, slopes, qkv, d_out, *more)


def whole(shape):
    return pl.BlockSpec(shape, lambda *_: (0,) * len(shape))


def vmem(megabytes):
    return pltpu.CompilerParams(vmem_limit_bytes=megabytes * 1024 * 1024)


def half_turn(tile):
    return jnp.concatenate([tile[:, 64:], tile[:, :64]], axis=1)


def pack_kernel(F, C, rep_ref, joined_ref, expand_ref, out_ref):
    B = joined_ref.shape[0]
    E = expand_ref.shape[1] // (2 * F * C)
    D = joined_ref.shape[1] // 3
    first = lax.broadcasted_iota(jnp.int32, (B, 128), 1) < HD
    rep = rep_ref[0]
    keep = first == (rep == 0)
    for c in range(C):
        for p in range(F // 2):
            for q in range(3):
                one, two = [joined_ref[:, q * D + (f * C + c) * 128 :][:, :128] for f in (2 * p, 2 * p + 1)]
                mine = jnp.where(keep, jnp.where(first, one, two), half_turn(jnp.where(first, two, one)))
                out_ref[c, :, (p * 3 + q) * 128 : (p * 3 + q + 1) * 128] = mine
        for f in range(F):
            from_ = pl.multiple_of((f * C + c) * 2 * E + rep * E, 128)
            to = 3 * F * 64 + f * E
            out_ref[c, :, to : to + E] = expand_ref[:, pl.ds(from_, E)]


def pack(F, C, rep, joined, expand):
    B = joined.shape[0]
    width = 3 * F * 64 + expand.shape[1] // (2 * C)
    return pl.pallas_call(
        functools.partial(pack_kernel, F, C),
        out_shape=jax.ShapeDtypeStruct((C, B, width), BF),
        grid_spec=pltpu.PrefetchScalarGridSpec(
            num_scalar_prefetch=1,
            grid=(1,),
            in_specs=[whole(joined.shape), whole(expand.shape)],
            out_specs=whole((C, B, width)),
        ),
        compiler_params=vmem(24),
        cost_estimate=CHEAP,
    )(rep.reshape(1), joined, expand)


def unpack_joined_kernel(F, ref, out_ref):
    C, B = ref.shape[1:3]
    D = out_ref.shape[1] // 3
    first = lax.broadcasted_iota(jnp.int32, (B, 128), 1) < HD
    for c in range(C):
        for p in range(F // 2):
            for q in range(3):
                at = slice((p * 3 + q) * 128, (p * 3 + q + 1) * 128)
                one, two = ref[0, c, :, at].astype(F32), ref[1, c, :, at].astype(F32)
                for i, f in enumerate((2 * p, 2 * p + 1)):
                    tile = jnp.where(first, half_turn(one) if i else one, two if i else half_turn(two))
                    out_ref[:, q * D + (f * C + c) * 128 : q * D + (f * C + c + 1) * 128] = tile


def unpack_expand_kernel(F, ref, out_ref):
    C = ref.shape[1]
    E = ref.shape[3] // F
    for c in range(C):
        for f in range(F):
            for r in range(2):
                at = ((f * C + c) * 2 + r) * E
                out_ref[:, at : at + E] = ref[r, c, :, f * E : (f + 1) * E].astype(F32)


def unpack(kernel, F, parts, extra=0):
    R, C, B, width = parts.shape
    width -= extra
    return pl.pallas_call(
        functools.partial(kernel, F),
        out_shape=jax.ShapeDtypeStruct((B, R * C * width), F32),
        grid=(1,),
        in_specs=[whole((R, C, B, width))],
        out_specs=whole((B, R * C * width)),
        compiler_params=vmem(32),
        cost_estimate=CHEAP,
    )(parts)


def normed(values):
    average = jnp.mean(values, axis=-1, keepdims=True)
    centred = values - average
    variance = jnp.mean(centred * centred, axis=-1, keepdims=True)
    inverse = lax.rsqrt(variance + 1e-05)
    return centred * inverse, inverse


def norm_kernel(x_ref, gain_ref, shift_ref, out_ref):
    n, _ = normed(x_ref[...].astype(F32))
    out_ref[...] = (n * gain_ref[...] + shift_ref[...]).astype(BF)


def norm(x, gain, shift):
    rows, D = x.shape
    step = min(rows, 256)
    return pl.pallas_call(
        norm_kernel,
        out_shape=jax.ShapeDtypeStruct((rows, D), BF),
        grid=(rows // step,),
        in_specs=[pl.BlockSpec((step, D), lambda i: (i, 0)), whole((1, D)), whole((1, D))],
        out_specs=pl.BlockSpec((step, D), lambda i: (i, 0)),
        compiler_params=vmem(24),
        cost_estimate=CHEAP,
    )(x, gain.reshape(1, D), shift.reshape(1, D))


def attended_kernel(table_ref, o_ref, w_ref, v_ref, x_ref, bias_ref, gain_ref, shift_ref, mid_ref, out_ref):
    d = pl.program_id(0)
    half = pl.num_programs(0) // 2
    weight = jnp.where(d < half, w_ref[0], v_ref[0])
    product = dot(o_ref[0], weight, 1, 0)

    @pl.when(d == 0)
    def _():
        mid_ref[...] = product + x_ref[...].astype(F32) + bias_ref[...]

    @pl.when(d > 0)
    def _():
        mid_ref[...] += product

    @pl.when(d == pl.num_programs(0) - 1)
    def _():
        n, _ = normed(mid_ref[...])
        out_ref[...] = (n * gain_ref[...] + shift_ref[...]).astype(BF)


def attended(table, o, weights, x, bias, gain, shift):
    N, t, W = o.shape
    D = x.shape[1]
    half = N // 2
    weights = [w.reshape(half, W, D) for w in weights]
    return pl.pallas_call(
        attended_kernel,
        out_shape=(jax.ShapeDtypeStruct((t, D), F32), jax.ShapeDtypeStruct((t, D), BF)),
        grid_spec=pltpu.PrefetchScalarGridSpec(
            num_scalar_prefetch=1,
            grid=(N,),
            in_specs=[
                pl.BlockSpec((1, t, W), lambda d, table: (table[d], 0, 0)),
                pl.BlockSpec((1, W, D), lambda d, table: (jnp.minimum(d, half - 1), 0, 0)),
                pl.BlockSpec((1, W, D), lambda d, table: (jnp.maximum(d - half, 0), 0, 0)),
                whole((t, D)),
                whole((1, D)),
                whole((1, D)),
                whole((1, D)),
            ],
            out_specs=(whole((t, D)), whole((t, D))),
        ),
        compiler_params=vmem(32),
        cost_estimate=CHEAP,
    )(table, o, *weights, x, bias.reshape(1, D), gain.reshape(1, D), shift.reshape(1, D))


def turned_kernel(table_ref, a_ref, b_ref, c_ref, mid_ref, g_ref, gain_ref, w_ref, v_ref, d_mid_ref, d_att_ref, sums_ref, d_o_ref):
    d = pl.program_id(0)
    half = pl.num_programs(0) // 2

    @pl.when(d == 0)
    def _():
        grad = a_ref[...].astype(F32) + b_ref[...].astype(F32) + c_ref[...].astype(F32)
        n, inverse = normed(mid_ref[...])
        g = g_ref[...].astype(F32)
        u = grad * gain_ref[...]
        mean_u = jnp.mean(u, axis=-1, keepdims=True)
        mean_un = jnp.mean(u * n, axis=-1, keepdims=True)
        d_mid = g + (u - mean_u - n * mean_un) * inverse
        d_att = d_mid.astype(BF)
        d_mid_ref[...] = d_mid
        d_att_ref[...] = d_att
        rows = (grad * n, grad, d_att.astype(F32), g)
        for i, row in enumerate(rows):
            sums_ref[i : i + 1] = jnp.sum(row, axis=0, keepdims=True)

    weight = jnp.where(d < half, w_ref[0], v_ref[0])
    d_o_ref[0] = dot(d_att_ref[...], weight, 1, 1).astype(BF)


def turned(table, parts, mid, g, gain, weights):
    t, D = mid.shape
    N = table.shape[0]
    half = N // 2
    W = D // N
    weights = [w.reshape(half, W, D) for w in weights]
    full = whole((t, D))
    return pl.pallas_call(
        turned_kernel,
        out_shape=(
            jax.ShapeDtypeStruct((t, D), F32),
            jax.ShapeDtypeStruct((t, D), BF),
            jax.ShapeDtypeStruct((4, D), F32),
            jax.ShapeDtypeStruct((N, t, W), BF),
        ),
        grid_spec=pltpu.PrefetchScalarGridSpec(
            num_scalar_prefetch=1,
            grid=(N,),
            in_specs=[
                full,
                full,
                full,
                full,
                full,
                whole((1, D)),
                pl.BlockSpec((1, W, D), lambda d, table: (jnp.minimum(d, half - 1), 0, 0)),
                pl.BlockSpec((1, W, D), lambda d, table: (jnp.maximum(d - half, 0), 0, 0)),
            ],
            out_specs=(full, full, whole((4, D)), pl.BlockSpec((1, t, W), lambda d, table: (table[d], 0, 0))),
        ),
        compiler_params=vmem(48),
        cost_estimate=CHEAP,
    )(table, *parts, mid, g, gain.reshape(1, D), *weights)


def outer_kernel(table_ref, o_ref, d_att_ref, own_ref, oth_ref):
    d = pl.program_id(0)
    product = dot(o_ref[0], d_att_ref[...], 0, 0).astype(BF)

    @pl.when(d < pl.num_programs(0) // 2)
    def _():
        own_ref[0] = product

    @pl.when(d >= pl.num_programs(0) // 2)
    def _():
        oth_ref[0] = product


def outer(table, o, d_att):
    N, t, W = o.shape
    D = d_att.shape[1]
    half = N // 2
    return pl.pallas_call(
        outer_kernel,
        out_shape=(jax.ShapeDtypeStruct((half, W, D), BF), jax.ShapeDtypeStruct((half, W, D), BF)),
        grid_spec=pltpu.PrefetchScalarGridSpec(
            num_scalar_prefetch=1,
            grid=(N,),
            in_specs=[pl.BlockSpec((1, t, W), lambda d, table: (table[d], 0, 0)), whole((t, D))],
            out_specs=(
                pl.BlockSpec((1, W, D), lambda d, table: (jnp.minimum(d, half - 1), 0, 0)),
                pl.BlockSpec((1, W, D), lambda d, table: (jnp.maximum(d - half, 0), 0, 0)),
            ),
        ),
        compiler_params=vmem(24),
        cost_estimate=CHEAP,
    )(table, o, d_att)


def last_kernel(a_ref, b_ref, c_ref, x_ref, d_mid_ref, gain_ref, out_ref):
    grad = a_ref[...].astype(F32) + b_ref[...].astype(F32) + c_ref[...].astype(F32)
    n, inverse = normed(x_ref[...].astype(F32))
    u = grad * gain_ref[...]
    mean_u = jnp.mean(u, axis=-1, keepdims=True)
    mean_un = jnp.mean(u * n, axis=-1, keepdims=True)
    out_ref[...] = d_mid_ref[...] + (u - mean_u - n * mean_un) * inverse


def last(parts, x, d_mid, gain):
    t, D = x.shape
    full = whole((t, D))
    return pl.pallas_call(
        last_kernel,
        out_shape=jax.ShapeDtypeStruct((t, D), F32),
        grid=(1,),
        in_specs=[full] * 5 + [whole((1, D))],
        out_specs=full,
        compiler_params=vmem(48),
        cost_estimate=pl.CostEstimate(flops=4 * 10**9, transcendentals=0, bytes_accessed=1),
    )(*parts, x, d_mid, gain.reshape(1, D))


def pair_up_kernel(rep_ref, own_ref, other_ref, out_ref):
    m = own_ref.shape[0]
    mine = pl.multiple_of(rep_ref[0] * m, 8)
    theirs = pl.multiple_of((1 - rep_ref[0]) * m, 8)
    out_ref[pl.ds(mine, m)] = own_ref[...].astype(F32)
    out_ref[pl.ds(theirs, m)] = other_ref[...].astype(F32)


def pair_up(rep, own, other):
    m, D = own.shape
    return pl.pallas_call(
        pair_up_kernel,
        out_shape=jax.ShapeDtypeStruct((2 * m, D), F32),
        grid_spec=pltpu.PrefetchScalarGridSpec(
            num_scalar_prefetch=1,
            grid=(1,),
            in_specs=[whole((m, D)), whole((m, D))],
            out_specs=whole((2 * m, D)),
        ),
        compiler_params=vmem(24),
        cost_estimate=CHEAP,
    )(rep.reshape(1), own, other)


def columns_kernel(count, *refs):
    grads, w_ref, sums_ref, gain_ref, shift_ref, rest_ref, out_ref = refs[:count], *refs[count:]
    width = grads[0].shape[1]
    by_d = jnp.zeros((w_ref.shape[0], 1), F32)
    by_g = jnp.zeros((w_ref.shape[0], 1), F32)
    for p, grad_ref in enumerate(grads):
        w = w_ref[:, p * width : (p + 1) * width].astype(F32)
        by_d += jnp.sum(w * sums_ref[:, p * width : (p + 1) * width], axis=1, keepdims=True)
        by_g += jnp.sum(w * grad_ref[...].astype(F32), axis=1, keepdims=True)
    by_n = (by_g - shift_ref[:, :1] * by_d) / gain_ref[:, :1]
    lane = lax.broadcasted_iota(jnp.int32, (w_ref.shape[0], 128), 1)
    small = jnp.where(lane == 0, by_n, jnp.where(lane == 1, by_d, rest_ref[...]))
    out_ref[:, :width] = grads[-1][...]
    out_ref[:, width:] = small.astype(BF)


def with_columns(grads, weight, sums, gain, shift, rest):
    D, width = grads[0].shape
    step = 512
    rows = lambda w: pl.BlockSpec((step, w), lambda i: (i, 0))
    return pl.pallas_call(
        functools.partial(columns_kernel, len(grads)),
        out_shape=jax.ShapeDtypeStruct((D, width + 128), BF),
        grid=(D // step,),
        in_specs=[rows(width)] * len(grads) + [rows(weight.shape[1]), whole(sums.shape), rows(128), rows(128), rows(128)],
        out_specs=rows(width + 128),
        compiler_params=vmem(32),
        cost_estimate=CHEAP,
    )(*grads, weight, sums, gain, shift, rest)


def part_weights_kernel(m, rows, early_ref, late_ref, expand_ref, shrink_ref):
    half = shrink_ref.shape[0] // 2
    width = late_ref.shape[2]
    expand_ref[...] = late_ref[0, :rows]
    shrink_ref[:half] = early_ref[0, m : m + half]
    shrink_ref[half:, :width] = late_ref[0, rows : rows + half]
    shrink_ref[half:, width:] = late_ref[0, rows + half : rows + 2 * half]


def part_weights(early, late, m, rows):
    F, _, D = early.shape
    width = late.shape[2]
    half = (late.shape[1] - rows) // 2
    return pl.pallas_call(
        functools.partial(part_weights_kernel, m, rows),
        out_shape=(jax.ShapeDtypeStruct((F * rows, width), BF), jax.ShapeDtypeStruct((F * 2 * half, D), BF)),
        grid=(F,),
        in_specs=[
            pl.BlockSpec((1,) + early.shape[1:], lambda f: (f, 0, 0)),
            pl.BlockSpec((1,) + late.shape[1:], lambda f: (f, 0, 0)),
        ],
        out_specs=(pl.BlockSpec((rows, width), lambda f: (f, 0)), pl.BlockSpec((2 * half, D), lambda f: (f, 0))),
        compiler_params=vmem(32),
        cost_estimate=CHEAP,
    )(early, late)


def gelu_and_slope(values):
    half = 0.5 + 0.5 * lax.erf(values * 0.7071067811865476)
    density = jnp.exp(values * values * -0.5) * 0.3989422804014327
    return (values * half).astype(BF), (half + values * density).astype(BF)


def together(*values):
    return lax.optimization_barrier(values)


class Plain:
    def __init__(self, R, C):
        self.R, self.C, self.N = R, C, R * C
        self.axes = ("rep", "ctx")
        self.groups = (1, R, C)
        place = jnp.arange(C, dtype=jnp.int32)
        self.order = jnp.stack([place * 0, place, place * 0])
        self.table = jnp.arange(self.N, dtype=jnp.int32)

    def gather(self, x):
        return [lax.all_gather(x, self.axes, axis=0, tiled=True)]

    def gather_two(self, x, g, ready):
        return self.gather(x), self.gather(g), ready

    def scatter_core(self, rows, part, ready=None):
        out = part(0, 0, self.N * rows).astype(BF)
        return out if ready is None else (out, ready)

    def scatter_far(self, state):
        return state

    def scatter_near(self, state):
        return lax.psum_scatter(state, self.axes, scatter_dimension=0, tiled=True)

    def scatter_end(self, state):
        return state, jnp.zeros_like(state), jnp.zeros_like(state)

    def swap(self, parts):
        return lax.all_to_all(parts, self.axes, 0, 0, tiled=True)

    def swap_ctx(self, blocks):
        return lax.all_to_all(blocks, "ctx", 0, 0, tiled=True)

    def prefixes(self, prefix):
        return lax.all_gather(prefix, "rep", axis=0, tiled=True)


class Near(Plain):
    def __init__(self, R, F, C):
        super().__init__(R, C)
        self.F = F
        self.ctx = lax.axis_index("ctx")
        self.rep = lax.axis_index("rep")
        self.fsdp = lax.axis_index("fsdp")
        self.groups = (2, 2, 2)
        place = jnp.arange(C, dtype=jnp.int32) ^ self.ctx
        self.order = jnp.stack([place & 1, place >> 1, place * 0 + self.rep])
        d = jnp.arange(8, dtype=jnp.int32)
        self.table = (self.rep * 4 + self.ctx) ^ ((d & 2) * 2 + (d & 1) * 2 + (d >> 2))

    def over(self, x, d):
        return lax.ppermute(x, "ctx", [(i, i ^ d) for i in range(4)])

    def x(self, x):
        return lax.ppermute(x, "rep", [(0, 1), (1, 0)])

    def y(self, x):
        return self.over(x, 2)

    def core(self, x):
        return self.over(x, 1)

    def gather(self, x):
        return self.gather_core(self.gather_far(x, self.x(x), self.y(x)))

    def gather_far(self, x, from_x, from_y):
        half = x.shape[0] // 2
        near = jnp.concatenate([x, from_y, from_x, jnp.zeros_like(x)], axis=0)
        return near, self.y(from_x[:half]), self.x(from_y[half:])

    def gather_core(self, pieces):
        own, low, high = pieces
        at = own.shape[0] - 2 * low.shape[0]
        own = lax.dynamic_update_slice_in_dim(own, low, at, 0)
        own = lax.dynamic_update_slice_in_dim(own, high, at + low.shape[0], 0)
        return [own, self.core(own)]

    def gather_two(self, x, g, ready):
        t = x.shape[0]
        both = jnp.concatenate([x, g], axis=0)
        from_x = self.x(both)
        both, ready = together(both, ready)
        from_y = self.y(both)
        far_x, far_g = together(self.y(from_x[:t]), self.x(from_y[t:]))
        x = jnp.concatenate([x, from_y[:t], from_x[:t], far_x], axis=0)
        g = jnp.concatenate([g, from_y[t:], from_x[t:], far_g], axis=0)
        return [x, self.core(x)], [g, self.core(g)], ready

    def scatter_core(self, rows, part, ready=None):
        far_x = part(1, 2 * rows, 4 * rows).astype(BF)
        near_x = part(1, 0, 2 * rows).astype(BF)
        far_x, near_x, halfway = together(far_x, near_x, () if ready is None else ready)
        far_x = (part(0, 2 * rows, 4 * rows) + self.core(far_x).astype(F32)).astype(BF)
        near_x = (part(0, 0, 2 * rows) + self.core(near_x).astype(F32)).astype(BF)
        return (far_x, near_x) if ready is None else ((far_x, near_x), halfway)

    def scatter_given(self, own, oth):
        total = (own.astype(F32) + self.core(oth).astype(F32)).astype(BF)
        return total[total.shape[0] // 2 :], total[: total.shape[0] // 2]

    def scatter_far(self, state):
        far_x, near_x = state
        rows = far_x.shape[0] // 2
        half = rows // 2
        return far_x, near_x, self.y(far_x[rows : rows + half]), self.x(far_x[rows + half :])

    def scatter_near(self, state):
        far_x, near_x, to_y, to_x = state
        rows = far_x.shape[0] // 2
        half = rows // 2
        by_x, near_y = far_x[:rows].astype(F32), near_x[rows:].astype(F32)
        by_x = jnp.concatenate([by_x[:half] + to_y.astype(F32), by_x[half:]], axis=0)
        by_y = jnp.concatenate([near_y[:half], near_y[half:] + to_x.astype(F32)], axis=0)
        return near_x, self.x(by_x.astype(BF)), self.y(by_y.astype(BF))

    def scatter_end(self, state):
        return state

    def prefixes(self, prefix):
        return jnp.concatenate([prefix, self.x(prefix)])

    def gather_ctx(self, x):
        x = jnp.stack([x, self.y(x)])
        x = jnp.stack([x, self.core(x)], axis=1).reshape(4, *x.shape[1:])
        x = jnp.take(x, jnp.arange(4) ^ self.ctx, axis=0)
        return x.transpose(1, 0, 2).reshape(-1, x.shape[2])


def added(parts):
    rows = parts[-1].shape[0]
    return sum(a[:rows].astype(F32) for a in parts)


def scatter_shifts(x, axis, size):
    me = lax.axis_index(axis)
    total = lax.dynamic_index_in_dim(x, me, 0, keepdims=False)
    for s in range(1, size):
        mine = lax.dynamic_index_in_dim(x, lax.rem(me + s, size), 0, keepdims=False)
        total = total.astype(F32) + lax.ppermute(mine, axis, [(i, (i + s) % size) for i in range(size)]).astype(F32)
    return total.astype(x.dtype)


def shards(
    sizes,
    inputs,
    prefix,
    joined_weight,
    query_bias,
    value_bias,
    dense_weight,
    dense_bias,
    expand_weight,
    expand_bias,
    shrink_weight,
    shrink_bias,
    first_gain,
    first_shift,
    second_gain,
    second_shift,
    cotangent,
):
    R, F, C = sizes
    N = R * C
    rep = lax.axis_index("rep")
    ctx = lax.axis_index("ctx")
    S, t, D = inputs.shape
    assert S == 1
    B = joined_weight.shape[0]
    FFB = shrink_weight.shape[0]
    FF = FFB * F * C
    E = FFB // R
    W = D // N
    near = R == 2 and C == 4 and B == 2 * HD
    tp = Near(R, F, C) if near else Plain(R, C)
    K, _, Y = tp.groups
    G = range(K)
    n = N // K
    pairs = W // 128

    def half_rows(weight):
        m = weight.shape[0] // R
        return lax.dynamic_slice_in_dim(weight, rep * m, m, 0)

    def widen(blocks):
        return lax.all_gather(blocks.reshape(C * B, -1), "fsdp", axis=0, tiled=True)

    def to_owners(part):
        blocks = jnp.concatenate([part.reshape(C, B, -1)] * R)
        return lax.all_to_all(blocks, ("rep", "ctx"), 0, 0, tiled=True).reshape(R, C, B, -1)

    def over_rep(x):
        return lax.ppermute(x, "rep", [(0, 1), (1, 0)])

    x = inputs.reshape(t, D)
    g = cotangent.reshape(t, D)
    small = jnp.concatenate(
        [first_gain, first_shift, second_gain, second_shift, dense_bias, shrink_bias, query_bias, value_bias, expand_bias]
    )
    if near:
        low, high = jnp.split(half_rows(shrink_weight), 2)
        m = B // R
        small = jnp.pad(small.reshape(1, -1), ((0, 15), (0, D - small.shape[0])))
        early = lax.all_gather(jnp.concatenate([half_rows(dense_weight), low, small]), "fsdp", axis=0, tiled=False)
        dense_rows = early[:, :m].reshape(F * m, D)
        small = tp.gather_ctx(early[:, m + low.shape[0], : 8 * B + FFB])
        blocks = lax.all_to_all(pack(F, C, rep, joined_weight, expand_weight), "ctx", 0, 0, tiled=True)
        joined_blocks, expand_blocks = blocks[:, :, : 3 * W], blocks[:, :, 3 * W :]
    else:
        dense_rows = lax.all_gather(dense_weight, ("fsdp", "ctx"), axis=0, tiled=True)
        small = lax.all_gather(small, ("fsdp", "ctx"), axis=0, tiled=False)
        pieces = joined_weight.reshape(B, 3, R, C, pairs, 128)
        pieces = lax.dynamic_index_in_dim(pieces, rep, 2, keepdims=False).transpose(2, 0, 3, 1, 4)
        joined_blocks = lax.all_to_all(pieces.reshape(C, B, 3 * W), "ctx", 0, 0, tiled=True)
        pieces = expand_weight.reshape(B, F, C, R, E)
        pieces = lax.dynamic_index_in_dim(pieces, rep, 3, keepdims=False).transpose(2, 0, 1, 3)
        expand_blocks = lax.all_to_all(pieces.reshape(C, B, F * E), "ctx", 0, 0, tiled=True)
    x_all, g_all, (joined_blocks, expand_blocks) = tp.gather_two(x, g, (joined_blocks, expand_blocks))
    joined_cols = widen(joined_blocks)
    if near:
        late = jnp.concatenate([expand_blocks.reshape(C * B, -1), high[:, : D // 2], high[:, D // 2 :]])
        late = lax.all_gather(late, "fsdp", axis=0, tiled=False)
    else:
        expand_cols = widen(expand_blocks)
        shrink_rows = lax.all_gather(half_rows(shrink_weight), "fsdp", axis=0, tiled=True)
    prefixes = tp.prefixes(prefix)

    small = small.astype(F32)
    gain_one, shift_one, gain_two, shift_two, dbias, sbias, qbias, vbias = [
        small[:, i * B : (i + 1) * B].reshape(D) for i in range(8)
    ]
    ebias = small[:, 8 * B :].reshape(F, C, R, E)
    ebias = lax.dynamic_index_in_dim(lax.dynamic_index_in_dim(ebias, ctx, 1, False), rep, 1, False)
    ebias = ebias.reshape(F * E)

    def my_features(vector):
        if near:
            v = vector.reshape(F, C, R, -1)
            return lax.dynamic_index_in_dim(lax.dynamic_index_in_dim(v, ctx, 1, False), rep, 1, False).reshape(W)
        return lax.dynamic_slice_in_dim(vector, (rep * C + ctx) * W, W, 0)

    my_heads = my_features(jnp.repeat(jnp.arange(H, dtype=jnp.int32), HD)).reshape(-1, HD)[:, 0]
    slopes = jnp.exp2(-8.0 * (my_heads.astype(F32) + 1.0) / H)

    if near:
        own, dense_rows = together(x_all[0], dense_rows)
        x_all[0] = own
    a1_all = [norm(a, gain_one, shift_one) for a in x_all]
    if near:
        a1_all, joined_cols = together(a1_all, joined_cols)
    else:
        dense_all = [dense_rows[: D // 2], dense_rows[D // 2 :]]
    qkv_bias = jnp.stack([my_features(qbias), jnp.zeros((W,), F32), my_features(vbias)])
    qkv_bias = qkv_bias.reshape(3, pairs, 128).transpose(1, 0, 2).reshape(3 * W)
    qkv = jnp.stack([(dot(a, joined_cols, 1, 0) + qkv_bias).astype(BF) for a in a1_all])
    qkv = qkv.reshape(K, R, Y, t, 3 * W)
    if near:
        from_x, from_y, qkv = together(tp.x(dense_rows), tp.y(dense_rows), qkv)
        dense_all = tp.gather_far(dense_rows, from_x, from_y)
    out = attention_forward(tp.order, prefixes, slopes, qkv)
    out, g_all, dense_all = together(out, g_all, dense_all)
    if near:
        dense_all = tp.gather_core(dense_all)
    o = tp.swap(out.reshape(N, t, W))
    midway, a2 = attended(tp.table, o, dense_all, x, dbias, gain_two, shift_two)

    if near:
        pieces, late = together(tp.gather_far(a2, tp.x(a2), tp.y(a2)), late)
        expand_cols, shrink_rows = part_weights(early, late, m, C * B)
        a2_all = tp.gather_core(pieces)
    else:
        a2_all = tp.gather(a2)
    act, slope = [], []
    for i in G:
        got = gelu_and_slope(dot(a2_all[i], expand_cols, 1, 0) + ebias)
        if i + 1 < K:
            got, a2_all[i + 1] = together(got, a2_all[i + 1])
        act.append(got[0])
        slope.append(got[1])
    shrink_grad = sum(dot(act[i], g_all[i], 0, 0) for i in G).astype(BF)
    slope, shrink_grad, act = together(slope, shrink_grad, act)
    shrink_part = lax.psum_scatter(shrink_grad, "fsdp", scatter_dimension=0, tiled=True)
    d_exp = [(dot(g_all[i], shrink_rows, 1, 1) * slope[i].astype(F32)).astype(BF) for i in G]
    d_exp_sum = sum(jnp.sum(d.astype(F32), axis=0) for d in d_exp)

    d_a2 = tp.scatter_core(t, lambda i, a, b: dot(d_exp[i][a:b], expand_cols, 1, 1))
    d_a2, act = together(d_a2, act)
    d_a2 = tp.scatter_far(d_a2)
    branch = tp.scatter_core(t, lambda i, a, b: dot(act[i][a:b], shrink_rows, 1, 0))
    d_a2, d_exp, branch = together(d_a2, d_exp, branch)
    d_a2 = tp.scatter_near(d_a2)
    expand_grad = sum(dot(a2_all[i], d_exp[i], 0, 0) for i in G).astype(BF)
    d_a2, expand_grad, branch = together(d_a2, expand_grad, branch)
    expand_part = lax.psum_scatter(expand_grad, "fsdp", scatter_dimension=0, tiled=True)
    branch = tp.scatter_far(branch)
    d_mid, d_att, sums_two, d_o = turned(tp.table, tp.scatter_end(d_a2), midway, g, gain_two, dense_all)

    d_o, shrink_part, branch = together(d_o, shrink_part, branch)
    d_o = tp.swap(d_o).reshape(R, C, t, W)
    dense_part = outer(tp.table, o, d_att) if near else ()
    d_o, dense_part, branch, shrink_part = together(d_o, dense_part, branch, shrink_part)
    branch = tp.scatter_near(branch)
    shrink_other = over_rep(shrink_part)
    if near:
        dense_part = tp.scatter_given(*[a.reshape(n * W, D) for a in dense_part])
    d_qkv, joined_grad, expand_all = None, [], ()
    for p in range(pairs):
        d_qkv = attention_backward(p, tp.order, prefixes, slopes[2 * p : 2 * p + 2], qkv, d_o, d_qkv)
        d_qkv, dense_part, branch = together(d_qkv, dense_part, branch)
        if p == 0 and near:
            dense_part = tp.scatter_far(dense_part)
        if p == pairs - 1:
            d_qkv, expand_part, shrink_other = together(d_qkv, expand_part, shrink_other)
            expand_all = to_owners(expand_part)
        mine = d_qkv.reshape(K, n * t, 3 * W)[:, :, 384 * p : 384 * (p + 1)]
        grad = sum(dot(a1_all[i], mine[i], 0, 0) for i in G).astype(BF)
        d_qkv, grad, d_o = together(d_qkv, grad, d_o)
        joined_grad.append(grad)
    d_qkv = d_qkv.reshape(K, n * t, 3 * W)
    layer_output = midway + added(tp.scatter_end(branch)) + sbias

    d_qkv_sum = jnp.sum(d_qkv.astype(F32), axis=(0, 1))

    def place(vector, width):
        if near or width != D:
            full = jnp.zeros((F, C, R, width // (F * C * R)), F32)
            full = lax.dynamic_update_slice(full, vector.reshape(F, 1, 1, -1), (0, ctx, rep, 0))
            return full.reshape(F * C, width // D, B).transpose(0, 2, 1).reshape(D, width // D)
        return lax.dynamic_update_slice_in_dim(jnp.zeros((width,), F32), vector, (rep * C + ctx) * W, 0).reshape(D, 1)

    by_part = d_qkv_sum.reshape(pairs, 3, 128)
    rest = [jnp.zeros((D, 2), F32), sums_two.T, place(by_part[:, 0].reshape(W), D), place(by_part[:, 2].reshape(W), D)]
    rest.append(place(d_exp_sum, FF))
    rest = jnp.concatenate(rest, axis=1)
    used = rest.shape[1]
    rest = jnp.pad(rest, ((0, 0), (0, 128 - used)))
    lanes = lambda a: jnp.broadcast_to(a[:, None], (D, 128))
    grad = with_columns(joined_grad, joined_cols, d_qkv_sum.reshape(1, 3 * W), lanes(gain_one), lanes(shift_one), rest)
    joined_part = [lax.psum_scatter(a, "fsdp", scatter_dimension=0, tiled=True) for a in joined_grad[:-1]]
    grad, joined_part = together(grad, joined_part)
    joined_part.append(lax.psum_scatter(grad, "fsdp", scatter_dimension=0, tiled=True))
    if near:
        dense_part = tp.scatter_near(dense_part)
    d_a1, expand_all = tp.scatter_core(t, lambda i, a, b: dot(d_qkv[i, a:b], joined_cols, 1, 1), expand_all)
    shrink_out = ()
    if near:
        shrink_out = pair_up(rep, shrink_part, shrink_other)
        dense_part = added(tp.scatter_end(dense_part)).astype(BF).reshape(F, W // F, D)
    d_a1, shrink_out, layer_output, dense_part, joined_part = together(d_a1, shrink_out, layer_output, dense_part, joined_part)
    if near:
        dense_part = scatter_shifts(dense_part, "fsdp", F)
    d_a1 = together(*tp.scatter_far(d_a1)) if near else d_a1
    joined_all = to_owners(jnp.concatenate(joined_part, axis=1))
    d_a1 = tp.scatter_near(d_a1)
    if near:
        expand_out = unpack(unpack_expand_kernel, F, expand_all)
        d_a1, expand_out = together(d_a1, expand_out)
    d_a1, dense_part = together(d_a1, dense_part)
    dense_other = over_rep(dense_part) if near else ()
    input_gradient = last(tp.scatter_end(d_a1), x, d_mid, gain_one)
    if near:
        dense_out = pair_up(rep, dense_part, dense_other)
        input_gradient, dense_out, joined_all = together(input_gradient, dense_out, joined_all)

    def both_reps(own, other):
        first = rep == 0
        return jnp.stack([jnp.where(first, own, other), jnp.where(first, other, own)])

    little = jnp.sum(joined_all[:, :, :, 3 * W :].astype(F32), axis=(0, 1)).T
    if near:
        joined_out = unpack(unpack_joined_kernel, F, joined_all, 128)
    else:
        expand_out = expand_all.reshape(R, C, B, F, E).transpose(2, 3, 1, 0, 4).reshape(B, FF).astype(F32)
        both = joined_all[:, :, :, : 3 * W].reshape(R, C, B, pairs, 3, 128).transpose(2, 4, 0, 1, 3, 5)
        joined_out = both.reshape(B, 3 * D).astype(F32)
        shrink_out = both_reps(shrink_part, shrink_other).reshape(FFB, D).astype(F32)
        part = dot(o.transpose(1, 0, 2).reshape(t, D), d_att, 0, 0).astype(BF)
        part = lax.psum_scatter(part, ("fsdp", "ctx"), scatter_dimension=0, tiled=True)
        dense_out = lax.psum(part, "rep").astype(F32)
    gain_one_out, shift_one_out, gain_two_out, shift_two_out, dbias_out, sbias_out, qbias_out, vbias_out = [
        little[i] for i in range(8)
    ]
    ebias_out = little[8:used].reshape(FFB)

    return (
        layer_output.reshape(S, t, D),
        input_gradient.reshape(S, t, D),
        joined_out,
        qbias_out,
        vbias_out,
        dense_out,
        dbias_out,
        expand_out,
        ebias_out,
        shrink_out,
        sbias_out,
        gain_one_out,
        shift_one_out,
        gain_two_out,
        shift_two_out,
    )


def solution(mesh):
    sizes = (mesh.shape["rep"], mesh.shape["fsdp"], mesh.shape["ctx"])
    tokens = P(("rep", "fsdp"), "ctx", None)
    matrix = P(("fsdp", "ctx"), None)
    vector = P(("fsdp", "ctx"))
    weights = (matrix, vector, vector, matrix, vector, matrix, vector, matrix, vector, vector, vector, vector, vector)
    in_specs = (tokens, P(("rep", "fsdp")), *weights, tokens)
    out_specs = (tokens, tokens, *weights)

    def step(*arrays):
        return shards(sizes, *arrays)

    return jax.shard_map(step, mesh=mesh, in_specs=in_specs, out_specs=out_specs, check_vma=False)
```
